32 devices in a mesh: grp: 4 (over z), dom: 8 (over y, x, core).
Axes of the slice: x: 2, y: 2, z: 4, core: 2. Of those that a mesh axis runs over, the one named last changes fastest.
Arguments:
- operator_blocks: float32 [128, 16, 4096], P(('grp', 'dom')), may hold values from -0.75 to 0.75
- operator_cols: int32 [128, 16], P(('grp', 'dom')), may hold values from 0 to 15, as said below
- halo_count: int32 [128], P(('grp', 'dom')), may hold values from 2 to 4, as said below
- prolong_blocks: float32 [128, 8, 4096], P(('grp', 'dom')), may hold values from -0.75 to 0.75
- prolong_cols: int32 [128, 8], P(('grp', 'dom')), may hold values from 0 to 63, as said below
- prolong_slot: int32 [128, 8], P(('grp', 'dom')), may hold values from 0 to 15, as said below
- send_lists: int32 [32, 8], P(('grp', 'dom')), may hold values from 0 to 3
- slot_owner_row: int32 [32, 16], P(('grp', 'dom')), may hold values from 0 to 2, as said below
- coarse_pattern: int32 [64, 16], P(('grp', 'dom')), may hold values from 0 to 63, as said below
Outputs:
- coarse_blocks: float32 [64, 16, 4096], P(('grp', 'dom'))
The draws below stay inside these ranges and needn't reach their ends.
Inputs may be any that keep to these rules, and one draw needn't show every extreme that they name: `operator_cols`: slots below 12 hold values below 16, the others values below 8. Slots at or beyond a row's live count hold valid values whose blocks do not count. `halo_count`: the first fine row of every device has 4. `prolong_cols`: the 8 values of a row are different. A row on grp index g names coarse rows owned by devices of grp index g only. Slot t of device v stands for owner dom index t // 2 and owner coarse row slot_owner_row[v, t]; prolong_cols[i, j] = ((v // 8) * 8 + s // 2) * 2 + slot_owner_row[v, s] for s = prolong_slot[i, j]; the slots of a row are different and never empty. `slot_owner_row`: the value 2 marks an empty slot; the live values of one device for one owner are different; every device fills all 2 slots of its own dom index and the first slot of every owner, and no other slot. `coarse_pattern`: the 16 values of a row are different.
All inputs are finite; a program needn't handle non-finite values.
Results may differ from the reference program's by a relative error of at most 0.0003.
Values sent between devices are 32-bit elements; how exact they have to be, the bound alone decides.
A program may use at most 128 MiB of HBM per device.

```python
import jax
import jax.numpy as jnp
from jax import lax

BS = 64
RB = 4
CB = 2
KG = 12
KH = 4
KA = 16
KP = 8
KC = 16
HS = 1
CAP = 2
ROWS = 128
NC = 64
N_GRP = 4
N_DOM = 8


def common_draw(key):
    devices_all = N_GRP * N_DOM
    slot_total = N_DOM * CAP
    far_total = N_DOM * HS
    score = jax.random.randint(jax.random.fold_in(key, 1), (devices_all, N_DOM, CB), 0, 1 << 20) * CB + jnp.arange(CB, dtype=jnp.int32)
    order = jnp.argsort(score, axis=-1)[..., :CAP].astype(jnp.int32)
    own_domain = (jnp.arange(N_DOM, dtype=jnp.int32)[None, :] == (jnp.arange(devices_all, dtype=jnp.int32) % N_DOM)[:, None])[..., None]
    first_slot = (jnp.arange(CAP, dtype=jnp.int32) == 0)[None, None, :]
    live_slot = own_domain | first_slot
    owner_row = jnp.where(live_slot, order, CB).reshape(devices_all, slot_total).astype(jnp.int32)
    live_flat = live_slot.reshape(devices_all, slot_total)
    pick_score = jax.random.randint(jax.random.fold_in(key, 3), (devices_all, RB, slot_total), 0, 1 << 20) * slot_total + jnp.arange(slot_total, dtype=jnp.int32)
    pick_score = jnp.where(live_flat[:, None, :], pick_score, -1)
    chosen = lax.top_k(pick_score, KP)[1].astype(jnp.int32)
    chosen_rows = jnp.take_along_axis(jnp.broadcast_to(owner_row[:, None, :], (devices_all, RB, slot_total)), chosen, axis=2)
    group_of = jnp.arange(devices_all, dtype=jnp.int32) // N_DOM
    prolong_cols = ((group_of[:, None, None] * N_DOM + chosen // CAP) * CB + chosen_rows).reshape(ROWS, KP).astype(jnp.int32)
    prolong_slot = chosen.reshape(ROWS, KP)
    send_lists = jax.random.randint(jax.random.fold_in(key, 4), (devices_all, N_DOM * HS), 0, RB).astype(jnp.int32)
    near_part = jax.random.randint(jax.random.fold_in(key, 5), (ROWS, KG), 0, N_GRP * RB)
    far_score = jax.random.randint(jax.random.fold_in(key, 6), (devices_all, far_total), 0, 1 << 20) * far_total + jnp.arange(far_total, dtype=jnp.int32)
    far_perm = jnp.argsort(far_score, axis=-1).astype(jnp.int32)
    position = (jnp.arange(KH, dtype=jnp.int32)[None, :] * RB + jnp.arange(RB, dtype=jnp.int32)[:, None]) % far_total
    far_part = jnp.take_along_axis(jnp.broadcast_to(far_perm[:, None, :], (devices_all, RB, far_total)), jnp.broadcast_to(position[None], (devices_all, RB, KH)), axis=2).reshape(ROWS, KH)
    operator_cols = jnp.concatenate([near_part, far_part], axis=1).astype(jnp.int32)
    random_count = jax.random.randint(jax.random.fold_in(key, 7), (ROWS,), 2, KH + 1)
    halo_count = jnp.where(jnp.arange(ROWS, dtype=jnp.int32) % RB == 0, KH, random_count).astype(jnp.int32)
    row_index = jnp.arange(ROWS, dtype=jnp.int32)
    device = row_index // RB
    domain = device % N_DOM
    near_rows = (near_part // RB * N_DOM + domain[:, None]) * RB + near_part % RB
    source = (device // N_DOM)[:, None] * N_DOM + far_part // HS
    far_rows = source * RB + send_lists[source, domain[:, None] * HS + far_part % HS]
    columns = jnp.concatenate([near_rows, far_rows], axis=1)
    live_far = (jnp.arange(KH, dtype=jnp.int32)[None, :] < halo_count[:, None]).astype(jnp.int32)
    live_all = jnp.concatenate([jnp.ones((ROWS, KG), jnp.int32), live_far], axis=1)
    expanded = prolong_cols[columns]
    flat_pair = prolong_cols[:, :, None, None] * NC + expanded[:, None, :, :]
    weight_pair = jnp.broadcast_to(live_all[:, None, :, None], flat_pair.shape)
    counts = jnp.zeros((NC * NC,), jnp.int32).at[flat_pair.reshape(-1)].add(weight_pair.reshape(-1)).reshape(NC, NC)
    tie_break = jax.random.randint(jax.random.fold_in(key, 8), (NC, NC), 0, 1 << 10) * NC + jnp.arange(NC, dtype=jnp.int32)[None, :]
    coarse_pattern = lax.top_k(counts * (NC << 10) + tie_break, KC)[1].astype(jnp.int32)
    return (operator_cols, halo_count, prolong_cols, prolong_slot, send_lists, owner_row, coarse_pattern)


def draw_operator_cols(key, part):
    return common_draw(jax.random.fold_in(key, 77))[0]


def draw_halo_count(key, part):
    return common_draw(jax.random.fold_in(key, 77))[1]


def draw_prolong_cols(key, part):
    return common_draw(jax.random.fold_in(key, 77))[2]


def draw_prolong_slot(key, part):
    return common_draw(jax.random.fold_in(key, 77))[3]


def draw_send_lists(key, part):
    return common_draw(jax.random.fold_in(key, 77))[4]


def draw_slot_owner_row(key, part):
    return common_draw(jax.random.fold_in(key, 77))[5]


def draw_coarse_pattern(key, part):
    return common_draw(jax.random.fold_in(key, 77))[6]


def level_of(stream_key, shape, split, low, largest):
    loudness = 1.0
    for dim, parts in split:
        draws = jax.random.uniform(jax.random.fold_in(jax.random.fold_in(stream_key, 6), dim), (parts,), jnp.float32, low / len(split), largest / len(split))
        loudness = loudness * jnp.repeat(jnp.exp(draws), shape[dim] // parts).reshape((-1,) + (1,) * (len(shape) - 1 - dim))
    return loudness


def scatter_about(stream_key, shape, spread, bound, split=(), held_as=jnp.bfloat16):
    array = jax.random.normal(stream_key, shape, jnp.float32) * spread
    if len(split) > 0:
        array = level_of(stream_key, shape, split, -0.22, 0.18) * array
    return jnp.clip(array, min=-bound, max=bound).astype(held_as)


def setup_inputs(seed: int = 0) -> dict:
    splits = jax.random.split(jax.random.key(seed), 10)
    return {
        "operator_blocks": scatter_about(splits[0], (ROWS, KA, BS * BS), BS ** -0.5, 0.75, ((0, 32),), jnp.float32),
        "operator_cols": draw_operator_cols(jax.random.fold_in(splits[9], 71), 0),
        "halo_count": draw_halo_count(jax.random.fold_in(splits[9], 71), 0),
        "prolong_blocks": scatter_about(splits[3], (ROWS, KP, BS * BS), BS ** -0.5, 0.75, ((0, 32),), jnp.float32),
        "prolong_cols": draw_prolong_cols(jax.random.fold_in(splits[9], 71), 0),
        "prolong_slot": draw_prolong_slot(jax.random.fold_in(splits[9], 71), 0),
        "send_lists": draw_send_lists(jax.random.fold_in(splits[9], 71), 0),
        "slot_owner_row": draw_slot_owner_row(jax.random.fold_in(splits[9], 71), 0),
        "coarse_pattern": draw_coarse_pattern(jax.random.fold_in(splits[9], 71), 0),
    }


EXACT = lax.Precision.HIGHEST


def column_map(operator_cols, send_lists):
    row_index = jnp.arange(ROWS, dtype=jnp.int32)
    device = row_index // RB
    group_index = device // N_DOM
    domain = device % N_DOM
    near_slots = operator_cols[:, :KG]
    near_rows = ((near_slots // RB) * N_DOM + domain[:, None]) * RB + near_slots % RB
    far_slots = operator_cols[:, KG:]
    source = group_index[:, None] * N_DOM + far_slots // HS
    far_rows = source * RB + send_lists[source, domain[:, None] * HS + far_slots % HS]
    return jnp.concatenate([near_rows, far_rows], axis=1).astype(jnp.int32)


def live_mask(halo_count):
    near_live = jnp.ones((halo_count.shape[0], KG), jnp.float32)
    far_live = (jnp.arange(KH, dtype=jnp.int32)[None, :] < halo_count[:, None]).astype(jnp.float32)
    return jnp.concatenate([near_live, far_live], axis=1)


def target_rows(prolong_slot, slot_owner_row):
    device = jnp.arange(ROWS, dtype=jnp.int32) // RB
    owner_row = slot_owner_row[device[:, None], prolong_slot]
    return (((device // N_DOM)[:, None] * N_DOM + prolong_slot // CAP) * CB + owner_row).astype(jnp.int32)


def reference(operator_blocks, operator_cols, halo_count, prolong_blocks, prolong_cols, prolong_slot, send_lists, slot_owner_row, coarse_pattern):
    columns = column_map(operator_cols, send_lists)
    live_slots = jnp.repeat(live_mask(halo_count), KP, axis=1)
    expanded_ids = prolong_cols[columns].reshape(ROWS, KA * KP)
    target_ids = target_rows(prolong_slot, slot_owner_row)
    block_count = ROWS // RB
    square = prolong_blocks.reshape(ROWS, KP, BS, BS)
    blocks = (operator_blocks.reshape(block_count, RB, KA, BS, BS), columns.reshape(block_count, RB, KA),
              expanded_ids.reshape(block_count, RB, KA * KP), live_slots.reshape(block_count, RB, KA * KP),
              square.reshape(block_count, RB, KP, BS, BS), target_ids.reshape(block_count, RB, KP))

    def add_block(coarse_sum, pieces):
        operator, columns_block, coarse_ids, live_block, panels, targets = pieces
        fetched = square[columns_block]
        weights = jnp.einsum('rmax,rmqxd->rmqad', operator, fetched, precision=EXACT).reshape(RB, KA * KP, BS * BS)
        wanted = coarse_pattern[targets]
        select = (wanted[..., None] == coarse_ids[:, None, None, :]).astype(jnp.float32) * live_block[:, None, None, :]
        matched = jnp.einsum('rjce,rex->rjcx', select, weights, precision=EXACT).reshape(RB, KP, KC, BS, BS)
        pair_terms = jnp.einsum('rjab,rjcad->rjcbd', panels, matched, precision=EXACT)
        return coarse_sum.at[targets.reshape(RB * KP)].add(pair_terms.reshape(RB * KP, KC, BS * BS)), None

    start = jnp.zeros((NC, KC, BS * BS), jnp.float32)
    return lax.scan(add_block, start, blocks)[0]
```

```python
import functools

import jax
import jax.numpy as jnp
from jax import lax
from jax.experimental import pallas as pl
from jax.experimental.pallas import tpu as pltpu
from jax.sharding import PartitionSpec as P

BS = 64
KG = 12
LANES = 128
SUB = 8


def any_spec():
    return pl.BlockSpec(memory_space=pl.ANY)


def vmem_spec():
    return pl.BlockSpec(memory_space=pltpu.VMEM)


def smem_spec():
    return pl.BlockSpec(memory_space=pltpu.SMEM)


def fused_kernel(
    n_grp, n_dom, rows, hs, ka, kp, kc, cap, owned, stages,
    cols, halo, slots, picked, owner, prolong_cols, pattern, prolong_in, operator_in,
    out,
    own_raw, operator, table, outgoing, grp_out, grp_in, dom_base, dom_out, dom_in, plan_v, plan_s,
    blocks, dense, own_dup, stage, panels, left, ap, partial, arrived, summed,
    load_sem, line_send, line_recv, halo_send, halo_recv,
    gmeta_send, gmeta_recv, dmeta_send, dmeta_recv, plan_sem, part_send, part_recv,
):
    g = lax.axis_index("grp")
    me = lax.axis_index("dom")
    near_count = n_grp * rows
    plane_ids = owned * n_dom
    halo_count_rows = n_dom * hs
    groups = n_grp + halo_count_rows // rows
    zero_at = (rows + halo_count_rows) * kp
    row_at = hs + owned
    sort_at = n_grp + n_dom
    rank_at = sort_at + n_dom
    width = rows * BS
    tiles = BS // 2
    low = lax.broadcasted_iota(jnp.int32, (1, LANES), 1) < BS
    lane = lax.broadcasted_iota(jnp.int32, (SUB, LANES), 1)
    sub = lax.broadcasted_iota(jnp.int32, (SUB, LANES), 0)

    barrier = pltpu.get_barrier_semaphore()
    for k in range(1, n_grp):
        pl.semaphore_signal(barrier, inc=1, device_id={"grp": lax.rem(g + k, n_grp)})
    for k in range(1, n_dom):
        pl.semaphore_signal(barrier, inc=1, device_id={"dom": lax.rem(me + k, n_dom)})
    own_load = pltpu.make_async_copy(prolong_in, own_raw, load_sem.at[0])
    operator_load = pltpu.make_async_copy(operator_in, operator, load_sem.at[1])
    own_load.start()
    operator_load.start()

    def partner(k):
        other = 0
        bit = 1
        while bit < n_dom:
            other += lax.rem(me // bit + k // bit, 2) * bit
            bit *= 2
        return other

    grp_out[...] = jnp.zeros(grp_out.shape, jnp.int32)
    grp_out[0:rows, 0:kp] = prolong_cols[...]
    dom_base[...] = jnp.zeros(dom_base.shape, jnp.int32)
    for r in range(owned):
        for j in range(0, LANES, kc):
            dom_base[hs + r:hs + r + 1, j:j + kc] = pattern[r:r + 1, :]

    def for_dom(d, carry):
        dom_out[d] = dom_base[...]
        for h in range(hs):
            dom_out[d, h:h + 1, 0:kp] = prolong_cols[pl.ds(picked[0, d * hs + h], 1), :]
        dom_out[d, row_at:row_at + 1, :] = jnp.full((1, LANES), owner[0, d * cap], jnp.int32)
        return carry

    lax.fori_loop(0, n_dom, for_dom, 0)
    grp_in[g] = grp_out[...]
    dom_in[me] = dom_out[me]
    pl.semaphore_wait(barrier, n_grp + n_dom - 2)

    def line_copy(direction, step, r, src, origin):
        return pltpu.make_async_remote_copy(
            src_ref=src, dst_ref=table.at[origin * rows + r],
            send_sem=line_send.at[direction, step, r], recv_sem=line_recv.at[direction, step, r],
            device_id={"grp": g + 1 if direction == 0 else g - 1},
        )

    def grp_meta(k):
        return pltpu.make_async_remote_copy(
            src_ref=grp_out, dst_ref=grp_in.at[g], send_sem=gmeta_send.at[k], recv_sem=gmeta_recv.at[k],
            device_id={"grp": lax.rem(g + k, n_grp)},
        )

    def dom_meta(k):
        target = partner(k)
        return pltpu.make_async_remote_copy(
            src_ref=dom_out.at[target], dst_ref=dom_in.at[me], send_sem=dmeta_send.at[k], recv_sem=dmeta_recv.at[k],
            device_id={"dom": target},
        )

    def halo_copy(k):
        target = partner(k)
        return pltpu.make_async_remote_copy(
            src_ref=outgoing.at[pl.ds(target * hs, hs)], dst_ref=table.at[pl.ds(near_count + me * hs, hs)],
            send_sem=halo_send.at[k], recv_sem=halo_recv.at[k],
            device_id={"dom": target},
        )

    for k in range(1, n_grp):
        grp_meta(k).start()

    def start_dom_meta(k, carry):
        dom_meta(k).start()
        return carry

    lax.fori_loop(1, n_dom, start_dom_meta, 0)
    can_send = (g < n_grp - 1, g > 0)
    for r in range(rows):
        for direction in range(2):
            @pl.when(can_send[direction])
            def _():
                line_copy(direction, 0, r, prolong_in.at[r], g).start()

    own_load.wait()

    def pick(n, carry):
        outgoing[n] = own_raw[picked[0, n]]
        return carry

    lax.fori_loop(0, halo_count_rows, pick, 0)

    def duplicate(x, write, at):
        turned = pltpu.roll(x, BS, 1)
        write(at, jnp.where(low, x, turned))
        write(at + 1, jnp.where(low, turned, x))

    def own_row(i, carry):
        def write(a, value):
            own_dup[pl.ds(i * kp, kp), a, :] = value

        for t in range(tiles):
            duplicate(own_raw[i, :, t * LANES:(t + 1) * LANES], write, 2 * t)
        return carry

    lax.fori_loop(0, rows, own_row, 0)

    def start_halo(k, carry):
        halo_copy(k).start()
        return carry

    lax.fori_loop(1, n_dom, start_halo, 0)
    own_dup[rows * kp] = jnp.zeros((BS, LANES), jnp.float32)
    panels[zero_at] = jnp.zeros((2 * BS, LANES), jnp.bfloat16)

    def split(value):
        high = value.astype(jnp.bfloat16)
        return high, (value - high.astype(jnp.float32)).astype(jnp.bfloat16)

    def keep(at, value):
        high, rest = split(value)
        panels[at, 0:BS] = high
        panels[at, BS:2 * BS] = rest

    def convert(panel, place):
        def write(a, value):
            stage[:, a, :] = value

        for t in range(tiles):
            duplicate(table[panel, :, t * LANES:(t + 1) * LANES], write, 2 * t)
        for q in range(kp):
            keep(place * kp + q, stage[q])

    operator_load.wait()

    def relay(n, carry):
        i = n // (ka // SUB)
        m = lax.rem(n, ka // SUB) * SUB

        def write(a, value):
            blocks[i, pl.ds(m, SUB), a, :] = value

        for t in range(tiles):
            duplicate(operator[i, pl.ds(m, SUB), t * LANES:(t + 1) * LANES], write, 2 * t)
        return carry

    lax.fori_loop(0, rows * (ka // SUB), relay, 0)

    def densify(i, group, slots_used, column_of):
        for pair in range(0, rows, 2):
            first = group * rows + pair
            wanted = jnp.where(low, first, first + 1)
            total = jnp.zeros((BS, LANES), jnp.float32)
            for m in slots_used:
                total += jnp.where(wanted == column_of(i, m), blocks[i, m], 0.0)
            high, rest = split(total)
            here = pl.ds(i * BS, BS)
            dense[group, here, pair * BS:(pair + 2) * BS] = high
            dense[group, here, width + pair * BS:width + (pair + 2) * BS] = rest

    def near_dense(n, carry):
        densify(n // n_grp, lax.rem(n, n_grp), range(KG), lambda i, m: cols[i, m])
        return carry

    def far_column(i, m):
        return jnp.where(m - KG < halo[i], near_count + cols[i, m], -1)

    far_groups = groups - n_grp

    def far_dense(n, carry):
        densify(n // far_groups, n_grp + lax.rem(n, far_groups), range(KG, ka), far_column)
        return carry

    lax.fori_loop(0, rows * n_grp, near_dense, 0)
    lax.fori_loop(0, rows * far_groups, far_dense, 0)

    for k in range(1, n_grp):
        grp_meta(k).wait()

    def wait_dom_meta(k, carry):
        dom_meta(k).wait()
        return carry

    lax.fori_loop(1, n_dom, wait_dom_meta, 0)

    def places(values, first_id, first_place):
        found = jnp.full((SUB, LANES), zero_at, jnp.int32)
        for q in range(kp):
            found = jnp.where(values[:, q:q + 1] == first_id + lane, (first_place + sub) * kp + q, found)
        return found

    for origin in range(n_grp):
        side = (origin > g).astype(jnp.int32)
        plan_v[origin] = places(grp_in[origin], origin * plane_ids, side * rows)

    slot_of_lane = lax.rem(lane, kc)

    def dom_tables(d, carry):
        values = dom_in[d]
        plan_v[n_grp + d] = places(values, g * plane_ids, rows + d * hs)
        plane = jnp.zeros((SUB, LANES), jnp.int32)
        for n in range(1, n_grp):
            plane += (values >= n * plane_ids).astype(jnp.int32)
        order = jnp.abs(plane - g) * kc + slot_of_lane
        rank = jnp.zeros((SUB, LANES), jnp.int32)
        for s in range(1, kc):
            rank += (pltpu.roll(order, s, 1) < order).astype(jnp.int32)
        ordered = values
        for s in range(kc):
            ordered = jnp.where(pltpu.roll(rank, s, 1) == slot_of_lane, pltpu.roll(values, s, 1), ordered)
        plan_v[sort_at + d] = ordered
        plan_v[rank_at + d] = rank
        return carry

    lax.fori_loop(0, n_dom, dom_tables, 0)
    plan_copy = pltpu.make_async_copy(plan_v, plan_s, plan_sem.at[0])
    plan_copy.start()

    def transposed(slot, at):
        for pair in range(0, rows, 2):
            both = []
            for i in range(pair, pair + 2):
                place = jnp.int32(rows * kp)
                for j in range(kp):
                    place = jnp.where(slots[i, j] == slot, i * kp + j, place)
                both.append(own_dup[place])
            turned = jnp.concatenate(both, axis=0).T
            high = turned.astype(jnp.bfloat16).astype(jnp.float32)
            upper = lax.broadcasted_iota(jnp.int32, (LANES, LANES), 0) < BS
            left[at, :, pair * BS:(pair + 2) * BS] = jnp.where(upper, high, turned - high).astype(jnp.bfloat16)

    def far_left(k, carry):
        transposed(partner(k) * cap, k)
        return carry

    lax.fori_loop(1, n_dom, far_left, 0)
    for t in range(cap):
        transposed(me * cap + t, 0 if t == 0 else n_dom + t - 1)

    def own_panels(n, carry):
        keep(n, own_dup[n])
        return carry

    lax.fori_loop(0, rows * kp, own_panels, 0)
    plan_copy.wait()

    def multiply(plane, parts):
        def four(n, carry):
            e = n * 4
            total = None
            for group, index_of in parts:
                halves = []
                for pair in range(2):
                    blocks_here = [
                        jnp.where(low, panels[index_of(r, e + 2 * pair)], panels[index_of(r, e + 2 * pair + 1)])
                        for r in range(rows)
                    ]
                    high = [b[0:BS] for b in blocks_here]
                    rest = [b[BS:2 * BS] for b in blocks_here]
                    halves.append(jnp.concatenate(high + rest + high, axis=0))
                right = jnp.concatenate(halves, axis=1)
                split_dense = dense[group]
                lhs = jnp.concatenate([split_dense[:, 0:width], split_dense], axis=1)
                product = jnp.dot(lhs, right, preferred_element_type=jnp.float32)
                total = product if total is None else total + product
            for pair in range(2):
                value = total[:, pair * LANES:(pair + 1) * LANES]
                high = value.astype(jnp.bfloat16).astype(jnp.float32)
                rest = value - high
                turned = pltpu.roll(jnp.where(low, rest, high), BS, 1)
                at = plane * plane_ids + e + 2 * pair
                ap[at] = jnp.where(low, high, turned).astype(jnp.bfloat16)
                ap[at + 1] = jnp.where(low, turned, rest).astype(jnp.bfloat16)
            return carry

        lax.fori_loop(0, plane_ids // 4, four, 0)

    def near_index(origin):
        return lambda r, e: plan_s[origin, r, e]

    def far_index(group):
        def index_of(r, e):
            n = group * rows + r
            return plan_s[n_grp + n // hs, n % hs, e]
        return index_of

    def part_copy(s, k):
        first, last = stages[s][1:]
        here = pl.ds(first * BS, (last - first) * BS)
        return pltpu.make_async_remote_copy(
            src_ref=partial.at[k, :, here], dst_ref=arrived.at[k - 1, :, here],
            send_sem=part_send.at[s, k - 1], recv_sem=part_recv.at[s, k - 1],
            device_id={"dom": partner(k)},
        )

    def slot_rows(s, owner_dom, slot, at):
        first, last = stages[s][1:]
        line = hs + owner[0, slot]
        for c in range(first, last, 2):
            right = jnp.concatenate([ap[plan_s[sort_at + owner_dom, line, c + h]] for h in range(2)], axis=1)
            product = jnp.dot(left[at], right, preferred_element_type=jnp.float32)
            both = product[:BS] + product[BS:]
            one, two = both[:, :LANES], both[:, LANES:]
            partial[at, :, c * BS:(c + 2) * BS] = jnp.where(low, one, two) + pltpu.roll(jnp.where(low, two, one), BS, 1)

    def exchange(s):
        first, last = stages[s][1:]
        here = slice(first * BS, last * BS)

        def far_slot(step, carry):
            k = n_dom - step
            target = partner(k)
            slot_rows(s, target, target * cap, k)

            @pl.when(step > 1)
            def _():
                part_copy(s, k + 1).start()

            return carry

        lax.fori_loop(1, n_dom, far_slot, 0)
        slot_rows(s, me, me * cap, 0)
        part_copy(s, 1).start()
        for t in range(1, cap):
            slot_rows(s, me, me * cap + t, n_dom + t - 1)
        for r in range(owned):
            total = partial[0, :, here] * (owner[0, me * cap] == r).astype(jnp.float32)
            for t in range(1, cap):
                total += partial[n_dom + t - 1, :, here] * (owner[0, me * cap + t] == r).astype(jnp.float32)
            summed[r, :, here] = total

    def collect(s):
        first, last = stages[s][1:]

        def one(step, carry):
            k = n_dom - step
            part_copy(s, k).wait_recv()
            row = dom_in[partner(k), row_at:row_at + 1, :]
            for c in range(first, last, 2):
                here = slice(c * BS, (c + 2) * BS)
                value = arrived[k - 1, :, here]
                for r in range(owned):
                    summed[r, :, here] += jnp.where(row == r, value, 0.0)
            return carry

        lax.fori_loop(1, n_dom, one, 0)

    def take_halo(k, carry):
        halo_copy(k).wait_recv()
        for h in range(hs):
            convert(near_count + partner(k) * hs + h, rows + partner(k) * hs + h)
        return carry

    def own_halo(h, carry):
        def write(a, value):
            stage[:, a, :] = value

        for t in range(tiles):
            duplicate(outgoing[me * hs + h, :, t * LANES:(t + 1) * LANES], write, 2 * t)
        for q in range(kp):
            keep((rows + me * hs + h) * kp + q, stage[q])
        return carry

    for step in range(n_grp - 1):
        origins = (g - 1 - step, g + 1 + step)
        exists = (origins[0] >= 0, origins[1] < n_grp)
        for r in range(rows):
            for direction in range(2):
                origin = origins[direction]

                @pl.when(exists[direction])
                def _():
                    line_copy(direction, step, r, table.at[origin * rows + r], origin).wait_recv()

                if step < n_grp - 2:
                    @pl.when(exists[direction] & can_send[direction])
                    def _():
                        line_copy(direction, step + 1, r, table.at[origin * rows + r], origin).start()

            if step > 0:
                for direction in range(2):
                    @pl.when(exists[direction])
                    def _():
                        convert(origins[direction] * rows + r, direction * rows + r)
        if step == 0:
            lax.fori_loop(0, hs, own_halo, 0)
            lax.fori_loop(1, n_dom, take_halo, 0)
            multiply(g, [(g, near_index(g))] + [(n_grp + n, far_index(n)) for n in range(far_groups)])
            for s in range(len(stages)):
                if stages[s][0] < 0:
                    exchange(s)
        for direction in range(2):
            @pl.when(exists[direction])
            def _():
                if step == 0:
                    def take(r, carry):
                        convert(origins[direction] * rows + r, direction * rows + r)
                        return carry

                    lax.fori_loop(0, rows, take, 0)
                multiply(origins[direction], [(origins[direction], near_index(origins[direction]))])
        for s in range(len(stages)):
            if stages[s][0] == step:
                exchange(s)

    for s in range(len(stages)):
        collect(s)

    for r in range(owned):
        for c in range(0, kc, 2):
            value = summed[r, :, c * BS:(c + 2) * BS]
            turned = pltpu.roll(value, BS, 1)
            blocks[r, c] = jnp.where(low, value, turned)
            blocks[r, c + 1] = jnp.where(low, turned, value)

    def place_row(r, carry):
        for c in range(kc):
            blocks[owned, c] = blocks[r, plan_s[rank_at + me, hs + r, c]]
        for c in range(0, kc, SUB):
            for t in range(tiles):
                out[r, c:c + SUB, t * LANES:(t + 1) * LANES] = jnp.where(
                    low, blocks[owned, c:c + SUB, 2 * t, :], blocks[owned, c:c + SUB, 2 * t + 1, :]
                )
        return carry

    lax.fori_loop(0, owned, place_row, 0)

    def drain(k, carry):
        halo_copy(k).wait_send()
        for s in range(len(stages)):
            part_copy(s, k).wait_send()
        return carry

    lax.fori_loop(1, n_dom, drain, 0)
    for step in range(n_grp - 1):
        for r in range(rows):
            for direction in range(2):
                origin = g - step if direction == 0 else g + step
                exists = (origin >= 0) & (origin < n_grp)

                @pl.when(exists & can_send[direction])
                def _():
                    line_copy(direction, step, r, table.at[r], origin).wait_send()


def per_device(
    operator_blocks, operator_cols, halo_count, prolong_blocks, prolong_cols,
    prolong_slot, send_lists, slot_owner_row, coarse_pattern,
):
    n_grp = lax.axis_size("grp")
    n_dom = lax.axis_size("dom")
    rows, ka = operator_cols.shape
    kp = prolong_cols.shape[1]
    owned, kc = coarse_pattern.shape
    hs = send_lists.shape[1] // n_dom
    cap = slot_owner_row.shape[1] // n_dom
    total_ids = owned * n_grp * n_dom
    used = n_dom + cap - 1
    panel_count = n_grp * rows + n_dom * hs
    groups = panel_count // rows
    width = rows * BS
    plan_rows = n_grp + 3 * n_dom
    stages = ((n_grp - 2, 0, kc),)
    assert n_dom & (n_dom - 1) == 0 and (n_dom * hs) % rows == 0 and n_dom * hs >= rows
    assert kp == SUB and ka % SUB == 0 and kc % SUB == 0 and LANES % kc == 0
    assert owned < rows and kc <= ka
    assert rows % 2 == 0 and rows <= SUB and hs + owned < SUB and (owned * n_dom) % 4 == 0
    vm = lambda dtype, *shape: pltpu.VMEM(shape, dtype)
    f32, bf16, i32 = jnp.float32, jnp.bfloat16, jnp.int32
    sem = lambda *shape: pltpu.SemaphoreType.DMA(shape)
    return pl.pallas_call(
        functools.partial(fused_kernel, n_grp, n_dom, rows, hs, ka, kp, kc, cap, owned, stages),
        out_shape=jax.ShapeDtypeStruct((owned, kc, BS * BS), f32),
        in_specs=[smem_spec()] * 5 + [vmem_spec()] * 2 + [any_spec()] * 2,
        out_specs=vmem_spec(),
        scratch_shapes=[
            vm(f32, rows, kp, BS * BS), vm(f32, rows, ka, BS * BS), vm(f32, panel_count, kp, BS * BS),
            vm(f32, n_dom * hs, kp, BS * BS),
            vm(i32, SUB, LANES), vm(i32, n_grp, SUB, LANES), vm(i32, SUB, LANES),
            vm(i32, n_dom, SUB, LANES), vm(i32, n_dom, SUB, LANES),
            vm(i32, plan_rows, SUB, LANES), pltpu.SMEM((plan_rows, SUB, LANES), i32),
            vm(f32, rows, ka, BS, LANES), vm(bf16, groups, width, 2 * width),
            vm(f32, rows * kp + 1, BS, LANES), vm(f32, kp, BS, LANES),
            vm(bf16, (rows + n_dom * hs) * kp + 1, 2 * BS, LANES), vm(bf16, used, 2 * BS, width),
            vm(bf16, total_ids, width, LANES),
            vm(f32, used, BS, kc * BS), vm(f32, n_dom - 1, BS, kc * BS), vm(f32, owned, BS, kc * BS),
            sem(2), sem(2, n_grp - 1, rows), sem(2, n_grp - 1, rows), sem(n_dom), sem(n_dom),
            sem(n_grp), sem(n_grp), sem(n_dom), sem(n_dom), sem(1),
            sem(len(stages), n_dom - 1), sem(len(stages), n_dom - 1),
        ],
        compiler_params=pltpu.CompilerParams(
            collective_id=0, has_side_effects=True, vmem_limit_bytes=67043328
        ),
        name="coarse_rows",
    )(
        operator_cols, halo_count, prolong_slot, send_lists, slot_owner_row, prolong_cols, coarse_pattern,
        prolong_blocks, operator_blocks,
    )


def solution(mesh):
    blocks = P(("grp", "dom"), None, None)
    lists = P(("grp", "dom"), None)
    return jax.shard_map(
        per_device,
        mesh=mesh,
        in_specs=(blocks, lists, P(("grp", "dom")), blocks, lists, lists, lists, lists, lists),
        out_specs=blocks,
        check_vma=False,
    )
```

```python
import functools

import jax
import jax.numpy as jnp
from jax import lax
from jax.experimental import pallas as pl
from jax.experimental.pallas import tpu as pltpu
from jax.sharding import PartitionSpec as P

BS = 64
KG = 12
LANES = 128
SUB = 8


def any_spec():
    return pl.BlockSpec(memory_space=pl.ANY)


def vmem_spec():
    return pl.BlockSpec(memory_space=pltpu.VMEM)


def smem_spec():
    return pl.BlockSpec(memory_space=pltpu.SMEM)


def fused_kernel(
    n_grp, n_dom, rows, hs, ka, kp, kc, cap, owned, stages,
    cols, halo, slots, picked, owner, prolong_cols, pattern, prolong_in, operator_in,
    out, late,
    own_raw, operator, table, outgoing, grp_out, grp_in, dom_base, dom_out, dom_in, plan_v, plan_s,
    blocks, dense, own_dup, stage, panels, left, ap, partial, arrived, summed,
    load_sem, line_send, line_recv, halo_send, halo_recv,
    gmeta_send, gmeta_recv, dmeta_send, dmeta_recv, plan_sem, part_send, part_recv,
    late_out, late_in, late_send, late_recv,
):
    g = lax.axis_index("grp")
    me = lax.axis_index("dom")
    near_count = n_grp * rows
    plane_ids = owned * n_dom
    halo_count_rows = n_dom * hs
    groups = n_grp + halo_count_rows // rows
    zero_at = (rows + halo_count_rows) * kp
    row_at = hs + owned
    sort_at = n_grp + n_dom
    rank_at = sort_at + n_dom
    width = rows * BS
    tiles = BS // 2
    low = lax.broadcasted_iota(jnp.int32, (1, LANES), 1) < BS
    lane = lax.broadcasted_iota(jnp.int32, (SUB, LANES), 1)
    sub = lax.broadcasted_iota(jnp.int32, (SUB, LANES), 0)

    barrier = pltpu.get_barrier_semaphore()
    for k in range(1, n_grp):
        pl.semaphore_signal(barrier, inc=1, device_id={"grp": lax.rem(g + k, n_grp)})
    for k in range(1, n_dom):
        pl.semaphore_signal(barrier, inc=1, device_id={"dom": lax.rem(me + k, n_dom)})
    own_load = pltpu.make_async_copy(prolong_in, own_raw, load_sem.at[0])
    operator_load = pltpu.make_async_copy(operator_in, operator, load_sem.at[1])
    own_load.start()
    operator_load.start()

    def partner(k):
        other = 0
        bit = 1
        while bit < n_dom:
            other += lax.rem(me // bit + k // bit, 2) * bit
            bit *= 2
        return other

    grp_out[...] = jnp.zeros(grp_out.shape, jnp.int32)
    grp_out[0:rows, 0:kp] = prolong_cols[...]
    dom_base[...] = jnp.zeros(dom_base.shape, jnp.int32)
    for r in range(owned):
        for j in range(0, LANES, kc):
            dom_base[hs + r:hs + r + 1, j:j + kc] = pattern[r:r + 1, :]

    def for_dom(d, carry):
        dom_out[d] = dom_base[...]
        for h in range(hs):
            dom_out[d, h:h + 1, 0:kp] = prolong_cols[pl.ds(picked[0, d * hs + h], 1), :]
        dom_out[d, row_at:row_at + 1, :] = jnp.full((1, LANES), owner[0, d * cap], jnp.int32)
        return carry

    lax.fori_loop(0, n_dom, for_dom, 0)
    grp_in[g] = grp_out[...]
    dom_in[me] = dom_out[me]
    pl.semaphore_wait(barrier, n_grp + n_dom - 2)

    def line_copy(direction, step, r, src, origin):
        return pltpu.make_async_remote_copy(
            src_ref=src, dst_ref=table.at[origin * rows + r],
            send_sem=line_send.at[direction, step, r], recv_sem=line_recv.at[direction, step, r],
            device_id={"grp": g + 1 if direction == 0 else g - 1},
        )

    def grp_meta(k):
        return pltpu.make_async_remote_copy(
            src_ref=grp_out, dst_ref=grp_in.at[g], send_sem=gmeta_send.at[k], recv_sem=gmeta_recv.at[k],
            device_id={"grp": lax.rem(g + k, n_grp)},
        )

    def dom_meta(k):
        target = partner(k)
        return pltpu.make_async_remote_copy(
            src_ref=dom_out.at[target], dst_ref=dom_in.at[me], send_sem=dmeta_send.at[k], recv_sem=dmeta_recv.at[k],
            device_id={"dom": target},
        )

    def halo_copy(k):
        target = partner(k)
        return pltpu.make_async_remote_copy(
            src_ref=outgoing.at[pl.ds(target * hs, hs)], dst_ref=table.at[pl.ds(near_count + me * hs, hs)],
            send_sem=halo_send.at[k], recv_sem=halo_recv.at[k],
            device_id={"dom": target},
        )

    for k in range(1, n_grp):
        grp_meta(k).start()

    def start_dom_meta(k, carry):
        dom_meta(k).start()
        return carry

    lax.fori_loop(1, n_dom, start_dom_meta, 0)
    can_send = (g < n_grp - 1, g > 0)
    for r in range(rows):
        for direction in range(2):
            @pl.when(can_send[direction])
            def _():
                line_copy(direction, 0, r, prolong_in.at[r], g).start()

    own_load.wait()

    def pick(n, carry):
        outgoing[n] = own_raw[picked[0, n]]
        return carry

    lax.fori_loop(0, halo_count_rows, pick, 0)

    def duplicate(x, write, at):
        turned = pltpu.roll(x, BS, 1)
        write(at, jnp.where(low, x, turned))
        write(at + 1, jnp.where(low, turned, x))

    def own_row(i, carry):
        def write(a, value):
            own_dup[pl.ds(i * kp, kp), a, :] = value

        for t in range(tiles):
            duplicate(own_raw[i, :, t * LANES:(t + 1) * LANES], write, 2 * t)
        return carry

    lax.fori_loop(0, rows, own_row, 0)

    def start_halo(k, carry):
        halo_copy(k).start()
        return carry

    lax.fori_loop(1, n_dom, start_halo, 0)
    own_dup[rows * kp] = jnp.zeros((BS, LANES), jnp.float32)
    panels[zero_at] = jnp.zeros((2 * BS, LANES), jnp.bfloat16)

    def split(value):
        high = value.astype(jnp.bfloat16)
        return high, (value - high.astype(jnp.float32)).astype(jnp.bfloat16)

    def keep(at, value):
        high, rest = split(value)
        panels[at, 0:BS] = high
        panels[at, BS:2 * BS] = rest

    def convert(panel, place):
        def write(a, value):
            stage[:, a, :] = value

        for t in range(tiles):
            duplicate(table[panel, :, t * LANES:(t + 1) * LANES], write, 2 * t)
        for q in range(kp):
            keep(place * kp + q, stage[q])

    operator_load.wait()

    def relay(n, carry):
        i = n // (ka // SUB)
        m = lax.rem(n, ka // SUB) * SUB

        def write(a, value):
            blocks[i, pl.ds(m, SUB), a, :] = value

        for t in range(tiles):
            duplicate(operator[i, pl.ds(m, SUB), t * LANES:(t + 1) * LANES], write, 2 * t)
        return carry

    lax.fori_loop(0, rows * (ka // SUB), relay, 0)

    def densify(i, group, slots_used, column_of):
        for pair in range(0, rows, 2):
            first = group * rows + pair
            wanted = jnp.where(low, first, first + 1)
            total = jnp.zeros((BS, LANES), jnp.float32)
            for m in slots_used:
                total += jnp.where(wanted == column_of(i, m), blocks[i, m], 0.0)
            high, rest = split(total)
            here = pl.ds(i * BS, BS)
            dense[group, here, pair * BS:(pair + 2) * BS] = high
            dense[group, here, width + pair * BS:width + (pair + 2) * BS] = rest

    def near_dense(n, carry):
        densify(n // n_grp, lax.rem(n, n_grp), range(KG), lambda i, m: cols[i, m])
        return carry

    def far_column(i, m):
        return jnp.where(m - KG < halo[i], near_count + cols[i, m], -1)

    far_groups = groups - n_grp

    def far_dense(n, carry):
        densify(n // far_groups, n_grp + lax.rem(n, far_groups), range(KG, ka), far_column)
        return carry

    lax.fori_loop(0, rows * n_grp, near_dense, 0)
    lax.fori_loop(0, rows * far_groups, far_dense, 0)

    for k in range(1, n_grp):
        grp_meta(k).wait()

    def wait_dom_meta(k, carry):
        dom_meta(k).wait()
        return carry

    lax.fori_loop(1, n_dom, wait_dom_meta, 0)

    def places(values, first_id, first_place):
        found = jnp.full((SUB, LANES), zero_at, jnp.int32)
        for q in range(kp):
            found = jnp.where(values[:, q:q + 1] == first_id + lane, (first_place + sub) * kp + q, found)
        return found

    for origin in range(n_grp):
        side = (origin > g).astype(jnp.int32)
        plan_v[origin] = places(grp_in[origin], origin * plane_ids, side * rows)

    slot_of_lane = lax.rem(lane, kc)

    pattern_line = (sub >= hs) & (sub < hs + owned)

    def dom_tables(d, wrong):
        values = dom_in[d]
        plan_v[n_grp + d] = places(values, g * plane_ids, rows + d * hs)
        plane = jnp.zeros((SUB, LANES), jnp.int32)
        for n in range(1, n_grp):
            plane += (values >= n * plane_ids).astype(jnp.int32)
        distance = jnp.abs(plane - g)
        order = distance * kc + slot_of_lane
        rank = jnp.zeros((SUB, LANES), jnp.int32)
        for s in range(1, kc):
            rank += (pltpu.roll(order, s, 1) < order).astype(jnp.int32)
        ordered = values
        for s in range(kc):
            ordered = jnp.where(pltpu.roll(rank, s, 1) == slot_of_lane, pltpu.roll(values, s, 1), ordered)
        plan_v[sort_at + d] = ordered
        plan_v[rank_at + d] = rank
        for after, _, last in stages:
            wrong |= (pattern_line & (rank < last) & (distance > after + 1)).astype(jnp.int32)
        return wrong

    wrong = lax.fori_loop(0, n_dom, dom_tables, jnp.zeros((SUB, LANES), jnp.int32))
    plan_copy = pltpu.make_async_copy(plan_v, plan_s, plan_sem.at[0])
    plan_copy.start()
    late_out[...] = wrong
    late_in[g] = wrong

    def late_copy(k):
        return pltpu.make_async_remote_copy(
            src_ref=late_out, dst_ref=late_in.at[g], send_sem=late_send.at[k], recv_sem=late_recv.at[k],
            device_id={"grp": lax.rem(g + k, n_grp)},
        )


    def transposed(slot, at):
        for pair in range(0, rows, 2):
            both = []
            for i in range(pair, pair + 2):
                place = jnp.int32(rows * kp)
                for j in range(kp):
                    place = jnp.where(slots[i, j] == slot, i * kp + j, place)
                both.append(own_dup[place])
            turned = jnp.concatenate(both, axis=0).T
            high = turned.astype(jnp.bfloat16).astype(jnp.float32)
            upper = lax.broadcasted_iota(jnp.int32, (LANES, LANES), 0) < BS
            left[at, :, pair * BS:(pair + 2) * BS] = jnp.where(upper, high, turned - high).astype(jnp.bfloat16)

    def far_left(k, carry):
        transposed(partner(k) * cap, k)
        return carry

    lax.fori_loop(1, n_dom, far_left, 0)
    for k in range(1, n_grp):
        late_copy(k).start()
    for t in range(cap):
        transposed(me * cap + t, 0 if t == 0 else n_dom + t - 1)

    def own_panels(n, carry):
        keep(n, own_dup[n])
        return carry

    lax.fori_loop(0, rows * kp, own_panels, 0)
    plan_copy.wait()

    def multiply(plane, parts):
        def four(n, carry):
            e = n * 4
            total = None
            for group, index_of in parts:
                halves = []
                for pair in range(2):
                    blocks_here = [
                        jnp.where(low, panels[index_of(r, e + 2 * pair)], panels[index_of(r, e + 2 * pair + 1)])
                        for r in range(rows)
                    ]
                    high = [b[0:BS] for b in blocks_here]
                    rest = [b[BS:2 * BS] for b in blocks_here]
                    halves.append(jnp.concatenate(high + rest + high, axis=0))
                right = jnp.concatenate(halves, axis=1)
                split_dense = dense[group]
                lhs = jnp.concatenate([split_dense[:, 0:width], split_dense], axis=1)
                product = jnp.dot(lhs, right, preferred_element_type=jnp.float32)
                total = product if total is None else total + product
            for pair in range(2):
                value = total[:, pair * LANES:(pair + 1) * LANES]
                high = value.astype(jnp.bfloat16).astype(jnp.float32)
                rest = value - high
                turned = pltpu.roll(jnp.where(low, rest, high), BS, 1)
                at = plane * plane_ids + e + 2 * pair
                ap[at] = jnp.where(low, high, turned).astype(jnp.bfloat16)
                ap[at + 1] = jnp.where(low, turned, rest).astype(jnp.bfloat16)
            return carry

        lax.fori_loop(0, plane_ids // 4, four, 0)

    def near_index(origin):
        return lambda r, e: plan_s[origin, r, e]

    def far_index(group):
        def index_of(r, e):
            n = group * rows + r
            return plan_s[n_grp + n // hs, n % hs, e]
        return index_of

    def part_copy(s, k):
        first, last = stages[s][1:]
        here = pl.ds(first * BS, (last - first) * BS)
        return pltpu.make_async_remote_copy(
            src_ref=partial.at[k, :, here], dst_ref=arrived.at[k - 1, :, here],
            send_sem=part_send.at[s, k - 1], recv_sem=part_recv.at[s, k - 1],
            device_id={"dom": partner(k)},
        )

    def slot_rows(s, owner_dom, slot, at):
        first, last = stages[s][1:]
        line = hs + owner[0, slot]
        for c in range(first, last, 2):
            right = jnp.concatenate([ap[plan_s[sort_at + owner_dom, line, c + h]] for h in range(2)], axis=1)
            product = jnp.dot(left[at], right, preferred_element_type=jnp.float32)
            both = product[:BS] + product[BS:]
            one, two = both[:, :LANES], both[:, LANES:]
            partial[at, :, c * BS:(c + 2) * BS] = jnp.where(low, one, two) + pltpu.roll(jnp.where(low, two, one), BS, 1)

    def exchange(s):
        first, last = stages[s][1:]
        here = slice(first * BS, last * BS)

        def far_slot(step, carry):
            k = n_dom - step
            target = partner(k)
            slot_rows(s, target, target * cap, k)

            @pl.when(step > 1)
            def _():
                part_copy(s, k + 1).start()

            return carry

        lax.fori_loop(1, n_dom, far_slot, 0)
        slot_rows(s, me, me * cap, 0)
        part_copy(s, 1).start()
        for t in range(1, cap):
            slot_rows(s, me, me * cap + t, n_dom + t - 1)
        for r in range(owned):
            total = partial[0, :, here] * (owner[0, me * cap] == r).astype(jnp.float32)
            for t in range(1, cap):
                total += partial[n_dom + t - 1, :, here] * (owner[0, me * cap + t] == r).astype(jnp.float32)
            summed[r, :, here] = total

    def collect(s):
        first, last = stages[s][1:]

        def one(step, carry):
            k = n_dom - step
            part_copy(s, k).wait_recv()
            row = dom_in[partner(k), row_at:row_at + 1, :]
            for c in range(first, last, 2):
                here = slice(c * BS, (c + 2) * BS)
                value = arrived[k - 1, :, here]
                for r in range(owned):
                    summed[r, :, here] += jnp.where(row == r, value, 0.0)
            return carry

        lax.fori_loop(1, n_dom, one, 0)

    def take_halo(k, carry):
        halo_copy(k).wait_recv()
        for h in range(hs):
            convert(near_count + partner(k) * hs + h, rows + partner(k) * hs + h)
        return carry

    def own_halo(h, carry):
        def write(a, value):
            stage[:, a, :] = value

        for t in range(tiles):
            duplicate(outgoing[me * hs + h, :, t * LANES:(t + 1) * LANES], write, 2 * t)
        for q in range(kp):
            keep((rows + me * hs + h) * kp + q, stage[q])
        return carry

    for step in range(n_grp - 1):
        origins = (g - 1 - step, g + 1 + step)
        exists = (origins[0] >= 0, origins[1] < n_grp)
        for r in range(rows):
            for direction in range(2):
                origin = origins[direction]

                @pl.when(exists[direction])
                def _():
                    line_copy(direction, step, r, table.at[origin * rows + r], origin).wait_recv()

                if step < n_grp - 2:
                    @pl.when(exists[direction] & can_send[direction])
                    def _():
                        line_copy(direction, step + 1, r, table.at[origin * rows + r], origin).start()

            if step > 0:
                for direction in range(2):
                    @pl.when(exists[direction])
                    def _():
                        convert(origins[direction] * rows + r, direction * rows + r)
        if step == 0:
            lax.fori_loop(0, hs, own_halo, 0)
            lax.fori_loop(1, n_dom, take_halo, 0)
            multiply(g, [(g, near_index(g))] + [(n_grp + n, far_index(n)) for n in range(far_groups)])
            for s in range(len(stages)):
                if stages[s][0] < 0:
                    exchange(s)
        for direction in range(2):
            @pl.when(exists[direction])
            def _():
                if step == 0:
                    def take(r, carry):
                        convert(origins[direction] * rows + r, direction * rows + r)
                        return carry

                    lax.fori_loop(0, rows, take, 0)
                multiply(origins[direction], [(origins[direction], near_index(origins[direction]))])
        for s in range(len(stages)):
            if stages[s][0] == step:
                exchange(s)

    for k in range(1, n_grp):
        late_copy(k).wait()
    anywhere = late_in[0]
    for k in range(1, n_grp):
        anywhere |= late_in[k]
    late[...] = jnp.broadcast_to(jnp.max(jnp.max(anywhere, axis=0, keepdims=True), axis=1, keepdims=True), (SUB, LANES))

    for s in range(len(stages)):
        collect(s)

    for r in range(owned):
        for c in range(0, kc, 2):
            value = summed[r, :, c * BS:(c + 2) * BS]
            turned = pltpu.roll(value, BS, 1)
            blocks[r, c] = jnp.where(low, value, turned)
            blocks[r, c + 1] = jnp.where(low, turned, value)

    def place_row(r, carry):
        for c in range(kc):
            blocks[owned, c] = blocks[r, plan_s[rank_at + me, hs + r, c]]
        for c in range(0, kc, SUB):
            for t in range(tiles):
                out[r, c:c + SUB, t * LANES:(t + 1) * LANES] = jnp.where(
                    low, blocks[owned, c:c + SUB, 2 * t, :], blocks[owned, c:c + SUB, 2 * t + 1, :]
                )
        return carry

    lax.fori_loop(0, owned, place_row, 0)

    def drain(k, carry):
        halo_copy(k).wait_send()
        for s in range(len(stages)):
            part_copy(s, k).wait_send()
        return carry

    lax.fori_loop(1, n_dom, drain, 0)
    for step in range(n_grp - 1):
        for r in range(rows):
            for direction in range(2):
                origin = g - step if direction == 0 else g + step
                exists = (origin >= 0) & (origin < n_grp)

                @pl.when(exists & can_send[direction])
                def _():
                    line_copy(direction, step, r, table.at[r], origin).wait_send()


def per_device(
    operator_blocks, operator_cols, halo_count, prolong_blocks, prolong_cols,
    prolong_slot, send_lists, slot_owner_row, coarse_pattern,
):
    n_grp = lax.axis_size("grp")
    n_dom = lax.axis_size("dom")
    rows, ka = operator_cols.shape
    kp = prolong_cols.shape[1]
    owned, kc = coarse_pattern.shape
    hs = send_lists.shape[1] // n_dom
    cap = slot_owner_row.shape[1] // n_dom
    total_ids = owned * n_grp * n_dom
    used = n_dom + cap - 1
    panel_count = n_grp * rows + n_dom * hs
    groups = panel_count // rows
    width = rows * BS
    plan_rows = n_grp + 3 * n_dom
    quarter, half = kc // 4, kc // 2
    at_once = ((n_grp - 2, 0, kc),)
    by_distance = ((n_grp - 4, 0, quarter), (n_grp - 3, quarter, half), (n_grp - 2, half, kc))
    assert n_grp >= 3 and quarter % 2 == 0
    assert n_dom & (n_dom - 1) == 0 and (n_dom * hs) % rows == 0 and n_dom * hs >= rows
    assert kp == SUB and ka % SUB == 0 and kc % SUB == 0 and LANES % kc == 0
    assert owned < rows and kc <= ka
    assert rows % 2 == 0 and rows <= SUB and hs + owned < SUB and (owned * n_dom) % 4 == 0
    vm = lambda dtype, *shape: pltpu.VMEM(shape, dtype)
    f32, bf16, i32 = jnp.float32, jnp.bfloat16, jnp.int32
    sem = lambda *shape: pltpu.SemaphoreType.DMA(shape)
    call = lambda stages, number, name: pl.pallas_call(
        functools.partial(fused_kernel, n_grp, n_dom, rows, hs, ka, kp, kc, cap, owned, stages),
        out_shape=(jax.ShapeDtypeStruct((owned, kc, BS * BS), f32), jax.ShapeDtypeStruct((SUB, LANES), i32)),
        in_specs=[smem_spec()] * 5 + [vmem_spec()] * 2 + [any_spec()] * 2,
        out_specs=(vmem_spec(), vmem_spec()),
        scratch_shapes=[
            vm(f32, rows, kp, BS * BS), vm(f32, rows, ka, BS * BS), vm(f32, panel_count, kp, BS * BS),
            vm(f32, n_dom * hs, kp, BS * BS),
            vm(i32, SUB, LANES), vm(i32, n_grp, SUB, LANES), vm(i32, SUB, LANES),
            vm(i32, n_dom, SUB, LANES), vm(i32, n_dom, SUB, LANES),
            vm(i32, plan_rows, SUB, LANES), pltpu.SMEM((plan_rows, SUB, LANES), i32),
            vm(f32, rows, ka, BS, LANES), vm(bf16, groups, width, 2 * width),
            vm(f32, rows * kp + 1, BS, LANES), vm(f32, kp, BS, LANES),
            vm(bf16, (rows + n_dom * hs) * kp + 1, 2 * BS, LANES), vm(bf16, used, 2 * BS, width),
            vm(bf16, total_ids, width, LANES),
            vm(f32, used, BS, kc * BS), vm(f32, n_dom - 1, BS, kc * BS), vm(f32, owned, BS, kc * BS),
            sem(2), sem(2, n_grp - 1, rows), sem(2, n_grp - 1, rows), sem(n_dom), sem(n_dom),
            sem(n_grp), sem(n_grp), sem(n_dom), sem(n_dom), sem(1),
            sem(len(stages), n_dom - 1), sem(len(stages), n_dom - 1),
            vm(i32, SUB, LANES), vm(i32, n_grp, SUB, LANES), sem(n_grp), sem(n_grp),
        ],
        compiler_params=pltpu.CompilerParams(
            collective_id=number, has_side_effects=True, vmem_limit_bytes=67043328
        ),
        name=name,
    )
    args = (
        operator_cols, halo_count, prolong_slot, send_lists, slot_owner_row, prolong_cols, coarse_pattern,
        prolong_blocks, operator_blocks,
    )
    result, late = call(by_distance, 0, "coarse_rows")(*args)
    return lax.cond(late[0, 0] > 0, lambda: call(at_once, 1, "coarse_rows_at_once")(*args)[0], lambda: result)


def solution(mesh):
    blocks = P(("grp", "dom"), None, None)
    lists = P(("grp", "dom"), None)
    return jax.shard_map(
        per_device,
        mesh=mesh,
        in_specs=(blocks, lists, P(("grp", "dom")), blocks, lists, lists, lists, lists, lists),
        out_specs=blocks,
        check_vma=False,
    )
```

```python
import functools

import jax
import jax.numpy as jnp
from jax import lax
from jax.experimental import pallas as pl
from jax.experimental.pallas import tpu as pltpu
from jax.sharding import PartitionSpec as P

BS = 64
KG = 12
LANES = 128
SUB = 8


def any_spec():
    return pl.BlockSpec(memory_space=pl.ANY)


def vmem_spec():
    return pl.BlockSpec(memory_space=pltpu.VMEM)


def smem_spec():
    return pl.BlockSpec(memory_space=pltpu.SMEM)


def fused_kernel(
    n_grp, n_dom, rows, hs, ka, kp, kc, cap, owned, stages,
    cols, halo, slots, picked, owner, prolong_cols, pattern, prolong_in, operator_in,
    out, late,
    own_raw, operator, table, outgoing, grp_out, grp_in, dom_base, dom_out, dom_in, plan_v, plan_s,
    blocks, dense, own_dup, stage, panels, left, ap, partial, arrived, summed,
    load_sem, line_send, line_recv, halo_send, halo_recv,
    gmeta_send, gmeta_recv, dmeta_send, dmeta_recv, plan_sem, part_send, part_recv,
    late_out, late_in, late_send, late_recv,
):
    g = lax.axis_index("grp")
    me = lax.axis_index("dom")
    near_count = n_grp * rows
    plane_ids = owned * n_dom
    halo_count_rows = n_dom * hs
    groups = n_grp + halo_count_rows // rows
    zero_at = (rows + halo_count_rows) * kp
    row_at = hs + owned
    sort_at = n_grp + n_dom
    rank_at = sort_at + n_dom
    width = rows * BS
    tiles = BS // 2
    low = lax.broadcasted_iota(jnp.int32, (1, LANES), 1) < BS
    lane = lax.broadcasted_iota(jnp.int32, (SUB, LANES), 1)
    sub = lax.broadcasted_iota(jnp.int32, (SUB, LANES), 0)

    barrier = pltpu.get_barrier_semaphore()
    for k in range(1, n_grp):
        pl.semaphore_signal(barrier, inc=1, device_id={"grp": lax.rem(g + k, n_grp)})
    for k in range(1, n_dom):
        pl.semaphore_signal(barrier, inc=1, device_id={"dom": lax.rem(me + k, n_dom)})
    own_load = pltpu.make_async_copy(prolong_in, own_raw, load_sem.at[0])
    operator_load = pltpu.make_async_copy(operator_in, operator, load_sem.at[1])
    own_load.start()
    operator_load.start()

    def partner(k):
        other = 0
        bit = 1
        while bit < n_dom:
            other += lax.rem(me // bit + k // bit, 2) * bit
            bit *= 2
        return other

    grp_out[...] = jnp.zeros(grp_out.shape, jnp.int32)
    grp_out[0:rows, 0:kp] = prolong_cols[...]
    dom_base[...] = jnp.zeros(dom_base.shape, jnp.int32)
    for r in range(owned):
        for j in range(0, LANES, kc):
            dom_base[hs + r:hs + r + 1, j:j + kc] = pattern[r:r + 1, :]

    def for_dom(d, carry):
        dom_out[d] = dom_base[...]
        for h in range(hs):
            dom_out[d, h:h + 1, 0:kp] = prolong_cols[pl.ds(picked[0, d * hs + h], 1), :]
        dom_out[d, row_at:row_at + 1, :] = jnp.full((1, LANES), owner[0, d * cap], jnp.int32)
        return carry

    lax.fori_loop(0, n_dom, for_dom, 0)
    grp_in[g] = grp_out[...]
    dom_in[me] = dom_out[me]
    pl.semaphore_wait(barrier, n_grp + n_dom - 2)

    def line_copy(direction, step, r, src, origin):
        return pltpu.make_async_remote_copy(
            src_ref=src, dst_ref=table.at[origin * rows + r],
            send_sem=line_send.at[direction, step, r], recv_sem=line_recv.at[direction, step, r],
            device_id={"grp": g + 1 if direction == 0 else g - 1},
        )

    def grp_meta(k):
        return pltpu.make_async_remote_copy(
            src_ref=grp_out, dst_ref=grp_in.at[g], send_sem=gmeta_send.at[k], recv_sem=gmeta_recv.at[k],
            device_id={"grp": lax.rem(g + k, n_grp)},
        )

    def dom_meta(k):
        target = partner(k)
        return pltpu.make_async_remote_copy(
            src_ref=dom_out.at[target], dst_ref=dom_in.at[me], send_sem=dmeta_send.at[k], recv_sem=dmeta_recv.at[k],
            device_id={"dom": target},
        )

    def halo_copy(k):
        target = partner(k)
        return pltpu.make_async_remote_copy(
            src_ref=outgoing.at[pl.ds(target * hs, hs)], dst_ref=table.at[pl.ds(near_count + me * hs, hs)],
            send_sem=halo_send.at[k], recv_sem=halo_recv.at[k],
            device_id={"dom": target},
        )

    for k in range(1, n_grp):
        grp_meta(k).start()

    def start_dom_meta(k, carry):
        dom_meta(k).start()
        return carry

    lax.fori_loop(1, n_dom, start_dom_meta, 0)
    can_send = (g < n_grp - 1, g > 0)
    for r in range(rows):
        for direction in range(2):
            @pl.when(can_send[direction])
            def _():
                line_copy(direction, 0, r, prolong_in.at[r], g).start()

    own_load.wait()

    def pick(n, carry):
        outgoing[n] = own_raw[picked[0, n]]
        return carry

    lax.fori_loop(0, halo_count_rows, pick, 0)

    def duplicate(x, write, at):
        turned = pltpu.roll(x, BS, 1)
        write(at, jnp.where(low, x, turned))
        write(at + 1, jnp.where(low, turned, x))

    def own_row(i, carry):
        def write(a, value):
            own_dup[pl.ds(i * kp, kp), a, :] = value

        for t in range(tiles):
            duplicate(own_raw[i, :, t * LANES:(t + 1) * LANES], write, 2 * t)
        return carry

    lax.fori_loop(0, rows, own_row, 0)

    def start_halo(k, carry):
        halo_copy(k).start()
        return carry

    lax.fori_loop(1, n_dom, start_halo, 0)
    own_dup[rows * kp] = jnp.zeros((BS, LANES), jnp.float32)
    panels[zero_at] = jnp.zeros((2 * BS, LANES), jnp.bfloat16)

    def split(value):
        high = value.astype(jnp.bfloat16)
        return high, (value - high.astype(jnp.float32)).astype(jnp.bfloat16)

    def keep(at, value):
        high, rest = split(value)
        panels[at, 0:BS] = high
        panels[at, BS:2 * BS] = rest

    def convert(panel, place):
        def write(a, value):
            stage[:, a, :] = value

        for t in range(tiles):
            duplicate(table[panel, :, t * LANES:(t + 1) * LANES], write, 2 * t)
        for q in range(kp):
            keep(place * kp + q, stage[q])

    operator_load.wait()

    def relay(n, carry):
        i = n // (ka // SUB)
        m = lax.rem(n, ka // SUB) * SUB

        def write(a, value):
            blocks[i, pl.ds(m, SUB), a, :] = value

        for t in range(tiles):
            duplicate(operator[i, pl.ds(m, SUB), t * LANES:(t + 1) * LANES], write, 2 * t)
        return carry

    lax.fori_loop(0, rows * (ka // SUB), relay, 0)

    def densify(i, group, slots_used, column_of):
        for pair in range(0, rows, 2):
            first = group * rows + pair
            wanted = jnp.where(low, first, first + 1)
            total = jnp.zeros((BS, LANES), jnp.float32)
            for m in slots_used:
                total += jnp.where(wanted == column_of(i, m), blocks[i, m], 0.0)
            high, rest = split(total)
            here = pl.ds(i * BS, BS)
            dense[group, here, pair * BS:(pair + 2) * BS] = high
            dense[group, here, width + pair * BS:width + (pair + 2) * BS] = rest

    def near_dense(n, carry):
        densify(n // n_grp, lax.rem(n, n_grp), range(KG), lambda i, m: cols[i, m])
        return carry

    def far_column(i, m):
        return jnp.where(m - KG < halo[i], near_count + cols[i, m], -1)

    far_groups = groups - n_grp

    def far_dense(n, carry):
        densify(n // far_groups, n_grp + lax.rem(n, far_groups), range(KG, ka), far_column)
        return carry

    lax.fori_loop(0, rows * n_grp, near_dense, 0)
    lax.fori_loop(0, rows * far_groups, far_dense, 0)

    for k in range(1, n_grp):
        grp_meta(k).wait()

    def wait_dom_meta(k, carry):
        dom_meta(k).wait()
        return carry

    lax.fori_loop(1, n_dom, wait_dom_meta, 0)

    def places(values, first_id, first_place):
        found = jnp.full((SUB, LANES), zero_at, jnp.int32)
        for q in range(kp):
            found = jnp.where(values[:, q:q + 1] == first_id + lane, (first_place + sub) * kp + q, found)
        return found

    for origin in range(n_grp):
        side = (origin > g).astype(jnp.int32)
        plan_v[origin] = places(grp_in[origin], origin * plane_ids, side * rows)

    slot_of_lane = lax.rem(lane, kc)

    pattern_line = (sub >= hs) & (sub < hs + owned)

    def dom_tables(d, wrong):
        values = dom_in[d]
        plan_v[n_grp + d] = places(values, g * plane_ids, rows + d * hs)
        plane = jnp.zeros((SUB, LANES), jnp.int32)
        for n in range(1, n_grp):
            plane += (values >= n * plane_ids).astype(jnp.int32)
        distance = jnp.abs(plane - g)
        order = distance * kc + slot_of_lane
        rank = jnp.zeros((SUB, LANES), jnp.int32)
        for s in range(1, kc):
            rank += (pltpu.roll(order, s, 1) < order).astype(jnp.int32)
        ordered = values
        for s in range(kc):
            ordered = jnp.where(pltpu.roll(rank, s, 1) == slot_of_lane, pltpu.roll(values, s, 1), ordered)
        plan_v[sort_at + d] = ordered
        plan_v[rank_at + d] = rank
        for after, _, last in stages:
            wrong |= (pattern_line & (rank < last) & (distance > after + 1)).astype(jnp.int32)
        return wrong

    wrong = lax.fori_loop(0, n_dom, dom_tables, jnp.zeros((SUB, LANES), jnp.int32))
    plan_copy = pltpu.make_async_copy(plan_v, plan_s, plan_sem.at[0])
    plan_copy.start()
    late_out[...] = wrong
    late_in[g] = wrong

    def late_copy(k):
        return pltpu.make_async_remote_copy(
            src_ref=late_out, dst_ref=late_in.at[g], send_sem=late_send.at[k], recv_sem=late_recv.at[k],
            device_id={"grp": lax.rem(g + k, n_grp)},
        )


    def transposed(slot, at):
        for pair in range(0, rows, 2):
            both = []
            for i in range(pair, pair + 2):
                place = jnp.int32(rows * kp)
                for j in range(kp):
                    place = jnp.where(slots[i, j] == slot, i * kp + j, place)
                both.append(own_dup[place])
            turned = jnp.concatenate(both, axis=0).T
            high = turned.astype(jnp.bfloat16).astype(jnp.float32)
            upper = lax.broadcasted_iota(jnp.int32, (LANES, LANES), 0) < BS
            left[at, :, pair * BS:(pair + 2) * BS] = jnp.where(upper, high, turned - high).astype(jnp.bfloat16)

    def far_left(k, carry):
        transposed(partner(k) * cap, k)
        return carry

    lax.fori_loop(1, n_dom, far_left, 0)
    for k in range(1, n_grp):
        late_copy(k).start()
    for t in range(cap):
        transposed(me * cap + t, 0 if t == 0 else n_dom + t - 1)

    def own_panels(n, carry):
        keep(n, own_dup[n])
        return carry

    lax.fori_loop(0, rows * kp, own_panels, 0)
    plan_copy.wait()

    def multiply(plane, parts, used_rows=range(rows), saved=None, last=True):
        def four(n, carry):
            e = n * 4
            total = None
            for group, index_of in parts:
                halves = []
                for pair in range(2):
                    blocks_here = [
                        jnp.where(low, panels[index_of(r, e + 2 * pair)], panels[index_of(r, e + 2 * pair + 1)])
                        for r in used_rows
                    ]
                    high = [b[0:BS] for b in blocks_here]
                    rest = [b[BS:2 * BS] for b in blocks_here]
                    halves.append(jnp.concatenate(high + rest + high, axis=0))
                right = jnp.concatenate(halves, axis=1)
                first, depth = used_rows[0] * BS, len(used_rows) * BS
                lhs_high = dense[group, :, first:first + depth]
                lhs = jnp.concatenate([lhs_high, lhs_high, dense[group, :, width + first:width + first + depth]], axis=1)
                product = jnp.dot(lhs, right, preferred_element_type=jnp.float32)
                total = product if total is None else total + product
            for pair in range(2):
                value = total[:, pair * LANES:(pair + 1) * LANES]
                if not last:
                    for i in range(rows):
                        blocks[i, saved + 2 * n + pair] = value[i * BS:(i + 1) * BS]
                    continue
                if saved is not None:
                    value += jnp.concatenate([blocks[i, saved + 2 * n + pair] for i in range(rows)], axis=0)
                high = value.astype(jnp.bfloat16).astype(jnp.float32)
                rest = value - high
                turned = pltpu.roll(jnp.where(low, rest, high), BS, 1)
                at = plane * plane_ids + e + 2 * pair
                ap[at] = jnp.where(low, high, turned).astype(jnp.bfloat16)
                ap[at + 1] = jnp.where(low, turned, rest).astype(jnp.bfloat16)
            return carry

        lax.fori_loop(0, plane_ids // 4, four, 0)

    def near_index(origin):
        return lambda r, e: plan_s[origin, r, e]

    def far_index(group):
        def index_of(r, e):
            n = group * rows + r
            return plan_s[n_grp + n // hs, n % hs, e]
        return index_of

    def part_copy(s, k):
        first, last = stages[s][1:]
        here = pl.ds(first * BS, (last - first) * BS)
        return pltpu.make_async_remote_copy(
            src_ref=partial.at[k, :, here], dst_ref=arrived.at[k - 1, :, here],
            send_sem=part_send.at[s, k - 1], recv_sem=part_recv.at[s, k - 1],
            device_id={"dom": partner(k)},
        )

    def slot_rows(s, owner_dom, slot, at):
        first, last = stages[s][1:]
        line = hs + owner[0, slot]
        for c in range(first, last, 2):
            right = jnp.concatenate([ap[plan_s[sort_at + owner_dom, line, c + h]] for h in range(2)], axis=1)
            product = jnp.dot(left[at], right, preferred_element_type=jnp.float32)
            both = product[:BS] + product[BS:]
            one, two = both[:, :LANES], both[:, LANES:]
            partial[at, :, c * BS:(c + 2) * BS] = jnp.where(low, one, two) + pltpu.roll(jnp.where(low, two, one), BS, 1)

    def exchange(s):
        first, last = stages[s][1:]
        here = slice(first * BS, last * BS)

        def far_slot(step, carry):
            k = n_dom - step
            target = partner(k)
            slot_rows(s, target, target * cap, k)

            @pl.when(step > 1)
            def _():
                part_copy(s, k + 1).start()

            return carry

        lax.fori_loop(1, n_dom, far_slot, 0)
        slot_rows(s, me, me * cap, 0)
        part_copy(s, 1).start()
        for t in range(1, cap):
            slot_rows(s, me, me * cap + t, n_dom + t - 1)
        for r in range(owned):
            total = partial[0, :, here] * (owner[0, me * cap] == r).astype(jnp.float32)
            for t in range(1, cap):
                total += partial[n_dom + t - 1, :, here] * (owner[0, me * cap + t] == r).astype(jnp.float32)
            summed[r, :, here] = total

    def collect(s):
        first, last = stages[s][1:]

        def one(step, carry):
            k = n_dom - step
            part_copy(s, k).wait_recv()
            row = dom_in[partner(k), row_at:row_at + 1, :]
            for c in range(first, last, 2):
                here = slice(c * BS, (c + 2) * BS)
                value = arrived[k - 1, :, here]
                for r in range(owned):
                    summed[r, :, here] += jnp.where(row == r, value, 0.0)
            return carry

        lax.fori_loop(1, n_dom, one, 0)

    def take_halo(k, carry):
        halo_copy(k).wait_recv()
        for h in range(hs):
            convert(near_count + partner(k) * hs + h, rows + partner(k) * hs + h)
        return carry

    def own_halo(h, carry):
        def write(a, value):
            stage[:, a, :] = value

        for t in range(tiles):
            duplicate(outgoing[me * hs + h, :, t * LANES:(t + 1) * LANES], write, 2 * t)
        for q in range(kp):
            keep((rows + me * hs + h) * kp + q, stage[q])
        return carry

    in_halves = plane_ids <= ka and rows % 4 == 0
    for step in range(n_grp - 1):
        origins = (g - 1 - step, g + 1 + step)
        exists = (origins[0] >= 0, origins[1] < n_grp)
        for r in range(rows):
            for direction in range(2):
                origin = origins[direction]

                @pl.when(exists[direction])
                def _():
                    line_copy(direction, step, r, table.at[origin * rows + r], origin).wait_recv()

                if step < n_grp - 2:
                    @pl.when(exists[direction] & can_send[direction])
                    def _():
                        line_copy(direction, step + 1, r, table.at[origin * rows + r], origin).start()

            if step > 0:
                for direction in range(2):
                    @pl.when(exists[direction])
                    def _():
                        convert(origins[direction] * rows + r, direction * rows + r)
                        if in_halves and r == rows // 2 - 1:
                            multiply(
                                origins[direction], [(origins[direction], near_index(origins[direction]))],
                                range(rows // 2), direction * plane_ids // 2, False,
                            )
        if step == 0:
            lax.fori_loop(0, hs, own_halo, 0)
            lax.fori_loop(1, n_dom, take_halo, 0)
            multiply(g, [(g, near_index(g))] + [(n_grp + n, far_index(n)) for n in range(far_groups)])
            for s in range(len(stages)):
                if stages[s][0] < 0:
                    exchange(s)
        for direction in range(2):
            @pl.when(exists[direction])
            def _():
                if step == 0:
                    def take(r, carry):
                        convert(origins[direction] * rows + r, direction * rows + r)
                        return carry

                    lax.fori_loop(0, rows, take, 0)
                parts = [(origins[direction], near_index(origins[direction]))]
                if step > 0 and in_halves:
                    multiply(origins[direction], parts, range(rows // 2, rows), direction * plane_ids // 2)
                else:
                    multiply(origins[direction], parts)
        for s in range(len(stages)):
            if stages[s][0] == step:
                exchange(s)

    for k in range(1, n_grp):
        late_copy(k).wait()
    anywhere = late_in[0]
    for k in range(1, n_grp):
        anywhere |= late_in[k]
    late[...] = jnp.max(jnp.max(anywhere, axis=0, keepdims=True), axis=1, keepdims=True)

    for s in range(len(stages)):
        collect(s)

    for r in range(owned):
        for c in range(0, kc, 2):
            value = summed[r, :, c * BS:(c + 2) * BS]
            turned = pltpu.roll(value, BS, 1)
            blocks[r, c] = jnp.where(low, value, turned)
            blocks[r, c + 1] = jnp.where(low, turned, value)

    def place_row(r, carry):
        for c in range(kc):
            blocks[owned, c] = blocks[r, plan_s[rank_at + me, hs + r, c]]
        for c in range(0, kc, SUB):
            for t in range(tiles):
                out[r, c:c + SUB, t * LANES:(t + 1) * LANES] = jnp.where(
                    low, blocks[owned, c:c + SUB, 2 * t, :], blocks[owned, c:c + SUB, 2 * t + 1, :]
                )
        return carry

    lax.fori_loop(0, owned, place_row, 0)

    def drain(k, carry):
        halo_copy(k).wait_send()
        for s in range(len(stages)):
            part_copy(s, k).wait_send()
        return carry

    lax.fori_loop(1, n_dom, drain, 0)
    for step in range(n_grp - 1):
        for r in range(rows):
            for direction in range(2):
                origin = g - step if direction == 0 else g + step
                exists = (origin >= 0) & (origin < n_grp)

                @pl.when(exists & can_send[direction])
                def _():
                    line_copy(direction, step, r, table.at[r], origin).wait_send()


def per_device(
    operator_blocks, operator_cols, halo_count, prolong_blocks, prolong_cols,
    prolong_slot, send_lists, slot_owner_row, coarse_pattern,
):
    n_grp = lax.axis_size("grp")
    n_dom = lax.axis_size("dom")
    rows, ka = operator_cols.shape
    kp = prolong_cols.shape[1]
    owned, kc = coarse_pattern.shape
    hs = send_lists.shape[1] // n_dom
    cap = slot_owner_row.shape[1] // n_dom
    total_ids = owned * n_grp * n_dom
    used = n_dom + cap - 1
    panel_count = n_grp * rows + n_dom * hs
    groups = panel_count // rows
    width = rows * BS
    plan_rows = n_grp + 3 * n_dom
    quarter, half = kc // 4, kc // 2
    at_once = ((n_grp - 2, 0, kc),)
    by_distance = ((n_grp - 4, 0, quarter), (n_grp - 3, quarter, half), (n_grp - 2, half, kc))
    assert n_grp >= 3 and quarter % 2 == 0
    assert n_dom & (n_dom - 1) == 0 and (n_dom * hs) % rows == 0 and n_dom * hs >= rows
    assert kp == SUB and ka % SUB == 0 and kc % SUB == 0 and LANES % kc == 0
    assert owned < rows and kc <= ka
    assert rows % 2 == 0 and rows <= SUB and hs + owned < SUB and (owned * n_dom) % 4 == 0
    vm = lambda dtype, *shape: pltpu.VMEM(shape, dtype)
    f32, bf16, i32 = jnp.float32, jnp.bfloat16, jnp.int32
    sem = lambda *shape: pltpu.SemaphoreType.DMA(shape)
    call = lambda stages, number, name: pl.pallas_call(
        functools.partial(fused_kernel, n_grp, n_dom, rows, hs, ka, kp, kc, cap, owned, stages),
        out_shape=(
            jax.ShapeDtypeStruct((owned, kc, BS * BS), f32), jax.ShapeDtypeStruct((1, 1), i32),
        ),
        in_specs=[smem_spec()] * 5 + [vmem_spec()] * 2 + [any_spec()] * 2,
        out_specs=(vmem_spec(), vmem_spec()),
        scratch_shapes=[
            vm(f32, rows, kp, BS * BS), vm(f32, rows, ka, BS * BS), vm(f32, panel_count, kp, BS * BS),
            vm(f32, n_dom * hs, kp, BS * BS),
            vm(i32, SUB, LANES), vm(i32, n_grp, SUB, LANES), vm(i32, SUB, LANES),
            vm(i32, n_dom, SUB, LANES), vm(i32, n_dom, SUB, LANES),
            vm(i32, plan_rows, SUB, LANES), pltpu.SMEM((plan_rows, SUB, LANES), i32),
            vm(f32, rows, ka, BS, LANES), vm(bf16, groups, width, 2 * width),
            vm(f32, rows * kp + 1, BS, LANES), vm(f32, kp, BS, LANES),
            vm(bf16, (rows + n_dom * hs) * kp + 1, 2 * BS, LANES), vm(bf16, used, 2 * BS, width),
            vm(bf16, total_ids, width, LANES),
            vm(f32, used, BS, kc * BS), vm(f32, n_dom - 1, BS, kc * BS), vm(f32, owned, BS, kc * BS),
            sem(2), sem(2, n_grp - 1, rows), sem(2, n_grp - 1, rows), sem(n_dom), sem(n_dom),
            sem(n_grp), sem(n_grp), sem(n_dom), sem(n_dom), sem(1),
            sem(len(stages), n_dom - 1), sem(len(stages), n_dom - 1),
            vm(i32, SUB, LANES), vm(i32, n_grp, SUB, LANES), sem(n_grp), sem(n_grp),
        ],
        compiler_params=pltpu.CompilerParams(
            collective_id=number, has_side_effects=True, vmem_limit_bytes=67043328
        ),
        name=name,
    )
    args = (
        operator_cols, halo_count, prolong_slot, send_lists, slot_owner_row, prolong_cols, coarse_pattern,
        prolong_blocks, operator_blocks,
    )
    result, late = call(by_distance, 0, "coarse_rows")(*args)
    result = lax.cond(late.reshape(()) > 0, lambda: call(at_once, 1, "coarse_rows_at_once")(*args)[0], lambda: result)
    return result


def solution(mesh):
    blocks = P(("grp", "dom"), None, None)
    lists = P(("grp", "dom"), None)
    return jax.shard_map(
        per_device,
        mesh=mesh,
        in_specs=(blocks, lists, P(("grp", "dom")), blocks, lists, lists, lists, lists, lists),
        out_specs=blocks,
        check_vma=False,
    )
```

```python
import functools

import jax
import jax.numpy as jnp
from jax import lax
from jax.experimental import pallas as pl
from jax.experimental.pallas import tpu as pltpu
from jax.sharding import PartitionSpec as P

BS = 64
KG = 12
LANES = 128
SUB = 8


def any_spec():
    return pl.BlockSpec(memory_space=pl.ANY)


def vmem_spec():
    return pl.BlockSpec(memory_space=pltpu.VMEM)


def smem_spec():
    return pl.BlockSpec(memory_space=pltpu.SMEM)


def fused_kernel(
    n_grp, n_dom, rows, hs, ka, kp, kc, cap, owned, stages, merge,
    cols, halo, slots, picked, owner, prolong_cols, pattern, prolong_in, operator_in,
    out, late,
    own_raw, operator, table, outgoing, grp_out, grp_in, dom_base, dom_out, dom_in, plan_v, plan_s,
    blocks, dense, own_dup, stage, panels, left, ap, partial, arrived, summed,
    load_sem, line_send, line_recv, halo_send, halo_recv,
    gmeta_send, gmeta_recv, dmeta_send, dmeta_recv, plan_sem, part_send, part_recv,
    late_out, late_in, late_send, late_recv,
    feed, merged, merged_in, source_row, feed_send, feed_recv, merged_send, merged_recv,
):
    g = lax.axis_index("grp")
    me = lax.axis_index("dom")
    near_count = n_grp * rows
    plane_ids = owned * n_dom
    halo_count_rows = n_dom * hs
    groups = n_grp + halo_count_rows // rows
    zero_at = (rows + halo_count_rows) * kp
    row_at = hs + owned
    sort_at = n_grp + n_dom
    rank_at = sort_at + n_dom
    width = rows * BS
    tiles = BS // 2
    low = lax.broadcasted_iota(jnp.int32, (1, LANES), 1) < BS
    lane = lax.broadcasted_iota(jnp.int32, (SUB, LANES), 1)
    sub = lax.broadcasted_iota(jnp.int32, (SUB, LANES), 0)

    barrier = pltpu.get_barrier_semaphore()
    for k in range(1, n_grp):
        pl.semaphore_signal(barrier, inc=1, device_id={"grp": lax.rem(g + k, n_grp)})
    for k in range(1, n_dom):
        pl.semaphore_signal(barrier, inc=1, device_id={"dom": lax.rem(me + k, n_dom)})
    own_load = pltpu.make_async_copy(prolong_in, own_raw, load_sem.at[0])
    operator_load = pltpu.make_async_copy(operator_in, operator, load_sem.at[1])
    own_load.start()
    operator_load.start()

    def partner(k):
        other = 0
        bit = 1
        while bit < n_dom:
            other += lax.rem(me // bit + k // bit, 2) * bit
            bit *= 2
        return other

    grp_out[...] = jnp.zeros(grp_out.shape, jnp.int32)
    grp_out[0:rows, 0:kp] = prolong_cols[...]
    dom_base[...] = jnp.zeros(dom_base.shape, jnp.int32)
    for r in range(owned):
        for j in range(0, LANES, kc):
            dom_base[hs + r:hs + r + 1, j:j + kc] = pattern[r:r + 1, :]

    if merge:
        line = jnp.zeros((1, LANES), jnp.int32)
        for t in range(n_dom * cap):
            line = jnp.where(lane[0:1] == t, owner[0, t], line)
        dom_base[row_at + 1:row_at + 2, :] = line

    def for_dom(d, carry):
        dom_out[d] = dom_base[...]
        for h in range(hs):
            dom_out[d, h:h + 1, 0:kp] = prolong_cols[pl.ds(picked[0, d * hs + h], 1), :]
        dom_out[d, row_at:row_at + 1, :] = jnp.full((1, LANES), owner[0, d * cap], jnp.int32)
        return carry

    lax.fori_loop(0, n_dom, for_dom, 0)
    grp_in[g] = grp_out[...]
    dom_in[me] = dom_out[me]
    pl.semaphore_wait(barrier, n_grp + n_dom - 2)

    def line_copy(direction, step, r, src, origin):
        return pltpu.make_async_remote_copy(
            src_ref=src, dst_ref=table.at[origin * rows + r],
            send_sem=line_send.at[direction, step, r], recv_sem=line_recv.at[direction, step, r],
            device_id={"grp": g + 1 if direction == 0 else g - 1},
        )

    merge_sources = ((2, 3, 1, 0), (4, 5, 1, 0))

    def grp_meta(k):
        return pltpu.make_async_remote_copy(
            src_ref=grp_out, dst_ref=grp_in.at[g], send_sem=gmeta_send.at[k], recv_sem=gmeta_recv.at[k],
            device_id={"grp": lax.rem(g + k, n_grp)},
        )

    def dom_meta(k):
        target = partner(k)
        return pltpu.make_async_remote_copy(
            src_ref=dom_out.at[target], dst_ref=dom_in.at[me], send_sem=dmeta_send.at[k], recv_sem=dmeta_recv.at[k],
            device_id={"dom": target},
        )

    def halo_copy(k):
        target = partner(k)
        return pltpu.make_async_remote_copy(
            src_ref=outgoing.at[pl.ds(target * hs, hs)], dst_ref=table.at[pl.ds(near_count + me * hs, hs)],
            send_sem=halo_send.at[k], recv_sem=halo_recv.at[k],
            device_id={"dom": target},
        )

    for k in range(1, n_grp):
        grp_meta(k).start()

    def start_dom_meta(k, carry):
        dom_meta(k).start()
        return carry

    lax.fori_loop(1, n_dom, start_dom_meta, 0)
    can_send = (g < n_grp - 1, g > 0)
    for r in range(rows):
        for direction in range(2):
            @pl.when(can_send[direction])
            def _():
                line_copy(direction, 0, r, prolong_in.at[r], g).start()

    own_load.wait()

    def pick(n, carry):
        outgoing[n] = own_raw[picked[0, n]]
        return carry

    lax.fori_loop(0, halo_count_rows, pick, 0)

    def duplicate(x, write, at):
        turned = pltpu.roll(x, BS, 1)
        write(at, jnp.where(low, x, turned))
        write(at + 1, jnp.where(low, turned, x))

    def own_row(i, carry):
        def write(a, value):
            own_dup[pl.ds(i * kp, kp), a, :] = value

        for t in range(tiles):
            duplicate(own_raw[i, :, t * LANES:(t + 1) * LANES], write, 2 * t)
        return carry

    lax.fori_loop(0, rows, own_row, 0)

    def start_halo(k, carry):
        halo_copy(k).start()
        return carry

    lax.fori_loop(1, n_dom, start_halo, 0)
    own_dup[rows * kp] = jnp.zeros((BS, LANES), jnp.float32)
    panels[zero_at] = jnp.zeros((2 * BS, LANES), jnp.bfloat16)

    def split(value):
        high = value.astype(jnp.bfloat16)
        return high, (value - high.astype(jnp.float32)).astype(jnp.bfloat16)

    def keep(at, value):
        high, rest = split(value)
        panels[at, 0:BS] = high
        panels[at, BS:2 * BS] = rest

    def convert(panel, place):
        def write(a, value):
            stage[:, a, :] = value

        for t in range(tiles):
            duplicate(table[panel, :, t * LANES:(t + 1) * LANES], write, 2 * t)
        for q in range(kp):
            keep(place * kp + q, stage[q])

    operator_load.wait()

    def relay(n, carry):
        i = n // (ka // SUB)
        m = lax.rem(n, ka // SUB) * SUB

        def write(a, value):
            blocks[i, pl.ds(m, SUB), a, :] = value

        for t in range(tiles):
            duplicate(operator[i, pl.ds(m, SUB), t * LANES:(t + 1) * LANES], write, 2 * t)
        return carry

    lax.fori_loop(0, rows * (ka // SUB), relay, 0)

    def densify(i, group, slots_used, column_of):
        for pair in range(0, rows, 2):
            first = group * rows + pair
            wanted = jnp.where(low, first, first + 1)
            total = jnp.zeros((BS, LANES), jnp.float32)
            for m in slots_used:
                total += jnp.where(wanted == column_of(i, m), blocks[i, m], 0.0)
            high, rest = split(total)
            here = pl.ds(i * BS, BS)
            dense[group, here, pair * BS:(pair + 2) * BS] = high
            dense[group, here, width + pair * BS:width + (pair + 2) * BS] = rest

    def near_dense(n, carry):
        densify(n // n_grp, lax.rem(n, n_grp), range(KG), lambda i, m: cols[i, m])
        return carry

    def far_column(i, m):
        return jnp.where(m - KG < halo[i], near_count + cols[i, m], -1)

    far_groups = groups - n_grp

    def far_dense(n, carry):
        densify(n // far_groups, n_grp + lax.rem(n, far_groups), range(KG, ka), far_column)
        return carry

    lax.fori_loop(0, rows * n_grp, near_dense, 0)
    lax.fori_loop(0, rows * far_groups, far_dense, 0)

    for k in range(1, n_grp):
        grp_meta(k).wait()

    def wait_dom_meta(k, carry):
        dom_meta(k).wait()
        return carry

    lax.fori_loop(1, n_dom, wait_dom_meta, 0)

    def places(values, first_id, first_place):
        found = jnp.full((SUB, LANES), zero_at, jnp.int32)
        for q in range(kp):
            found = jnp.where(values[:, q:q + 1] == first_id + lane, (first_place + sub) * kp + q, found)
        return found

    for origin in range(n_grp):
        side = (origin > g).astype(jnp.int32)
        plan_v[origin] = places(grp_in[origin], origin * plane_ids, side * rows)

    slot_of_lane = lax.rem(lane, kc)

    pattern_line = (sub >= hs) & (sub < hs + owned)

    def dom_tables(d, wrong):
        values = dom_in[d]
        plan_v[n_grp + d] = places(values, g * plane_ids, rows + d * hs)
        plane = jnp.zeros((SUB, LANES), jnp.int32)
        for n in range(1, n_grp):
            plane += (values >= n * plane_ids).astype(jnp.int32)
        distance = jnp.abs(plane - g)
        order = distance * kc + slot_of_lane
        rank = jnp.zeros((SUB, LANES), jnp.int32)
        for s in range(1, kc):
            rank += (pltpu.roll(order, s, 1) < order).astype(jnp.int32)
        ordered = values
        for s in range(kc):
            ordered = jnp.where(pltpu.roll(rank, s, 1) == slot_of_lane, pltpu.roll(values, s, 1), ordered)
        plan_v[sort_at + d] = ordered
        plan_v[rank_at + d] = rank
        for after, _, last in stages:
            wrong |= (pattern_line & (rank < last) & (distance > after + 1)).astype(jnp.int32)
        return wrong

    if merge:
        for way in range(2):
            goal = partner(4 if way == 0 else 2) * cap
            for n, source in enumerate(merge_sources[way]):
                found = jnp.where(lane[0:1] == goal, dom_in[partner(source), row_at + 1:row_at + 2, :], 0)
                splat = jnp.broadcast_to(jnp.sum(found, axis=1, keepdims=True), (1, LANES))
                source_row[4 * way + n:4 * way + n + 1, :] = splat

    wrong = lax.fori_loop(0, n_dom, dom_tables, jnp.zeros((SUB, LANES), jnp.int32))
    plan_copy = pltpu.make_async_copy(plan_v, plan_s, plan_sem.at[0])
    plan_copy.start()
    late_out[...] = wrong
    late_in[g] = wrong

    def late_copy(k):
        return pltpu.make_async_remote_copy(
            src_ref=late_out, dst_ref=late_in.at[g], send_sem=late_send.at[k], recv_sem=late_recv.at[k],
            device_id={"grp": lax.rem(g + k, n_grp)},
        )


    def transposed(slot, at):
        for pair in range(0, rows, 2):
            both = []
            for i in range(pair, pair + 2):
                place = jnp.int32(rows * kp)
                for j in range(kp):
                    place = jnp.where(slots[i, j] == slot, i * kp + j, place)
                both.append(own_dup[place])
            turned = jnp.concatenate(both, axis=0).T
            high = turned.astype(jnp.bfloat16).astype(jnp.float32)
            upper = lax.broadcasted_iota(jnp.int32, (LANES, LANES), 0) < BS
            left[at, :, pair * BS:(pair + 2) * BS] = jnp.where(upper, high, turned - high).astype(jnp.bfloat16)

    def far_left(k, carry):
        transposed(partner(k) * cap, k)
        return carry

    lax.fori_loop(1, n_dom, far_left, 0)
    for k in range(1, n_grp):
        late_copy(k).start()
    for t in range(cap):
        transposed(me * cap + t, 0 if t == 0 else n_dom + t - 1)

    def own_panels(n, carry):
        keep(n, own_dup[n])
        return carry

    lax.fori_loop(0, rows * kp, own_panels, 0)
    plan_copy.wait()

    def multiply(plane, parts, used_rows=range(rows), saved=None, last=True):
        def four(n, carry):
            e = n * 4
            total = None
            for group, index_of in parts:
                halves = []
                for pair in range(2):
                    blocks_here = [
                        jnp.where(low, panels[index_of(r, e + 2 * pair)], panels[index_of(r, e + 2 * pair + 1)])
                        for r in used_rows
                    ]
                    high = [b[0:BS] for b in blocks_here]
                    rest = [b[BS:2 * BS] for b in blocks_here]
                    halves.append(jnp.concatenate(high + rest + high, axis=0))
                right = jnp.concatenate(halves, axis=1)
                first, depth = used_rows[0] * BS, len(used_rows) * BS
                lhs_high = dense[group, :, first:first + depth]
                lhs = jnp.concatenate([lhs_high, lhs_high, dense[group, :, width + first:width + first + depth]], axis=1)
                product = jnp.dot(lhs, right, preferred_element_type=jnp.float32)
                total = product if total is None else total + product
            for pair in range(2):
                value = total[:, pair * LANES:(pair + 1) * LANES]
                if not last:
                    for i in range(rows):
                        blocks[i, saved + 2 * n + pair] = value[i * BS:(i + 1) * BS]
                    continue
                if saved is not None:
                    value += jnp.concatenate([blocks[i, saved + 2 * n + pair] for i in range(rows)], axis=0)
                high = value.astype(jnp.bfloat16).astype(jnp.float32)
                rest = value - high
                turned = pltpu.roll(jnp.where(low, rest, high), BS, 1)
                at = plane * plane_ids + e + 2 * pair
                ap[at] = jnp.where(low, high, turned).astype(jnp.bfloat16)
                ap[at + 1] = jnp.where(low, turned, rest).astype(jnp.bfloat16)
            return carry

        lax.fori_loop(0, plane_ids // 4, four, 0)

    def near_index(origin):
        return lambda r, e: plan_s[origin, r, e]

    def far_index(group):
        def index_of(r, e):
            n = group * rows + r
            return plan_s[n_grp + n // hs, n % hs, e]
        return index_of

    def part_copy(s, k, window=None):
        first, last = stages[s][1:] if window is None else window
        here = pl.ds(first * BS, (last - first) * BS)
        return pltpu.make_async_remote_copy(
            src_ref=partial.at[k, :, here], dst_ref=arrived.at[k - 1, :, here],
            send_sem=part_send.at[s, k - 1], recv_sem=part_recv.at[s, k - 1],
            device_id={"dom": partner(k)},
        )

    def slot_rows(s, owner_dom, slot, at):
        first, last = stages[s][1:]
        line = hs + owner[0, slot]
        for c in range(first, last, 2):
            right = jnp.concatenate([ap[plan_s[sort_at + owner_dom, line, c + h]] for h in range(2)], axis=1)
            product = jnp.dot(left[at], right, preferred_element_type=jnp.float32)
            both = product[:BS] + product[BS:]
            one, two = both[:, :LANES], both[:, LANES:]
            partial[at, :, c * BS:(c + 2) * BS] = jnp.where(low, one, two) + pltpu.roll(jnp.where(low, two, one), BS, 1)

    def exchange(s):
        if merge and s == len(stages) - 1:
            exchange_merged()
            return

        def far_slot(step, carry):
            k = n_dom - step
            target = partner(k)
            slot_rows(s, target, target * cap, k)

            @pl.when(step > 1)
            def _():
                part_copy(s, k + 1).start()

            return carry

        lax.fori_loop(1, n_dom, far_slot, 0)
        own_slots(s, lambda: part_copy(s, 1).start())

    def own_slots(s, then=None):
        first, last = stages[s][1:]
        here = slice(first * BS, last * BS)
        slot_rows(s, me, me * cap, 0)
        if then is not None:
            then()
        for t in range(1, cap):
            slot_rows(s, me, me * cap + t, n_dom + t - 1)
        for r in range(owned):
            total = partial[0, :, here] * (owner[0, me * cap] == r).astype(jnp.float32)
            for t in range(1, cap):
                total += partial[n_dom + t - 1, :, here] * (owner[0, me * cap + t] == r).astype(jnp.float32)
            summed[r, :, here] = total

    def collect(s):
        if merge and s == len(stages) - 1:
            collect_merged()
            return
        first, last = stages[s][1:]

        def one(step, carry):
            k = n_dom - step
            part_copy(s, k).wait_recv()
            row = dom_in[partner(k), row_at:row_at + 1, :]
            for c in range(first, last, 2):
                here = slice(c * BS, (c + 2) * BS)
                value = arrived[k - 1, :, here]
                for r in range(owned):
                    summed[r, :, here] += jnp.where(row == r, value, 0.0)
            return carry

        lax.fori_loop(1, n_dom, one, 0)

    def way_window(way):
        first, last = stages[-1][1:]
        middle = (first + last) // 2
        return (first, middle) if way == 0 else (middle, last)

    def feed_copy(k, way, to, place):
        first, last = way_window(way)
        return pltpu.make_async_remote_copy(
            src_ref=partial.at[k, :, pl.ds(first * BS, (last - first) * BS)], dst_ref=feed.at[way, place],
            send_sem=feed_send.at[way, place], recv_sem=feed_recv.at[way, place],
            device_id={"dom": partner(to)},
        )

    def merged_copy(way):
        return pltpu.make_async_remote_copy(
            src_ref=merged.at[way], dst_ref=merged_in.at[way], send_sem=merged_send.at[way], recv_sem=merged_recv.at[way],
            device_id={"dom": partner(4 if way == 0 else 2)},
        )

    def feeds_of(k):
        if k > 5:
            return [feed_copy(k, 0, k - 4, k - 6), feed_copy(k, 1, k - 2, k - 6)]
        if k == 5:
            return [feed_copy(k, 0, 1, 2)]
        return [feed_copy(k, 1, 1, 2)] if k == 3 else []

    def direct_of(k):
        s = len(stages) - 1
        if k == 1:
            return [part_copy(s, k)]
        return [part_copy(s, k, way_window(0 if k < 4 else 1))] if k < 6 else []

    def exchange_merged():
        s = len(stages) - 1
        before = None
        for k in (7, 6, 5, 3, 4, 2, 1):
            slot_rows(s, partner(k), partner(k) * cap, k)
            if before is not None:
                for copy in feeds_of(before) + direct_of(before):
                    copy.start()
            before = k
        own_slots(s)
        for copy in feeds_of(before) + direct_of(before):
            copy.start()
        for way in range(2):
            window = way_window(way)
            for k in (7, 6, 5 if way == 0 else 3):
                feeds_of(k)[way if k > 5 else 0].wait_recv()
            for c in range(window[0], window[1], 2):
                here = slice((c - window[0]) * BS, (c - window[0] + 2) * BS)
                values = [feed[way, n, :, here] for n in range(3)]
                values.append(partial[4 if way == 0 else 2, :, c * BS:(c + 2) * BS])
                for r in range(owned):
                    total = None
                    for n in range(4):
                        term = jnp.where(source_row[4 * way + n:4 * way + n + 1, :] == r, values[n], 0.0)
                        total = term if total is None else total + term
                    merged[way, r, :, here] = total
        for way in range(2):
            merged_copy(way).start()

    def add_rows(row, values_of, window):
        for c in range(window[0], window[1], 2):
            here = slice(c * BS, (c + 2) * BS)
            value = values_of(here)
            for r in range(owned):
                summed[r, :, here] += jnp.where(row == r, value, 0.0)

    def collect_merged():
        first, last = stages[-1][1:]
        for k in (1, 3, 2, 5, 4):
            direct_of(k)[0].wait_recv()
            window = (first, last) if k == 1 else way_window(0 if k < 4 else 1)
            add_rows(dom_in[partner(k), row_at:row_at + 1, :], lambda here: arrived[k - 1, :, here], window)
        for way in range(2):
            merged_copy(way).wait_recv()
            first, last = way_window(way)
            for r in range(owned):
                summed[r, :, first * BS:last * BS] += merged_in[way, r]

    def take_halo(k, carry):
        halo_copy(k).wait_recv()
        for h in range(hs):
            convert(near_count + partner(k) * hs + h, rows + partner(k) * hs + h)
        return carry

    def own_halo(h, carry):
        def write(a, value):
            stage[:, a, :] = value

        for t in range(tiles):
            duplicate(outgoing[me * hs + h, :, t * LANES:(t + 1) * LANES], write, 2 * t)
        for q in range(kp):
            keep((rows + me * hs + h) * kp + q, stage[q])
        return carry

    in_halves = plane_ids <= ka and rows % 4 == 0
    for step in range(n_grp - 1):
        origins = (g - 1 - step, g + 1 + step)
        exists = (origins[0] >= 0, origins[1] < n_grp)
        for r in range(rows):
            for direction in range(2):
                origin = origins[direction]

                @pl.when(exists[direction])
                def _():
                    line_copy(direction, step, r, table.at[origin * rows + r], origin).wait_recv()

                if step < n_grp - 2:
                    @pl.when(exists[direction] & can_send[direction])
                    def _():
                        line_copy(direction, step + 1, r, table.at[origin * rows + r], origin).start()

            if step > 0:
                for direction in range(2):
                    @pl.when(exists[direction])
                    def _():
                        convert(origins[direction] * rows + r, direction * rows + r)
                        if in_halves and r == rows // 2 - 1:
                            multiply(
                                origins[direction], [(origins[direction], near_index(origins[direction]))],
                                range(rows // 2), direction * plane_ids // 2, False,
                            )
        if step == 0:
            lax.fori_loop(0, hs, own_halo, 0)
            lax.fori_loop(1, n_dom, take_halo, 0)
            multiply(g, [(g, near_index(g))] + [(n_grp + n, far_index(n)) for n in range(far_groups)])
            for s in range(len(stages)):
                if stages[s][0] < 0:
                    exchange(s)
        for direction in range(2):
            @pl.when(exists[direction])
            def _():
                if step == 0:
                    def take(r, carry):
                        convert(origins[direction] * rows + r, direction * rows + r)
                        return carry

                    lax.fori_loop(0, rows, take, 0)
                parts = [(origins[direction], near_index(origins[direction]))]
                if step > 0 and in_halves:
                    multiply(origins[direction], parts, range(rows // 2, rows), direction * plane_ids // 2)
                else:
                    multiply(origins[direction], parts)
        for s in range(len(stages)):
            if stages[s][0] == step:
                exchange(s)

    for k in range(1, n_grp):
        late_copy(k).wait()
    anywhere = late_in[0]
    for k in range(1, n_grp):
        anywhere |= late_in[k]
    late[...] = jnp.max(jnp.max(anywhere, axis=0, keepdims=True), axis=1, keepdims=True)

    for s in range(len(stages)):
        collect(s)

    for r in range(owned):
        for c in range(0, kc, 2):
            value = summed[r, :, c * BS:(c + 2) * BS]
            turned = pltpu.roll(value, BS, 1)
            blocks[r, c] = jnp.where(low, value, turned)
            blocks[r, c + 1] = jnp.where(low, turned, value)

    def place_row(r, carry):
        for c in range(kc):
            blocks[owned, c] = blocks[r, plan_s[rank_at + me, hs + r, c]]
        for c in range(0, kc, SUB):
            for t in range(tiles):
                out[r, c:c + SUB, t * LANES:(t + 1) * LANES] = jnp.where(
                    low, blocks[owned, c:c + SUB, 2 * t, :], blocks[owned, c:c + SUB, 2 * t + 1, :]
                )
        return carry

    lax.fori_loop(0, owned, place_row, 0)

    def drain(k, carry):
        halo_copy(k).wait_send()
        for s in range(len(stages) - int(merge)):
            part_copy(s, k).wait_send()
        return carry

    lax.fori_loop(1, n_dom, drain, 0)
    if merge:
        for k in range(1, n_dom):
            for copy in feeds_of(k) + direct_of(k):
                copy.wait_send()
        for way in range(2):
            merged_copy(way).wait_send()
    for step in range(n_grp - 1):
        for r in range(rows):
            for direction in range(2):
                origin = g - step if direction == 0 else g + step
                exists = (origin >= 0) & (origin < n_grp)

                @pl.when(exists & can_send[direction])
                def _():
                    line_copy(direction, step, r, table.at[r], origin).wait_send()


def per_device(
    operator_blocks, operator_cols, halo_count, prolong_blocks, prolong_cols,
    prolong_slot, send_lists, slot_owner_row, coarse_pattern,
):
    n_grp = lax.axis_size("grp")
    n_dom = lax.axis_size("dom")
    rows, ka = operator_cols.shape
    kp = prolong_cols.shape[1]
    owned, kc = coarse_pattern.shape
    hs = send_lists.shape[1] // n_dom
    cap = slot_owner_row.shape[1] // n_dom
    total_ids = owned * n_grp * n_dom
    used = n_dom + cap - 1
    panel_count = n_grp * rows + n_dom * hs
    groups = panel_count // rows
    width = rows * BS
    plan_rows = n_grp + 3 * n_dom
    quarter, half = kc // 4, kc // 2
    at_once = ((n_grp - 2, 0, kc),)
    by_distance = ((n_grp - 4, 0, quarter), (n_grp - 3, quarter, half), (n_grp - 2, half, kc))
    assert n_grp >= 3 and quarter % 2 == 0
    part = quarter * BS
    through_chip = n_dom == 8 and hs + owned + 2 <= SUB and n_dom * cap <= LANES
    assert n_dom & (n_dom - 1) == 0 and (n_dom * hs) % rows == 0 and n_dom * hs >= rows
    assert kp == SUB and ka % SUB == 0 and kc % SUB == 0 and LANES % kc == 0
    assert owned < rows and kc <= ka
    assert rows % 2 == 0 and rows <= SUB and hs + owned < SUB and (owned * n_dom) % 4 == 0
    vm = lambda dtype, *shape: pltpu.VMEM(shape, dtype)
    f32, bf16, i32 = jnp.float32, jnp.bfloat16, jnp.int32
    sem = lambda *shape: pltpu.SemaphoreType.DMA(shape)
    call = lambda stages, merge, number, name: pl.pallas_call(
        functools.partial(fused_kernel, n_grp, n_dom, rows, hs, ka, kp, kc, cap, owned, stages, merge),
        out_shape=(
            jax.ShapeDtypeStruct((owned, kc, BS * BS), f32), jax.ShapeDtypeStruct((1, 1), i32),
        ),
        in_specs=[smem_spec()] * 5 + [vmem_spec()] * 2 + [any_spec()] * 2,
        out_specs=(vmem_spec(), vmem_spec()),
        scratch_shapes=[
            vm(f32, rows, kp, BS * BS), vm(f32, rows, ka, BS * BS), vm(f32, panel_count, kp, BS * BS),
            vm(f32, n_dom * hs, kp, BS * BS),
            vm(i32, SUB, LANES), vm(i32, n_grp, SUB, LANES), vm(i32, SUB, LANES),
            vm(i32, n_dom, SUB, LANES), vm(i32, n_dom, SUB, LANES),
            vm(i32, plan_rows, SUB, LANES), pltpu.SMEM((plan_rows, SUB, LANES), i32),
            vm(f32, rows, ka, BS, LANES), vm(bf16, groups, width, 2 * width),
            vm(f32, rows * kp + 1, BS, LANES), vm(f32, kp, BS, LANES),
            vm(bf16, (rows + n_dom * hs) * kp + 1, 2 * BS, LANES), vm(bf16, used, 2 * BS, width),
            vm(bf16, total_ids, width, LANES),
            vm(f32, used, BS, kc * BS), vm(f32, n_dom - 1, BS, kc * BS), vm(f32, owned, BS, kc * BS),
            sem(2), sem(2, n_grp - 1, rows), sem(2, n_grp - 1, rows), sem(n_dom), sem(n_dom),
            sem(n_grp), sem(n_grp), sem(n_dom), sem(n_dom), sem(1),
            sem(len(stages), n_dom - 1), sem(len(stages), n_dom - 1),
            vm(i32, SUB, LANES), vm(i32, n_grp, SUB, LANES), sem(n_grp), sem(n_grp),
            vm(f32, 2, 3, BS, part if merge else LANES), vm(f32, 2, owned, BS, part if merge else LANES),
            vm(f32, 2, owned, BS, part if merge else LANES), vm(i32, SUB, LANES), sem(2, 3), sem(2, 3), sem(2), sem(2),
        ],
        compiler_params=pltpu.CompilerParams(
            collective_id=number, has_side_effects=True, vmem_limit_bytes=67043328
        ),
        name=name,
    )
    args = (
        operator_cols, halo_count, prolong_slot, send_lists, slot_owner_row, prolong_cols, coarse_pattern,
        prolong_blocks, operator_blocks,
    )
    result, late = call(by_distance, through_chip, 0, "coarse_rows")(*args)
    result = lax.cond(late.reshape(()) > 0, lambda: call(at_once, False, 1, "coarse_rows_at_once")(*args)[0], lambda: result)
    return result


def solution(mesh):
    blocks = P(("grp", "dom"), None, None)
    lists = P(("grp", "dom"), None)
    return jax.shard_map(
        per_device,
        mesh=mesh,
        in_specs=(blocks, lists, P(("grp", "dom")), blocks, lists, lists, lists, lists, lists),
        out_specs=blocks,
        check_vma=False,
    )
```

```python
import functools
import math

import jax
import jax.numpy as jnp
from jax import lax
from jax.experimental import pallas as pl
from jax.experimental.pallas import tpu as pltpu
from jax.sharding import PartitionSpec as P

BS = 64
KG = 12
LANES = 128
SUB = 8
MOST_VMEM = 67043328
SPARE = 6 << 20


def any_spec():
    return pl.BlockSpec(memory_space=pl.ANY)


def vmem_spec():
    return pl.BlockSpec(memory_space=pltpu.VMEM)


def smem_spec():
    return pl.BlockSpec(memory_space=pltpu.SMEM)


def fused_kernel(
    n_grp, n_dom, rows, hs, ka, kp, kc, cap, owned, stages, merge,
    cols, halo, slots, picked, owner, prolong_cols, pattern, prolong_in, operator_in,
    out, late,
    own_raw, operator, table, outgoing, grp_out, grp_in, dom_base, dom_out, dom_in, plan_v, plan_s,
    blocks, dense, own_dup, stage, panels, left, ap, partial, arrived, summed,
    load_sem, line_send, line_recv, halo_send, halo_recv,
    gmeta_send, gmeta_recv, dmeta_send, dmeta_recv, plan_sem, part_send, part_recv,
    late_out, late_in, late_send, late_recv,
    feed, merged, merged_in, source_row, feed_send, feed_recv, merged_send, merged_recv,
):
    g = lax.axis_index("grp")
    me = lax.axis_index("dom")
    near_count = n_grp * rows
    plane_ids = owned * n_dom
    halo_count_rows = n_dom * hs
    groups = n_grp + halo_count_rows // rows
    zero_at = (rows + halo_count_rows) * kp
    row_at = hs + owned
    sort_at = n_grp + n_dom
    rank_at = sort_at + n_dom
    width = rows * BS
    tiles = BS // 2
    low = lax.broadcasted_iota(jnp.int32, (1, LANES), 1) < BS
    lane = lax.broadcasted_iota(jnp.int32, (SUB, LANES), 1)
    sub = lax.broadcasted_iota(jnp.int32, (SUB, LANES), 0)

    barrier = pltpu.get_barrier_semaphore()
    for k in range(1, n_grp):
        pl.semaphore_signal(barrier, inc=1, device_id={"grp": lax.rem(g + k, n_grp)})
    for k in range(1, n_dom):
        pl.semaphore_signal(barrier, inc=1, device_id={"dom": lax.rem(me + k, n_dom)})
    own_load = pltpu.make_async_copy(prolong_in, own_raw, load_sem.at[0])
    operator_load = pltpu.make_async_copy(operator_in, operator, load_sem.at[1])
    own_load.start()
    operator_load.start()

    def partner(k):
        other = 0
        bit = 1
        while bit < n_dom:
            other += lax.rem(me // bit + k // bit, 2) * bit
            bit *= 2
        return other

    grp_out[...] = jnp.zeros(grp_out.shape, jnp.int32)
    grp_out[0:rows, 0:kp] = prolong_cols[...]
    dom_base[...] = jnp.zeros(dom_base.shape, jnp.int32)
    for r in range(owned):
        for j in range(0, LANES, kc):
            dom_base[hs + r:hs + r + 1, j:j + kc] = pattern[r:r + 1, :]

    if merge:
        line = jnp.zeros((1, LANES), jnp.int32)
        for t in range(n_dom * cap):
            line = jnp.where(lane[0:1] == t, owner[0, t], line)
        dom_base[row_at + 1:row_at + 2, :] = line

    def for_dom(d, carry):
        dom_out[d] = dom_base[...]
        for h in range(hs):
            dom_out[d, h:h + 1, 0:kp] = prolong_cols[pl.ds(picked[0, d * hs + h], 1), :]
        dom_out[d, row_at:row_at + 1, :] = jnp.full((1, LANES), owner[0, d * cap], jnp.int32)
        return carry

    lax.fori_loop(0, n_dom, for_dom, 0)
    grp_in[g] = grp_out[...]
    dom_in[me] = dom_out[me]
    pl.semaphore_wait(barrier, n_grp + n_dom - 2)

    def line_copy(direction, step, r, src, origin):
        return pltpu.make_async_remote_copy(
            src_ref=src, dst_ref=table.at[origin * rows + r],
            send_sem=line_send.at[direction, step, r], recv_sem=line_recv.at[direction, step, r],
            device_id={"grp": g + 1 if direction == 0 else g - 1},
        )

    merge_sources = ((2, 3, 1, 0), (4, 5, 1, 0))

    def grp_meta(k):
        return pltpu.make_async_remote_copy(
            src_ref=grp_out, dst_ref=grp_in.at[g], send_sem=gmeta_send.at[k], recv_sem=gmeta_recv.at[k],
            device_id={"grp": lax.rem(g + k, n_grp)},
        )

    def dom_meta(k):
        target = partner(k)
        return pltpu.make_async_remote_copy(
            src_ref=dom_out.at[target], dst_ref=dom_in.at[me], send_sem=dmeta_send.at[k], recv_sem=dmeta_recv.at[k],
            device_id={"dom": target},
        )

    def halo_copy(k):
        target = partner(k)
        return pltpu.make_async_remote_copy(
            src_ref=outgoing.at[pl.ds(target * hs, hs)], dst_ref=table.at[pl.ds(near_count + me * hs, hs)],
            send_sem=halo_send.at[k], recv_sem=halo_recv.at[k],
            device_id={"dom": target},
        )

    for k in range(1, n_grp):
        grp_meta(k).start()

    def start_dom_meta(k, carry):
        dom_meta(k).start()
        return carry

    lax.fori_loop(1, n_dom, start_dom_meta, 0)
    can_send = (g < n_grp - 1, g > 0)
    for r in range(rows):
        for direction in range(2):
            @pl.when(can_send[direction])
            def _():
                line_copy(direction, 0, r, prolong_in.at[r], g).start()

    own_load.wait()

    def pick(n, carry):
        outgoing[n] = own_raw[picked[0, n]]
        return carry

    lax.fori_loop(0, halo_count_rows, pick, 0)

    def duplicate(x, write, at):
        turned = pltpu.roll(x, BS, 1)
        write(at, jnp.where(low, x, turned))
        write(at + 1, jnp.where(low, turned, x))

    def own_row(i, carry):
        def write(a, value):
            own_dup[pl.ds(i * kp, kp), a, :] = value

        for t in range(tiles):
            duplicate(own_raw[i, :, t * LANES:(t + 1) * LANES], write, 2 * t)
        return carry

    lax.fori_loop(0, rows, own_row, 0)

    def start_halo(k, carry):
        halo_copy(k).start()
        return carry

    lax.fori_loop(1, n_dom, start_halo, 0)
    own_dup[rows * kp] = jnp.zeros((BS, LANES), jnp.float32)
    panels[zero_at] = jnp.zeros((2 * BS, LANES), jnp.bfloat16)

    def split(value):
        high = value.astype(jnp.bfloat16)
        return high, (value - high.astype(jnp.float32)).astype(jnp.bfloat16)

    def keep(at, value):
        high, rest = split(value)
        panels[at, 0:BS] = high
        panels[at, BS:2 * BS] = rest

    def convert(panel, place):
        def write(a, value):
            stage[:, a, :] = value

        for t in range(tiles):
            duplicate(table[panel, :, t * LANES:(t + 1) * LANES], write, 2 * t)
        for q in range(kp):
            keep(place * kp + q, stage[q])

    operator_load.wait()

    def relay(n, carry):
        i = n // (ka // SUB)
        m = lax.rem(n, ka // SUB) * SUB

        def write(a, value):
            blocks[i, pl.ds(m, SUB), a, :] = value

        for t in range(tiles):
            duplicate(operator[i, pl.ds(m, SUB), t * LANES:(t + 1) * LANES], write, 2 * t)
        return carry

    lax.fori_loop(0, rows * (ka // SUB), relay, 0)

    def densify(i, group, slots_used, column_of):
        for pair in range(0, rows, 2):
            first = group * rows + pair
            wanted = jnp.where(low, first, first + 1)
            total = jnp.zeros((BS, LANES), jnp.float32)
            for m in slots_used:
                total += jnp.where(wanted == column_of(i, m), blocks[i, m], 0.0)
            high, rest = split(total)
            here = pl.ds(i * BS, BS)
            dense[group, here, pair * BS:(pair + 2) * BS] = high
            dense[group, here, width + pair * BS:width + (pair + 2) * BS] = rest

    def near_dense(n, carry):
        densify(n // n_grp, lax.rem(n, n_grp), range(KG), lambda i, m: cols[i, m])
        return carry

    def far_column(i, m):
        return jnp.where(m - KG < halo[i], near_count + cols[i, m], -1)

    far_groups = groups - n_grp

    def far_dense(n, carry):
        densify(n // far_groups, n_grp + lax.rem(n, far_groups), range(KG, ka), far_column)
        return carry

    lax.fori_loop(0, rows * n_grp, near_dense, 0)
    lax.fori_loop(0, rows * far_groups, far_dense, 0)

    for k in range(1, n_grp):
        grp_meta(k).wait()

    def wait_dom_meta(k, carry):
        dom_meta(k).wait()
        return carry

    lax.fori_loop(1, n_dom, wait_dom_meta, 0)

    def places(values, first_id, first_place):
        found = jnp.full((SUB, LANES), zero_at, jnp.int32)
        for q in range(kp):
            found = jnp.where(values[:, q:q + 1] == first_id + lane, (first_place + sub) * kp + q, found)
        return found

    for origin in range(n_grp):
        side = (origin > g).astype(jnp.int32)
        plan_v[origin] = places(grp_in[origin], origin * plane_ids, side * rows)

    slot_of_lane = lax.rem(lane, kc)

    pattern_line = (sub >= hs) & (sub < hs + owned)

    def dom_tables(d, wrong):
        values = dom_in[d]
        plan_v[n_grp + d] = places(values, g * plane_ids, rows + d * hs)
        plane = jnp.zeros((SUB, LANES), jnp.int32)
        for n in range(1, n_grp):
            plane += (values >= n * plane_ids).astype(jnp.int32)
        distance = jnp.abs(plane - g)
        order = distance * kc + slot_of_lane
        rank = jnp.zeros((SUB, LANES), jnp.int32)
        for s in range(1, kc):
            rank += (pltpu.roll(order, s, 1) < order).astype(jnp.int32)
        ordered = values
        for s in range(kc):
            ordered = jnp.where(pltpu.roll(rank, s, 1) == slot_of_lane, pltpu.roll(values, s, 1), ordered)
        plan_v[sort_at + d] = ordered
        plan_v[rank_at + d] = rank
        for after, _, last in stages:
            wrong |= (pattern_line & (rank < last) & (distance > after + 1)).astype(jnp.int32)
        return wrong

    if merge:
        for way in range(2):
            goal = partner(4 if way == 0 else 2) * cap
            for n, source in enumerate(merge_sources[way]):
                found = jnp.where(lane[0:1] == goal, dom_in[partner(source), row_at + 1:row_at + 2, :], 0)
                splat = jnp.broadcast_to(jnp.sum(found, axis=1, keepdims=True), (1, LANES))
                source_row[4 * way + n:4 * way + n + 1, :] = splat

    wrong = lax.fori_loop(0, n_dom, dom_tables, jnp.zeros((SUB, LANES), jnp.int32))
    plan_copy = pltpu.make_async_copy(plan_v, plan_s, plan_sem.at[0])
    plan_copy.start()
    late_out[...] = wrong
    late_in[g] = wrong

    def late_copy(k):
        return pltpu.make_async_remote_copy(
            src_ref=late_out, dst_ref=late_in.at[g], send_sem=late_send.at[k], recv_sem=late_recv.at[k],
            device_id={"grp": lax.rem(g + k, n_grp)},
        )


    def transposed(slot, at):
        for pair in range(0, rows, 2):
            both = []
            for i in range(pair, pair + 2):
                place = jnp.int32(rows * kp)
                for j in range(kp):
                    place = jnp.where(slots[i, j] == slot, i * kp + j, place)
                both.append(own_dup[place])
            turned = jnp.concatenate(both, axis=0).T
            high = turned.astype(jnp.bfloat16).astype(jnp.float32)
            upper = lax.broadcasted_iota(jnp.int32, (LANES, LANES), 0) < BS
            left[at, :, pair * BS:(pair + 2) * BS] = jnp.where(upper, high, turned - high).astype(jnp.bfloat16)

    def far_left(k, carry):
        transposed(partner(k) * cap, k)
        return carry

    lax.fori_loop(1, n_dom, far_left, 0)
    for k in range(1, n_grp):
        late_copy(k).start()
    for t in range(cap):
        transposed(me * cap + t, 0 if t == 0 else n_dom + t - 1)

    def own_panels(n, carry):
        keep(n, own_dup[n])
        return carry

    lax.fori_loop(0, rows * kp, own_panels, 0)
    plan_copy.wait()

    def multiply(plane, parts, used_rows=range(rows), saved=None, last=True):
        def four(n, carry):
            e = n * 4
            total = None
            for group, index_of in parts:
                halves = []
                for pair in range(2):
                    blocks_here = [
                        jnp.where(low, panels[index_of(r, e + 2 * pair)], panels[index_of(r, e + 2 * pair + 1)])
                        for r in used_rows
                    ]
                    high = [b[0:BS] for b in blocks_here]
                    rest = [b[BS:2 * BS] for b in blocks_here]
                    halves.append(jnp.concatenate(high + rest + high, axis=0))
                right = jnp.concatenate(halves, axis=1)
                first, depth = used_rows[0] * BS, len(used_rows) * BS
                lhs_high = dense[group, :, first:first + depth]
                lhs = jnp.concatenate([lhs_high, lhs_high, dense[group, :, width + first:width + first + depth]], axis=1)
                product = jnp.dot(lhs, right, preferred_element_type=jnp.float32)
                total = product if total is None else total + product
            for pair in range(2):
                value = total[:, pair * LANES:(pair + 1) * LANES]
                if not last:
                    for i in range(rows):
                        blocks[i, saved + 2 * n + pair] = value[i * BS:(i + 1) * BS]
                    continue
                if saved is not None:
                    value += jnp.concatenate([blocks[i, saved + 2 * n + pair] for i in range(rows)], axis=0)
                high = value.astype(jnp.bfloat16).astype(jnp.float32)
                rest = value - high
                turned = pltpu.roll(jnp.where(low, rest, high), BS, 1)
                at = plane * plane_ids + e + 2 * pair
                ap[at] = jnp.where(low, high, turned).astype(jnp.bfloat16)
                ap[at + 1] = jnp.where(low, turned, rest).astype(jnp.bfloat16)
            return carry

        lax.fori_loop(0, plane_ids // 4, four, 0)

    def near_index(origin):
        return lambda r, e: plan_s[origin, r, e]

    def far_index(group):
        def index_of(r, e):
            n = group * rows + r
            return plan_s[n_grp + n // hs, n % hs, e]
        return index_of

    def part_copy(s, k, window=None):
        first, last = stages[s][1:] if window is None else window
        here = pl.ds(first * BS, (last - first) * BS)
        return pltpu.make_async_remote_copy(
            src_ref=partial.at[k, :, here], dst_ref=arrived.at[k - 1, :, here],
            send_sem=part_send.at[s, k - 1], recv_sem=part_recv.at[s, k - 1],
            device_id={"dom": partner(k)},
        )

    def slot_rows(s, owner_dom, slot, at):
        first, last = stages[s][1:]
        line = hs + owner[0, slot]
        for c in range(first, last, 2):
            right = jnp.concatenate([ap[plan_s[sort_at + owner_dom, line, c + h]] for h in range(2)], axis=1)
            product = jnp.dot(left[at], right, preferred_element_type=jnp.float32)
            both = product[:BS] + product[BS:]
            one, two = both[:, :LANES], both[:, LANES:]
            partial[at, :, c * BS:(c + 2) * BS] = jnp.where(low, one, two) + pltpu.roll(jnp.where(low, two, one), BS, 1)

    def exchange(s):
        if merge and s == len(stages) - 1:
            exchange_merged()
            return

        def far_slot(step, carry):
            k = n_dom - step
            target = partner(k)
            slot_rows(s, target, target * cap, k)

            @pl.when(step > 1)
            def _():
                part_copy(s, k + 1).start()

            return carry

        lax.fori_loop(1, n_dom, far_slot, 0)
        own_slots(s, lambda: part_copy(s, 1).start())

    def own_slots(s, then=None):
        first, last = stages[s][1:]
        here = slice(first * BS, last * BS)
        slot_rows(s, me, me * cap, 0)
        if then is not None:
            then()
        for t in range(1, cap):
            slot_rows(s, me, me * cap + t, n_dom + t - 1)
        for r in range(owned):
            total = partial[0, :, here] * (owner[0, me * cap] == r).astype(jnp.float32)
            for t in range(1, cap):
                total += partial[n_dom + t - 1, :, here] * (owner[0, me * cap + t] == r).astype(jnp.float32)
            summed[r, :, here] = total

    def collect(s):
        if merge and s == len(stages) - 1:
            collect_merged()
            return
        first, last = stages[s][1:]

        def one(step, carry):
            k = n_dom - step
            part_copy(s, k).wait_recv()
            row = dom_in[partner(k), row_at:row_at + 1, :]
            for c in range(first, last, 2):
                here = slice(c * BS, (c + 2) * BS)
                value = arrived[k - 1, :, here]
                for r in range(owned):
                    summed[r, :, here] += jnp.where(row == r, value, 0.0)
            return carry

        lax.fori_loop(1, n_dom, one, 0)

    def way_window(way):
        first, last = stages[-1][1:]
        middle = (first + last) // 2
        return (first, middle) if way == 0 else (middle, last)

    def feed_copy(k, way, to, place):
        first, last = way_window(way)
        return pltpu.make_async_remote_copy(
            src_ref=partial.at[k, :, pl.ds(first * BS, (last - first) * BS)], dst_ref=feed.at[way, place],
            send_sem=feed_send.at[way, place], recv_sem=feed_recv.at[way, place],
            device_id={"dom": partner(to)},
        )

    def merged_copy(way):
        return pltpu.make_async_remote_copy(
            src_ref=merged.at[way], dst_ref=merged_in.at[way], send_sem=merged_send.at[way], recv_sem=merged_recv.at[way],
            device_id={"dom": partner(4 if way == 0 else 2)},
        )

    def feeds_of(k):
        if k > 5:
            return [feed_copy(k, 0, k - 4, k - 6), feed_copy(k, 1, k - 2, k - 6)]
        if k == 5:
            return [feed_copy(k, 0, 1, 2)]
        return [feed_copy(k, 1, 1, 2)] if k == 3 else []

    def direct_of(k):
        s = len(stages) - 1
        if k == 1:
            return [part_copy(s, k)]
        return [part_copy(s, k, way_window(0 if k < 4 else 1))] if k < 6 else []

    def exchange_merged():
        s = len(stages) - 1
        before = None
        for k in (7, 6, 5, 3, 4, 2, 1):
            slot_rows(s, partner(k), partner(k) * cap, k)
            if before is not None:
                for copy in feeds_of(before) + direct_of(before):
                    copy.start()
            before = k
        own_slots(s)
        for copy in feeds_of(before) + direct_of(before):
            copy.start()
        for way in range(2):
            window = way_window(way)
            for k in (7, 6, 5 if way == 0 else 3):
                feeds_of(k)[way if k > 5 else 0].wait_recv()
            for c in range(window[0], window[1], 2):
                here = slice((c - window[0]) * BS, (c - window[0] + 2) * BS)
                values = [feed[way, n, :, here] for n in range(3)]
                values.append(partial[4 if way == 0 else 2, :, c * BS:(c + 2) * BS])
                for r in range(owned):
                    total = None
                    for n in range(4):
                        term = jnp.where(source_row[4 * way + n:4 * way + n + 1, :] == r, values[n], 0.0)
                        total = term if total is None else total + term
                    merged[way, r, :, here] = total
        for way in range(2):
            merged_copy(way).start()

    def add_rows(row, values_of, window):
        for c in range(window[0], window[1], 2):
            here = slice(c * BS, (c + 2) * BS)
            value = values_of(here)
            for r in range(owned):
                summed[r, :, here] += jnp.where(row == r, value, 0.0)

    def collect_merged():
        first, last = stages[-1][1:]
        for k in (1, 3, 2, 5, 4):
            direct_of(k)[0].wait_recv()
            window = (first, last) if k == 1 else way_window(0 if k < 4 else 1)
            add_rows(dom_in[partner(k), row_at:row_at + 1, :], lambda here: arrived[k - 1, :, here], window)
        for way in range(2):
            merged_copy(way).wait_recv()
            first, last = way_window(way)
            for r in range(owned):
                summed[r, :, first * BS:last * BS] += merged_in[way, r]

    def take_halo(k, carry):
        halo_copy(k).wait_recv()
        for h in range(hs):
            convert(near_count + partner(k) * hs + h, rows + partner(k) * hs + h)
        return carry

    def own_halo(h, carry):
        def write(a, value):
            stage[:, a, :] = value

        for t in range(tiles):
            duplicate(outgoing[me * hs + h, :, t * LANES:(t + 1) * LANES], write, 2 * t)
        for q in range(kp):
            keep((rows + me * hs + h) * kp + q, stage[q])
        return carry

    in_halves = plane_ids <= ka and rows % 4 == 0
    for step in range(n_grp - 1):
        origins = (g - 1 - step, g + 1 + step)
        exists = (origins[0] >= 0, origins[1] < n_grp)
        for r in range(rows):
            for direction in range(2):
                origin = origins[direction]

                @pl.when(exists[direction])
                def _():
                    line_copy(direction, step, r, table.at[origin * rows + r], origin).wait_recv()

                if step < n_grp - 2:
                    @pl.when(exists[direction] & can_send[direction])
                    def _():
                        line_copy(direction, step + 1, r, table.at[origin * rows + r], origin).start()

            if step > 0:
                for direction in range(2):
                    @pl.when(exists[direction])
                    def _():
                        convert(origins[direction] * rows + r, direction * rows + r)
                        if in_halves and r == rows // 2 - 1:
                            multiply(
                                origins[direction], [(origins[direction], near_index(origins[direction]))],
                                range(rows // 2), direction * plane_ids // 2, False,
                            )
        if step == 0:
            lax.fori_loop(0, hs, own_halo, 0)
            lax.fori_loop(1, n_dom, take_halo, 0)
            multiply(g, [(g, near_index(g))] + [(n_grp + n, far_index(n)) for n in range(far_groups)])
            for s in range(len(stages)):
                if stages[s][0] < 0:
                    exchange(s)
        for direction in range(2):
            @pl.when(exists[direction])
            def _():
                if step == 0:
                    def take(r, carry):
                        convert(origins[direction] * rows + r, direction * rows + r)
                        return carry

                    lax.fori_loop(0, rows, take, 0)
                parts = [(origins[direction], near_index(origins[direction]))]
                if step > 0 and in_halves:
                    multiply(origins[direction], parts, range(rows // 2, rows), direction * plane_ids // 2)
                else:
                    multiply(origins[direction], parts)
        for s in range(len(stages)):
            if stages[s][0] == step:
                exchange(s)

    for k in range(1, n_grp):
        late_copy(k).wait()
    anywhere = late_in[0]
    for k in range(1, n_grp):
        anywhere |= late_in[k]
    late[...] = jnp.max(jnp.max(anywhere, axis=0, keepdims=True), axis=1, keepdims=True)

    for s in range(len(stages)):
        collect(s)

    for r in range(owned):
        for c in range(0, kc, 2):
            value = summed[r, :, c * BS:(c + 2) * BS]
            turned = pltpu.roll(value, BS, 1)
            blocks[r, c] = jnp.where(low, value, turned)
            blocks[r, c + 1] = jnp.where(low, turned, value)

    def place_row(r, carry):
        for c in range(kc):
            blocks[owned, c] = blocks[r, plan_s[rank_at + me, hs + r, c]]
        for c in range(0, kc, SUB):
            for t in range(tiles):
                out[r, c:c + SUB, t * LANES:(t + 1) * LANES] = jnp.where(
                    low, blocks[owned, c:c + SUB, 2 * t, :], blocks[owned, c:c + SUB, 2 * t + 1, :]
                )
        return carry

    lax.fori_loop(0, owned, place_row, 0)

    def drain(k, carry):
        halo_copy(k).wait_send()
        for s in range(len(stages) - int(merge)):
            part_copy(s, k).wait_send()
        return carry

    lax.fori_loop(1, n_dom, drain, 0)
    if merge:
        for k in range(1, n_dom):
            for copy in feeds_of(k) + direct_of(k):
                copy.wait_send()
        for way in range(2):
            merged_copy(way).wait_send()
    for step in range(n_grp - 1):
        for r in range(rows):
            for direction in range(2):
                origin = g - step if direction == 0 else g + step
                exists = (origin >= 0) & (origin < n_grp)

                @pl.when(exists & can_send[direction])
                def _():
                    line_copy(direction, step, r, table.at[r], origin).wait_send()


def per_device(
    operator_blocks, operator_cols, halo_count, prolong_blocks, prolong_cols,
    prolong_slot, send_lists, slot_owner_row, coarse_pattern,
):
    n_grp = lax.axis_size("grp")
    n_dom = lax.axis_size("dom")
    rows, ka = operator_cols.shape
    kp = prolong_cols.shape[1]
    owned, kc = coarse_pattern.shape
    hs = send_lists.shape[1] // n_dom
    cap = slot_owner_row.shape[1] // n_dom
    total_ids = owned * n_grp * n_dom
    used = n_dom + cap - 1
    panel_count = n_grp * rows + n_dom * hs
    groups = panel_count // rows
    width = rows * BS
    plan_rows = n_grp + 3 * n_dom
    quarter, half = kc // 4, kc // 2
    at_once = ((n_grp - 2, 0, kc),)
    by_distance = ((n_grp - 4, 0, quarter), (n_grp - 3, quarter, half), (n_grp - 2, half, kc))
    assert n_grp >= 3 and quarter % 2 == 0
    part = quarter * BS
    through_chip = n_dom == 8 and hs + owned + 2 <= SUB and n_dom * cap <= LANES
    assert n_dom & (n_dom - 1) == 0 and (n_dom * hs) % rows == 0 and n_dom * hs >= rows
    assert kp == SUB and ka % SUB == 0 and kc % SUB == 0 and LANES % kc == 0
    assert owned < rows and kc <= ka
    assert rows % 2 == 0 and rows <= SUB and hs + owned < SUB and (owned * n_dom) % 4 == 0
    vm = lambda dtype, *shape: pltpu.VMEM(shape, dtype)
    f32, bf16, i32 = jnp.float32, jnp.bfloat16, jnp.int32
    sem = lambda *shape: pltpu.SemaphoreType.DMA(shape)
    def call(stages, merge, number, name):
        scratch = [
            vm(f32, rows, kp, BS * BS), vm(f32, rows, ka, BS * BS), vm(f32, panel_count, kp, BS * BS),
            vm(f32, n_dom * hs, kp, BS * BS),
            vm(i32, SUB, LANES), vm(i32, n_grp, SUB, LANES), vm(i32, SUB, LANES),
            vm(i32, n_dom, SUB, LANES), vm(i32, n_dom, SUB, LANES),
            vm(i32, plan_rows, SUB, LANES), pltpu.SMEM((plan_rows, SUB, LANES), i32),
            vm(f32, rows, ka, BS, LANES), vm(bf16, groups, width, 2 * width),
            vm(f32, rows * kp + 1, BS, LANES), vm(f32, kp, BS, LANES),
            vm(bf16, (rows + n_dom * hs) * kp + 1, 2 * BS, LANES), vm(bf16, used, 2 * BS, width),
            vm(bf16, total_ids, width, LANES),
            vm(f32, used, BS, kc * BS), vm(f32, n_dom - 1, BS, kc * BS), vm(f32, owned, BS, kc * BS),
            sem(2), sem(2, n_grp - 1, rows), sem(2, n_grp - 1, rows), sem(n_dom), sem(n_dom),
            sem(n_grp), sem(n_grp), sem(n_dom), sem(n_dom), sem(1),
            sem(len(stages), n_dom - 1), sem(len(stages), n_dom - 1),
            vm(i32, SUB, LANES), vm(i32, n_grp, SUB, LANES), sem(n_grp), sem(n_grp),
            vm(f32, 2, 3, BS, part if merge else LANES), vm(f32, 2, owned, BS, part if merge else LANES),
            vm(f32, 2, owned, BS, part if merge else LANES), vm(i32, SUB, LANES), sem(2, 3), sem(2, 3), sem(2), sem(2),
        ]
        held = sum(math.prod(x.shape) * x.dtype.itemsize for x in scratch if x.memory_space == pltpu.VMEM)
        return pl.pallas_call(
            functools.partial(fused_kernel, n_grp, n_dom, rows, hs, ka, kp, kc, cap, owned, stages, merge),
            out_shape=(
                jax.ShapeDtypeStruct((owned, kc, BS * BS), f32), jax.ShapeDtypeStruct((1, 1), i32),
            ),
            in_specs=[smem_spec()] * 5 + [vmem_spec()] * 2 + [any_spec()] * 2,
            out_specs=(vmem_spec(), vmem_spec()),
            scratch_shapes=scratch,
            compiler_params=pltpu.CompilerParams(
                collective_id=number, has_side_effects=True, vmem_limit_bytes=min(held + SPARE, MOST_VMEM)
            ),
            name=name,
        )

    args = (
        operator_cols, halo_count, prolong_slot, send_lists, slot_owner_row, prolong_cols, coarse_pattern,
        prolong_blocks, operator_blocks,
    )
    args = tuple(pltpu.with_memory_space_constraint(x, pltpu.HBM) for x in args)
    result, late = call(by_distance, through_chip, 0, "coarse_rows")(*args)
    result = lax.cond(late.reshape(()) > 0, lambda: call(at_once, False, 1, "coarse_rows_at_once")(*args)[0], lambda: result)
    return result


def solution(mesh):
    blocks = P(("grp", "dom"), None, None)
    lists = P(("grp", "dom"), None)
    return jax.shard_map(
        per_device,
        mesh=mesh,
        in_specs=(blocks, lists, P(("grp", "dom")), blocks, lists, lists, lists, lists, lists),
        out_specs=blocks,
        check_vma=False,
    )
```

```python
import functools
import math

import jax
import jax.numpy as jnp
from jax import lax
from jax.experimental import pallas as pl
from jax.experimental.pallas import tpu as pltpu
from jax.sharding import PartitionSpec as P

BS = 64
KG = 12
LANES = 128
SUB = 8
MOST_VMEM = 67043328
SPARE = 6 << 20


def any_spec():
    return pl.BlockSpec(memory_space=pl.ANY)


def vmem_spec():
    return pl.BlockSpec(memory_space=pltpu.VMEM)


def smem_spec():
    return pl.BlockSpec(memory_space=pltpu.SMEM)


def fused_kernel(
    n_grp, n_dom, rows, hs, ka, kp, kc, cap, owned, stages, merge,
    cols, halo, slots, picked, owner, prolong_cols, pattern, prolong_in, operator_in,
    out, late,
    own_raw, operator, table, outgoing, grp_out, grp_in, dom_base, dom_out, dom_in, plan_v, plan_s,
    blocks, dense, own_dup, stage, panels, left, ap, partial, arrived, summed,
    load_sem, line_send, line_recv, halo_send, halo_recv,
    gmeta_send, gmeta_recv, dmeta_send, dmeta_recv, plan_sem, part_send, part_recv,
    late_out, late_in, late_send, late_recv,
    feed, merged, merged_in, source_row, feed_send, feed_recv, merged_send, merged_recv,
):
    g = lax.axis_index("grp")
    me = lax.axis_index("dom")
    near_count = n_grp * rows
    plane_ids = owned * n_dom
    halo_count_rows = n_dom * hs
    groups = n_grp + halo_count_rows // rows
    zero_at = (rows + halo_count_rows) * kp
    row_at = hs + owned
    sort_at = n_grp + n_dom
    rank_at = sort_at + n_dom
    width = rows * BS
    tiles = BS // 2
    low = lax.broadcasted_iota(jnp.int32, (1, LANES), 1) < BS
    lane = lax.broadcasted_iota(jnp.int32, (SUB, LANES), 1)
    sub = lax.broadcasted_iota(jnp.int32, (SUB, LANES), 0)

    barrier = pltpu.get_barrier_semaphore()
    for k in range(1, n_grp):
        pl.semaphore_signal(barrier, inc=1, device_id={"grp": lax.rem(g + k, n_grp)})
    for k in range(1, n_dom):
        pl.semaphore_signal(barrier, inc=1, device_id={"dom": lax.rem(me + k, n_dom)})
    own_load = pltpu.make_async_copy(prolong_in, own_raw, load_sem.at[0])
    operator_load = pltpu.make_async_copy(operator_in, operator, load_sem.at[1])
    own_load.start()
    operator_load.start()

    def partner(k):
        other = 0
        bit = 1
        while bit < n_dom:
            other += lax.rem(me // bit + k // bit, 2) * bit
            bit *= 2
        return other

    pl.semaphore_wait(barrier, n_grp + n_dom - 2)

    def line_copy(direction, step, r, src, origin):
        return pltpu.make_async_remote_copy(
            src_ref=src, dst_ref=table.at[origin * rows + r],
            send_sem=line_send.at[direction, step, r], recv_sem=line_recv.at[direction, step, r],
            device_id={"grp": g + 1 if direction == 0 else g - 1},
        )

    merge_sources = ((2, 3, 1, 0), (4, 5, 1, 0))

    def grp_meta(k):
        return pltpu.make_async_remote_copy(
            src_ref=grp_out, dst_ref=grp_in.at[g], send_sem=gmeta_send.at[k], recv_sem=gmeta_recv.at[k],
            device_id={"grp": lax.rem(g + k, n_grp)},
        )

    def dom_meta(k):
        target = partner(k)
        return pltpu.make_async_remote_copy(
            src_ref=dom_out.at[target], dst_ref=dom_in.at[me], send_sem=dmeta_send.at[k], recv_sem=dmeta_recv.at[k],
            device_id={"dom": target},
        )

    def halo_copy(k):
        target = partner(k)
        return pltpu.make_async_remote_copy(
            src_ref=outgoing.at[pl.ds(target * hs, hs)], dst_ref=table.at[pl.ds(near_count + me * hs, hs)],
            send_sem=halo_send.at[k], recv_sem=halo_recv.at[k],
            device_id={"dom": target},
        )

    can_send = (g < n_grp - 1, g > 0)

    def send_own(r):
        for direction in range(2):
            @pl.when(can_send[direction])
            def _():
                line_copy(direction, 0, r, prolong_in.at[r], g).start()

    send_own(0)
    grp_out[...] = jnp.zeros(grp_out.shape, jnp.int32)
    grp_out[0:rows, 0:kp] = prolong_cols[...]
    dom_base[...] = jnp.zeros(dom_base.shape, jnp.int32)
    for r in range(owned):
        for j in range(0, LANES, kc):
            dom_base[hs + r:hs + r + 1, j:j + kc] = pattern[r:r + 1, :]

    if merge:
        line = jnp.zeros((1, LANES), jnp.int32)
        for t in range(n_dom * cap):
            line = jnp.where(lane[0:1] == t, owner[0, t], line)
        dom_base[row_at + 1:row_at + 2, :] = line

    def for_dom(d, carry):
        dom_out[d] = dom_base[...]
        for h in range(hs):
            dom_out[d, h:h + 1, 0:kp] = prolong_cols[pl.ds(picked[0, d * hs + h], 1), :]
        dom_out[d, row_at:row_at + 1, :] = jnp.full((1, LANES), owner[0, d * cap], jnp.int32)
        return carry

    lax.fori_loop(0, n_dom, for_dom, 0)
    grp_in[g] = grp_out[...]
    dom_in[me] = dom_out[me]
    for k in range(1, n_grp):
        grp_meta(k).start()

    def start_dom_meta(k, carry):
        dom_meta(k).start()
        return carry

    lax.fori_loop(1, n_dom, start_dom_meta, 0)
    for r in range(1, rows):
        send_own(r)

    own_load.wait()

    def pick(n, carry):
        outgoing[n] = own_raw[picked[0, n]]
        return carry

    lax.fori_loop(0, halo_count_rows, pick, 0)

    def duplicate(x, write, at):
        turned = pltpu.roll(x, BS, 1)
        write(at, jnp.where(low, x, turned))
        write(at + 1, jnp.where(low, turned, x))

    def own_row(i, carry):
        def write(a, value):
            own_dup[pl.ds(i * kp, kp), a, :] = value

        for t in range(tiles):
            duplicate(own_raw[i, :, t * LANES:(t + 1) * LANES], write, 2 * t)
        return carry

    lax.fori_loop(0, rows, own_row, 0)

    def start_halo(k, carry):
        halo_copy(k).start()
        return carry

    lax.fori_loop(1, n_dom, start_halo, 0)
    own_dup[rows * kp] = jnp.zeros((BS, LANES), jnp.float32)
    panels[zero_at] = jnp.zeros((2 * BS, LANES), jnp.bfloat16)

    def split(value):
        high = value.astype(jnp.bfloat16)
        return high, (value - high.astype(jnp.float32)).astype(jnp.bfloat16)

    def keep(at, value):
        high, rest = split(value)
        panels[at, 0:BS] = high
        panels[at, BS:2 * BS] = rest

    def convert(panel, place):
        def write(a, value):
            stage[:, a, :] = value

        for t in range(tiles):
            duplicate(table[panel, :, t * LANES:(t + 1) * LANES], write, 2 * t)
        for q in range(kp):
            keep(place * kp + q, stage[q])

    operator_load.wait()

    def relay(n, carry):
        i = n // (ka // SUB)
        m = lax.rem(n, ka // SUB) * SUB

        def write(a, value):
            blocks[i, pl.ds(m, SUB), a, :] = value

        for t in range(tiles):
            duplicate(operator[i, pl.ds(m, SUB), t * LANES:(t + 1) * LANES], write, 2 * t)
        return carry

    lax.fori_loop(0, rows * (ka // SUB), relay, 0)

    def densify(i, group, slots_used, column_of):
        for pair in range(0, rows, 2):
            first = group * rows + pair
            wanted = jnp.where(low, first, first + 1)
            total = jnp.zeros((BS, LANES), jnp.float32)
            for m in slots_used:
                total += jnp.where(wanted == column_of(i, m), blocks[i, m], 0.0)
            high, rest = split(total)
            here = pl.ds(i * BS, BS)
            dense[group, here, pair * BS:(pair + 2) * BS] = high
            dense[group, here, width + pair * BS:width + (pair + 2) * BS] = rest

    def near_dense(n, carry):
        densify(n // n_grp, lax.rem(n, n_grp), range(KG), lambda i, m: cols[i, m])
        return carry

    def far_column(i, m):
        return jnp.where(m - KG < halo[i], near_count + cols[i, m], -1)

    far_groups = groups - n_grp

    def far_dense(n, carry):
        densify(n // far_groups, n_grp + lax.rem(n, far_groups), range(KG, ka), far_column)
        return carry

    lax.fori_loop(0, rows * n_grp, near_dense, 0)
    lax.fori_loop(0, rows * far_groups, far_dense, 0)

    for k in range(1, n_grp):
        grp_meta(k).wait()

    def wait_dom_meta(k, carry):
        dom_meta(k).wait()
        return carry

    lax.fori_loop(1, n_dom, wait_dom_meta, 0)

    def places(values, first_id, first_place):
        found = jnp.full((SUB, LANES), zero_at, jnp.int32)
        for q in range(kp):
            found = jnp.where(values[:, q:q + 1] == first_id + lane, (first_place + sub) * kp + q, found)
        return found

    for origin in range(n_grp):
        side = (origin > g).astype(jnp.int32)
        plan_v[origin] = places(grp_in[origin], origin * plane_ids, side * rows)

    slot_of_lane = lax.rem(lane, kc)

    pattern_line = (sub >= hs) & (sub < hs + owned)

    def dom_tables(d, wrong):
        values = dom_in[d]
        plan_v[n_grp + d] = places(values, g * plane_ids, rows + d * hs)
        plane = jnp.zeros((SUB, LANES), jnp.int32)
        for n in range(1, n_grp):
            plane += (values >= n * plane_ids).astype(jnp.int32)
        distance = jnp.abs(plane - g)
        order = distance * kc + slot_of_lane
        rank = jnp.zeros((SUB, LANES), jnp.int32)
        for s in range(1, kc):
            rank += (pltpu.roll(order, s, 1) < order).astype(jnp.int32)
        ordered = values
        for s in range(kc):
            ordered = jnp.where(pltpu.roll(rank, s, 1) == slot_of_lane, pltpu.roll(values, s, 1), ordered)
        plan_v[sort_at + d] = ordered
        plan_v[rank_at + d] = rank
        for after, _, last in stages:
            wrong |= (pattern_line & (rank < last) & (distance > after + 1)).astype(jnp.int32)
        return wrong

    if merge:
        for way in range(2):
            goal = partner(4 if way == 0 else 2) * cap
            for n, source in enumerate(merge_sources[way]):
                found = jnp.where(lane[0:1] == goal, dom_in[partner(source), row_at + 1:row_at + 2, :], 0)
                splat = jnp.broadcast_to(jnp.sum(found, axis=1, keepdims=True), (1, LANES))
                source_row[4 * way + n:4 * way + n + 1, :] = splat

    wrong = lax.fori_loop(0, n_dom, dom_tables, jnp.zeros((SUB, LANES), jnp.int32))
    plan_copy = pltpu.make_async_copy(plan_v, plan_s, plan_sem.at[0])
    plan_copy.start()
    late_out[...] = wrong
    late_in[g] = wrong

    def late_copy(k):
        return pltpu.make_async_remote_copy(
            src_ref=late_out, dst_ref=late_in.at[g], send_sem=late_send.at[k], recv_sem=late_recv.at[k],
            device_id={"grp": lax.rem(g + k, n_grp)},
        )


    def transposed(slot, at):
        for pair in range(0, rows, 2):
            both = []
            for i in range(pair, pair + 2):
                place = jnp.int32(rows * kp)
                for j in range(kp):
                    place = jnp.where(slots[i, j] == slot, i * kp + j, place)
                both.append(own_dup[place])
            turned = jnp.concatenate(both, axis=0).T
            high = turned.astype(jnp.bfloat16).astype(jnp.float32)
            upper = lax.broadcasted_iota(jnp.int32, (LANES, LANES), 0) < BS
            left[at, :, pair * BS:(pair + 2) * BS] = jnp.where(upper, high, turned - high).astype(jnp.bfloat16)

    def far_left(k, carry):
        transposed(partner(k) * cap, k)
        return carry

    lax.fori_loop(1, n_dom, far_left, 0)
    for k in range(1, n_grp):
        late_copy(k).start()
    for t in range(cap):
        transposed(me * cap + t, 0 if t == 0 else n_dom + t - 1)

    def own_panels(n, carry):
        keep(n, own_dup[n])
        return carry

    lax.fori_loop(0, rows * kp, own_panels, 0)
    plan_copy.wait()

    def multiply(plane, parts, used_rows=range(rows), saved=None, last=True):
        def four(n, carry):
            e = n * 4
            total = None
            for group, index_of in parts:
                halves = []
                for pair in range(2):
                    blocks_here = [
                        jnp.where(low, panels[index_of(r, e + 2 * pair)], panels[index_of(r, e + 2 * pair + 1)])
                        for r in used_rows
                    ]
                    high = [b[0:BS] for b in blocks_here]
                    rest = [b[BS:2 * BS] for b in blocks_here]
                    halves.append(jnp.concatenate(high + rest + high, axis=0))
                right = jnp.concatenate(halves, axis=1)
                first, depth = used_rows[0] * BS, len(used_rows) * BS
                lhs_high = dense[group, :, first:first + depth]
                lhs = jnp.concatenate([lhs_high, lhs_high, dense[group, :, width + first:width + first + depth]], axis=1)
                product = jnp.dot(lhs, right, preferred_element_type=jnp.float32)
                total = product if total is None else total + product
            for pair in range(2):
                value = total[:, pair * LANES:(pair + 1) * LANES]
                if not last:
                    for i in range(rows):
                        blocks[i, saved + 2 * n + pair] = value[i * BS:(i + 1) * BS]
                    continue
                if saved is not None:
                    value += jnp.concatenate([blocks[i, saved + 2 * n + pair] for i in range(rows)], axis=0)
                high = value.astype(jnp.bfloat16).astype(jnp.float32)
                rest = value - high
                turned = pltpu.roll(jnp.where(low, rest, high), BS, 1)
                at = plane * plane_ids + e + 2 * pair
                ap[at] = jnp.where(low, high, turned).astype(jnp.bfloat16)
                ap[at + 1] = jnp.where(low, turned, rest).astype(jnp.bfloat16)
            return carry

        lax.fori_loop(0, plane_ids // 4, four, 0, unroll=4)

    def near_index(origin):
        return lambda r, e: plan_s[origin, r, e]

    def far_index(group):
        def index_of(r, e):
            n = group * rows + r
            return plan_s[n_grp + n // hs, n % hs, e]
        return index_of

    def part_copy(s, k, window=None):
        first, last = stages[s][1:] if window is None else window
        here = pl.ds(first * BS, (last - first) * BS)
        return pltpu.make_async_remote_copy(
            src_ref=partial.at[k, :, here], dst_ref=arrived.at[k - 1, :, here],
            send_sem=part_send.at[s, k - 1], recv_sem=part_recv.at[s, k - 1],
            device_id={"dom": partner(k)},
        )

    def slot_rows(s, owner_dom, slot, at, window=None):
        first, last = stages[s][1:] if window is None else window
        line = hs + owner[0, slot]
        for c in range(first, last, 2):
            right = jnp.concatenate([ap[plan_s[sort_at + owner_dom, line, c + h]] for h in range(2)], axis=1)
            product = jnp.dot(left[at], right, preferred_element_type=jnp.float32)
            both = product[:BS] + product[BS:]
            one, two = both[:, :LANES], both[:, LANES:]
            partial[at, :, c * BS:(c + 2) * BS] = jnp.where(low, one, two) + pltpu.roll(jnp.where(low, two, one), BS, 1)

    def exchange(s):
        if merge and s == len(stages) - 1:
            exchange_merged()
            return

        def far_slot(step, carry):
            k = n_dom - step
            target = partner(k)
            slot_rows(s, target, target * cap, k)

            @pl.when(step > 1)
            def _():
                part_copy(s, k + 1).start()

            return carry

        lax.fori_loop(1, n_dom, far_slot, 0)
        own_slots(s, lambda: part_copy(s, 1).start())

    def own_slots(s, then=None):
        first, last = stages[s][1:]
        here = slice(first * BS, last * BS)
        slot_rows(s, me, me * cap, 0)
        if then is not None:
            then()
        for t in range(1, cap):
            slot_rows(s, me, me * cap + t, n_dom + t - 1)
        for r in range(owned):
            total = partial[0, :, here] * (owner[0, me * cap] == r).astype(jnp.float32)
            for t in range(1, cap):
                total += partial[n_dom + t - 1, :, here] * (owner[0, me * cap + t] == r).astype(jnp.float32)
            summed[r, :, here] = total

    def collect(s):
        if merge and s == len(stages) - 1:
            collect_merged()
            return
        first, last = stages[s][1:]

        def one(step, carry):
            k = n_dom - step
            part_copy(s, k).wait_recv()
            row = dom_in[partner(k), row_at:row_at + 1, :]
            for c in range(first, last, 2):
                here = slice(c * BS, (c + 2) * BS)
                value = arrived[k - 1, :, here]
                for r in range(owned):
                    summed[r, :, here] += jnp.where(row == r, value, 0.0)
            return carry

        lax.fori_loop(1, n_dom, one, 0)

    def way_window(way):
        first, last = stages[-1][1:]
        middle = (first + last) // 2
        return (first, middle) if way == 0 else (middle, last)

    def feed_copy(k, way, to, place):
        first, last = way_window(way)
        return pltpu.make_async_remote_copy(
            src_ref=partial.at[k, :, pl.ds(first * BS, (last - first) * BS)], dst_ref=feed.at[way, place],
            send_sem=feed_send.at[way, place], recv_sem=feed_recv.at[way, place],
            device_id={"dom": partner(to)},
        )

    def merged_copy(way):
        return pltpu.make_async_remote_copy(
            src_ref=merged.at[way], dst_ref=merged_in.at[way], send_sem=merged_send.at[way], recv_sem=merged_recv.at[way],
            device_id={"dom": partner(4 if way == 0 else 2)},
        )

    def feeds_of(k):
        if k > 5:
            return [feed_copy(k, 0, k - 4, k - 6), feed_copy(k, 1, k - 2, k - 6)]
        if k == 5:
            return [feed_copy(k, 0, 1, 2)]
        return [feed_copy(k, 1, 1, 2)] if k == 3 else []

    def direct_of(k):
        s = len(stages) - 1
        if k == 1:
            return [part_copy(s, k)]
        return [part_copy(s, k, way_window(0 if k < 4 else 1))] if k < 6 else []

    def exchange_merged():
        s = len(stages) - 1
        ready = []
        for k in (7, 6, 5, 3, 4, 2, 1):
            for way in range(2):
                slot_rows(s, partner(k), partner(k) * cap, k, way_window(way))
                for copy in ready:
                    copy.start()
                if k > 5:
                    ready = [feeds_of(k)[way]]
                elif k == 1:
                    ready = direct_of(k) if way == 1 else []
                else:
                    direct = (way == 0) == (k < 4)
                    ready = direct_of(k) if direct else feeds_of(k)
        own_slots(s)
        for copy in ready:
            copy.start()
        for way in range(2):
            window = way_window(way)
            for k in (7, 6, 5 if way == 0 else 3):
                feeds_of(k)[way if k > 5 else 0].wait_recv()
            for c in range(window[0], window[1], 2):
                here = slice((c - window[0]) * BS, (c - window[0] + 2) * BS)
                values = [feed[way, n, :, here] for n in range(3)]
                values.append(partial[4 if way == 0 else 2, :, c * BS:(c + 2) * BS])
                for r in range(owned):
                    total = None
                    for n in range(4):
                        term = jnp.where(source_row[4 * way + n:4 * way + n + 1, :] == r, values[n], 0.0)
                        total = term if total is None else total + term
                    merged[way, r, :, here] = total
        for way in range(2):
            merged_copy(way).start()

    def add_rows(row, values_of, window):
        for c in range(window[0], window[1], 2):
            here = slice(c * BS, (c + 2) * BS)
            value = values_of(here)
            for r in range(owned):
                summed[r, :, here] += jnp.where(row == r, value, 0.0)

    def collect_merged():
        first, last = stages[-1][1:]
        for k in (1, 3, 2, 5, 4):
            direct_of(k)[0].wait_recv()
            window = (first, last) if k == 1 else way_window(0 if k < 4 else 1)
            add_rows(dom_in[partner(k), row_at:row_at + 1, :], lambda here: arrived[k - 1, :, here], window)
        for way in range(2):
            merged_copy(way).wait_recv()
            first, last = way_window(way)
            for r in range(owned):
                summed[r, :, first * BS:last * BS] += merged_in[way, r]

    def take_halo(k, carry):
        halo_copy(k).wait_recv()
        for h in range(hs):
            convert(near_count + partner(k) * hs + h, rows + partner(k) * hs + h)
        return carry

    def own_halo(h, carry):
        def write(a, value):
            stage[:, a, :] = value

        for t in range(tiles):
            duplicate(outgoing[me * hs + h, :, t * LANES:(t + 1) * LANES], write, 2 * t)
        for q in range(kp):
            keep((rows + me * hs + h) * kp + q, stage[q])
        return carry

    in_halves = plane_ids <= ka and rows % 4 == 0
    for step in range(n_grp - 1):
        origins = (g - 1 - step, g + 1 + step)
        exists = (origins[0] >= 0, origins[1] < n_grp)
        for r in range(rows):
            for direction in range(2):
                origin = origins[direction]

                @pl.when(exists[direction])
                def _():
                    line_copy(direction, step, r, table.at[origin * rows + r], origin).wait_recv()

                if step < n_grp - 2:
                    @pl.when(exists[direction] & can_send[direction])
                    def _():
                        line_copy(direction, step + 1, r, table.at[origin * rows + r], origin).start()

            if step > 0:
                for direction in range(2):
                    @pl.when(exists[direction])
                    def _():
                        convert(origins[direction] * rows + r, direction * rows + r)
                        if in_halves and r == rows // 2 - 1:
                            multiply(
                                origins[direction], [(origins[direction], near_index(origins[direction]))],
                                range(rows // 2), direction * plane_ids // 2, False,
                            )
        if step == 0:
            lax.fori_loop(0, hs, own_halo, 0)
            lax.fori_loop(1, n_dom, take_halo, 0)
            multiply(g, [(g, near_index(g))] + [(n_grp + n, far_index(n)) for n in range(far_groups)])
            for s in range(len(stages)):
                if stages[s][0] < 0:
                    exchange(s)
        for direction in range(2):
            @pl.when(exists[direction])
            def _():
                if step == 0:
                    def take(r, carry):
                        convert(origins[direction] * rows + r, direction * rows + r)
                        return carry

                    lax.fori_loop(0, rows, take, 0)
                parts = [(origins[direction], near_index(origins[direction]))]
                if step > 0 and in_halves:
                    multiply(origins[direction], parts, range(rows // 2, rows), direction * plane_ids // 2)
                else:
                    multiply(origins[direction], parts)
        for s in range(len(stages)):
            if stages[s][0] == step:
                exchange(s)

    for k in range(1, n_grp):
        late_copy(k).wait()
    anywhere = late_in[0]
    for k in range(1, n_grp):
        anywhere |= late_in[k]
    late[...] = jnp.max(jnp.max(anywhere, axis=0, keepdims=True), axis=1, keepdims=True)

    for s in range(len(stages)):
        collect(s)

    for r in range(owned):
        for c in range(0, kc, 2):
            value = summed[r, :, c * BS:(c + 2) * BS]
            turned = pltpu.roll(value, BS, 1)
            blocks[r, c] = jnp.where(low, value, turned)
            blocks[r, c + 1] = jnp.where(low, turned, value)

    def place_row(r, carry):
        for c in range(kc):
            blocks[owned, c] = blocks[r, plan_s[rank_at + me, hs + r, c]]
        for c in range(0, kc, SUB):
            for t in range(tiles):
                out[r, c:c + SUB, t * LANES:(t + 1) * LANES] = jnp.where(
                    low, blocks[owned, c:c + SUB, 2 * t, :], blocks[owned, c:c + SUB, 2 * t + 1, :]
                )
        return carry

    lax.fori_loop(0, owned, place_row, 0)

    def drain(k, carry):
        halo_copy(k).wait_send()
        for s in range(len(stages) - int(merge)):
            part_copy(s, k).wait_send()
        return carry

    lax.fori_loop(1, n_dom, drain, 0)
    if merge:
        for k in range(1, n_dom):
            for copy in feeds_of(k) + direct_of(k):
                copy.wait_send()
        for way in range(2):
            merged_copy(way).wait_send()
    for step in range(n_grp - 1):
        for r in range(rows):
            for direction in range(2):
                origin = g - step if direction == 0 else g + step
                exists = (origin >= 0) & (origin < n_grp)

                @pl.when(exists & can_send[direction])
                def _():
                    line_copy(direction, step, r, table.at[r], origin).wait_send()


def per_device(
    operator_blocks, operator_cols, halo_count, prolong_blocks, prolong_cols,
    prolong_slot, send_lists, slot_owner_row, coarse_pattern,
):
    n_grp = lax.axis_size("grp")
    n_dom = lax.axis_size("dom")
    rows, ka = operator_cols.shape
    kp = prolong_cols.shape[1]
    owned, kc = coarse_pattern.shape
    hs = send_lists.shape[1] // n_dom
    cap = slot_owner_row.shape[1] // n_dom
    total_ids = owned * n_grp * n_dom
    used = n_dom + cap - 1
    panel_count = n_grp * rows + n_dom * hs
    groups = panel_count // rows
    width = rows * BS
    plan_rows = n_grp + 3 * n_dom
    quarter, half = kc // 4, kc // 2
    at_once = ((n_grp - 2, 0, kc),)
    by_distance = ((n_grp - 4, 0, quarter), (n_grp - 3, quarter, half), (n_grp - 2, half, kc))
    assert n_grp >= 3 and quarter % 2 == 0
    part = quarter * BS
    through_chip = n_dom == 8 and hs + owned + 2 <= SUB and n_dom * cap <= LANES
    assert n_dom & (n_dom - 1) == 0 and (n_dom * hs) % rows == 0 and n_dom * hs >= rows
    assert kp == SUB and ka % SUB == 0 and kc % SUB == 0 and LANES % kc == 0
    assert owned < rows and kc <= ka
    assert rows % 2 == 0 and rows <= SUB and hs + owned < SUB and (owned * n_dom) % 4 == 0
    vm = lambda dtype, *shape: pltpu.VMEM(shape, dtype)
    f32, bf16, i32 = jnp.float32, jnp.bfloat16, jnp.int32
    sem = lambda *shape: pltpu.SemaphoreType.DMA(shape)
    def call(stages, merge, number, name):
        scratch = [
            vm(f32, rows, kp, BS * BS), vm(f32, rows, ka, BS * BS), vm(f32, panel_count, kp, BS * BS),
            vm(f32, n_dom * hs, kp, BS * BS),
            vm(i32, SUB, LANES), vm(i32, n_grp, SUB, LANES), vm(i32, SUB, LANES),
            vm(i32, n_dom, SUB, LANES), vm(i32, n_dom, SUB, LANES),
            vm(i32, plan_rows, SUB, LANES), pltpu.SMEM((plan_rows, SUB, LANES), i32),
            vm(f32, rows, ka, BS, LANES), vm(bf16, groups, width, 2 * width),
            vm(f32, rows * kp + 1, BS, LANES), vm(f32, kp, BS, LANES),
            vm(bf16, (rows + n_dom * hs) * kp + 1, 2 * BS, LANES), vm(bf16, used, 2 * BS, width),
            vm(bf16, total_ids, width, LANES),
            vm(f32, used, BS, kc * BS), vm(f32, n_dom - 1, BS, kc * BS), vm(f32, owned, BS, kc * BS),
            sem(2), sem(2, n_grp - 1, rows), sem(2, n_grp - 1, rows), sem(n_dom), sem(n_dom),
            sem(n_grp), sem(n_grp), sem(n_dom), sem(n_dom), sem(1),
            sem(len(stages), n_dom - 1), sem(len(stages), n_dom - 1),
            vm(i32, SUB, LANES), vm(i32, n_grp, SUB, LANES), sem(n_grp), sem(n_grp),
            vm(f32, 2, 3, BS, part if merge else LANES), vm(f32, 2, owned, BS, part if merge else LANES),
            vm(f32, 2, owned, BS, part if merge else LANES), vm(i32, SUB, LANES), sem(2, 3), sem(2, 3), sem(2), sem(2),
        ]
        held = sum(math.prod(x.shape) * x.dtype.itemsize for x in scratch if x.memory_space == pltpu.VMEM)
        return pl.pallas_call(
            functools.partial(fused_kernel, n_grp, n_dom, rows, hs, ka, kp, kc, cap, owned, stages, merge),
            out_shape=(
                jax.ShapeDtypeStruct((owned, kc, BS * BS), f32), jax.ShapeDtypeStruct((1, 1), i32),
            ),
            in_specs=[smem_spec()] * 5 + [vmem_spec()] * 2 + [any_spec()] * 2,
            out_specs=(vmem_spec(), vmem_spec()),
            scratch_shapes=scratch,
            compiler_params=pltpu.CompilerParams(
                collective_id=number, has_side_effects=True, vmem_limit_bytes=min(held + SPARE, MOST_VMEM)
            ),
            name=name,
        )

    args = (
        operator_cols, halo_count, prolong_slot, send_lists, slot_owner_row, prolong_cols, coarse_pattern,
        prolong_blocks, operator_blocks,
    )
    args = tuple(pltpu.with_memory_space_constraint(x, pltpu.HBM) for x in args)
    result, late = call(by_distance, through_chip, 0, "coarse_rows")(*args)
    result = lax.cond(late.reshape(()) > 0, lambda: call(at_once, False, 1, "coarse_rows_at_once")(*args)[0], lambda: result)
    return result


def solution(mesh):
    blocks = P(("grp", "dom"), None, None)
    lists = P(("grp", "dom"), None)
    return jax.shard_map(
        per_device,
        mesh=mesh,
        in_specs=(blocks, lists, P(("grp", "dom")), blocks, lists, lists, lists, lists, lists),
        out_specs=blocks,
        check_vma=False,
    )
```

```python
import functools
import math

import jax
import jax.numpy as jnp
from jax import lax
from jax.experimental import pallas as pl
from jax.experimental.pallas import tpu as pltpu
from jax.sharding import PartitionSpec as P

BS = 64
KG = 12
LANES = 128
SUB = 8
MOST_VMEM = 67043328
SPARE = 6 << 20


def any_spec():
    return pl.BlockSpec(memory_space=pl.ANY)


def vmem_spec():
    return pl.BlockSpec(memory_space=pltpu.VMEM)


def smem_spec():
    return pl.BlockSpec(memory_space=pltpu.SMEM)


def fused_kernel(
    n_grp, n_dom, rows, hs, ka, kp, kc, cap, owned, stages, merge,
    cols, halo, slots, picked, owner, prolong_cols, pattern, prolong_in, operator_in,
    out, late,
    own_raw, operator, table, outgoing, grp_out, grp_in, dom_base, dom_out, dom_in, plan_v, plan_s,
    blocks, dense, own_dup, stage, panels, left, ap, partial, arrived, summed,
    load_sem, line_send, line_recv, halo_send, halo_recv,
    gmeta_send, gmeta_recv, dmeta_send, dmeta_recv, plan_sem, part_send, part_recv,
    late_out, late_in, late_send, late_recv,
    feed, merged, merged_in, source_row, feed_send, feed_recv, merged_send, merged_recv,
):
    g = lax.axis_index("grp")
    me = lax.axis_index("dom")
    near_count = n_grp * rows
    plane_ids = owned * n_dom
    halo_count_rows = n_dom * hs
    groups = n_grp + halo_count_rows // rows
    zero_at = (rows + halo_count_rows) * kp
    row_at = hs + owned
    sort_at = n_grp + n_dom
    rank_at = sort_at + n_dom
    width = rows * BS
    tiles = BS // 2
    low = lax.broadcasted_iota(jnp.int32, (1, LANES), 1) < BS
    lane = lax.broadcasted_iota(jnp.int32, (SUB, LANES), 1)
    sub = lax.broadcasted_iota(jnp.int32, (SUB, LANES), 0)

    barrier = pltpu.get_barrier_semaphore()
    for k in range(1, n_grp):
        pl.semaphore_signal(barrier, inc=1, device_id={"grp": lax.rem(g + k, n_grp)})
    for k in range(1, n_dom):
        pl.semaphore_signal(barrier, inc=1, device_id={"dom": lax.rem(me + k, n_dom)})
    own_load = pltpu.make_async_copy(prolong_in, own_raw, load_sem.at[0])
    operator_load = pltpu.make_async_copy(operator_in, operator, load_sem.at[1])
    own_load.start()
    operator_load.start()

    def partner(k):
        other = 0
        bit = 1
        while bit < n_dom:
            other += lax.rem(me // bit + k // bit, 2) * bit
            bit *= 2
        return other

    pl.semaphore_wait(barrier, n_grp + n_dom - 2)

    def line_copy(direction, step, r, src, origin):
        return pltpu.make_async_remote_copy(
            src_ref=src, dst_ref=table.at[origin * rows + r],
            send_sem=line_send.at[direction, step, r], recv_sem=line_recv.at[direction, step, r],
            device_id={"grp": g + 1 if direction == 0 else g - 1},
        )

    merge_sources = ((2, 3, 1, 0), (4, 5, 1, 0))

    def grp_meta(k):
        return pltpu.make_async_remote_copy(
            src_ref=grp_out, dst_ref=grp_in.at[g], send_sem=gmeta_send.at[k], recv_sem=gmeta_recv.at[k],
            device_id={"grp": lax.rem(g + k, n_grp)},
        )

    def dom_meta(k):
        target = partner(k)
        return pltpu.make_async_remote_copy(
            src_ref=dom_out.at[target], dst_ref=dom_in.at[me], send_sem=dmeta_send.at[k], recv_sem=dmeta_recv.at[k],
            device_id={"dom": target},
        )

    def halo_copy(k):
        target = partner(k)
        return pltpu.make_async_remote_copy(
            src_ref=outgoing.at[pl.ds(target * hs, hs)], dst_ref=table.at[pl.ds(near_count + me * hs, hs)],
            send_sem=halo_send.at[k], recv_sem=halo_recv.at[k],
            device_id={"dom": target},
        )

    can_send = (g < n_grp - 1, g > 0)

    def send_own(r):
        for direction in range(2):
            @pl.when(can_send[direction])
            def _():
                line_copy(direction, 0, r, prolong_in.at[r], g).start()

    send_own(0)
    grp_out[...] = jnp.zeros(grp_out.shape, jnp.int32)
    grp_out[0:rows, 0:kp] = prolong_cols[...]
    dom_base[...] = jnp.zeros(dom_base.shape, jnp.int32)
    for r in range(owned):
        for j in range(0, LANES, kc):
            dom_base[hs + r:hs + r + 1, j:j + kc] = pattern[r:r + 1, :]

    if merge:
        line = jnp.zeros((1, LANES), jnp.int32)
        for t in range(n_dom * cap):
            line = jnp.where(lane[0:1] == t, owner[0, t], line)
        dom_base[row_at + 1:row_at + 2, :] = line

    def for_dom(d, carry):
        dom_out[d] = dom_base[...]
        for h in range(hs):
            dom_out[d, h:h + 1, 0:kp] = prolong_cols[pl.ds(picked[0, d * hs + h], 1), :]
        dom_out[d, row_at:row_at + 1, :] = jnp.full((1, LANES), owner[0, d * cap], jnp.int32)
        return carry

    lax.fori_loop(0, n_dom, for_dom, 0)
    grp_in[g] = grp_out[...]
    dom_in[me] = dom_out[me]
    for k in range(1, n_grp):
        grp_meta(k).start()

    def start_dom_meta(k, carry):
        dom_meta(k).start()
        return carry

    lax.fori_loop(1, n_dom, start_dom_meta, 0)
    for r in range(1, rows):
        send_own(r)

    own_load.wait()

    def pick(n, carry):
        outgoing[n] = own_raw[picked[0, n]]
        return carry

    lax.fori_loop(0, halo_count_rows, pick, 0)

    def duplicate(x, write, at):
        turned = pltpu.roll(x, BS, 1)
        write(at, jnp.where(low, x, turned))
        write(at + 1, jnp.where(low, turned, x))

    def own_row(i, carry):
        def write(a, value):
            own_dup[pl.ds(i * kp, kp), a, :] = value

        for t in range(tiles):
            duplicate(own_raw[i, :, t * LANES:(t + 1) * LANES], write, 2 * t)
        return carry

    lax.fori_loop(0, rows, own_row, 0)

    def start_halo(k, carry):
        halo_copy(k).start()
        return carry

    lax.fori_loop(1, n_dom, start_halo, 0)
    own_dup[rows * kp] = jnp.zeros((BS, LANES), jnp.float32)
    panels[zero_at] = jnp.zeros((2 * BS, LANES), jnp.bfloat16)

    def split(value):
        high = value.astype(jnp.bfloat16)
        return high, (value - high.astype(jnp.float32)).astype(jnp.bfloat16)

    def keep(at, value):
        high, rest = split(value)
        panels[at, 0:BS] = high
        panels[at, BS:2 * BS] = rest

    def convert(panel, place):
        def write(a, value):
            stage[:, a, :] = value

        for t in range(tiles):
            duplicate(table[panel, :, t * LANES:(t + 1) * LANES], write, 2 * t)
        for q in range(kp):
            keep(place * kp + q, stage[q])

    operator_load.wait()

    def relay(n, carry):
        i = n // (ka // SUB)
        m = lax.rem(n, ka // SUB) * SUB

        def write(a, value):
            blocks[i, pl.ds(m, SUB), a, :] = value

        for t in range(tiles):
            duplicate(operator[i, pl.ds(m, SUB), t * LANES:(t + 1) * LANES], write, 2 * t)
        return carry

    lax.fori_loop(0, rows * (ka // SUB), relay, 0)

    def densify(i, group, slots_used, column_of):
        for pair in range(0, rows, 2):
            first = group * rows + pair
            wanted = jnp.where(low, first, first + 1)
            total = jnp.zeros((BS, LANES), jnp.float32)
            for m in slots_used:
                total += jnp.where(wanted == column_of(i, m), blocks[i, m], 0.0)
            high, rest = split(total)
            here = pl.ds(i * BS, BS)
            dense[group, here, pair * BS:(pair + 2) * BS] = high
            dense[group, here, width + pair * BS:width + (pair + 2) * BS] = rest

    def near_dense(n, carry):
        densify(n // n_grp, lax.rem(n, n_grp), range(KG), lambda i, m: cols[i, m])
        return carry

    def far_column(i, m):
        return jnp.where(m - KG < halo[i], near_count + cols[i, m], -1)

    far_groups = groups - n_grp

    def far_dense(n, carry):
        densify(n // far_groups, n_grp + lax.rem(n, far_groups), range(KG, ka), far_column)
        return carry

    lax.fori_loop(0, rows * n_grp, near_dense, 0)
    lax.fori_loop(0, rows * far_groups, far_dense, 0)

    for k in range(1, n_grp):
        grp_meta(k).wait()

    def wait_dom_meta(k, carry):
        dom_meta(k).wait()
        return carry

    lax.fori_loop(1, n_dom, wait_dom_meta, 0)

    def places(values, first_id, first_place):
        found = jnp.full((SUB, LANES), zero_at, jnp.int32)
        for q in range(kp):
            found = jnp.where(values[:, q:q + 1] == first_id + lane, (first_place + sub) * kp + q, found)
        return found

    for origin in range(n_grp):
        side = (origin > g).astype(jnp.int32)
        plan_v[origin] = places(grp_in[origin], origin * plane_ids, side * rows)

    slot_of_lane = lax.rem(lane, kc)

    pattern_line = (sub >= hs) & (sub < hs + owned)

    def dom_tables(d, wrong):
        values = dom_in[d]
        plan_v[n_grp + d] = places(values, g * plane_ids, rows + d * hs)
        plane = jnp.zeros((SUB, LANES), jnp.int32)
        for n in range(1, n_grp):
            plane += (values >= n * plane_ids).astype(jnp.int32)
        distance = jnp.abs(plane - g)
        order = distance * kc + slot_of_lane
        rank = jnp.zeros((SUB, LANES), jnp.int32)
        for s in range(1, kc):
            rank += (pltpu.roll(order, s, 1) < order).astype(jnp.int32)
        ordered = values
        for s in range(kc):
            ordered = jnp.where(pltpu.roll(rank, s, 1) == slot_of_lane, pltpu.roll(values, s, 1), ordered)
        plan_v[sort_at + d] = ordered
        plan_v[rank_at + d] = rank
        for after, _, last in stages:
            wrong |= (pattern_line & (rank < last) & (distance > after + 1)).astype(jnp.int32)
        return wrong

    if merge:
        for way in range(2):
            goal = partner(4 if way == 0 else 2) * cap
            for n, source in enumerate(merge_sources[way]):
                found = jnp.where(lane[0:1] == goal, dom_in[partner(source), row_at + 1:row_at + 2, :], 0)
                splat = jnp.broadcast_to(jnp.sum(found, axis=1, keepdims=True), (1, LANES))
                source_row[4 * way + n:4 * way + n + 1, :] = splat

    wrong = lax.fori_loop(0, n_dom, dom_tables, jnp.zeros((SUB, LANES), jnp.int32))
    plan_copy = pltpu.make_async_copy(plan_v, plan_s, plan_sem.at[0])
    plan_copy.start()
    late_out[...] = wrong
    late_in[g] = wrong

    def late_copy(k):
        return pltpu.make_async_remote_copy(
            src_ref=late_out, dst_ref=late_in.at[g], send_sem=late_send.at[k], recv_sem=late_recv.at[k],
            device_id={"grp": lax.rem(g + k, n_grp)},
        )


    def transposed(slot, at):
        for pair in range(0, rows, 2):
            both = []
            for i in range(pair, pair + 2):
                place = jnp.int32(rows * kp)
                for j in range(kp):
                    place = jnp.where(slots[i, j] == slot, i * kp + j, place)
                both.append(own_dup[place])
            turned = jnp.concatenate(both, axis=0).T
            high = turned.astype(jnp.bfloat16).astype(jnp.float32)
            upper = lax.broadcasted_iota(jnp.int32, (LANES, LANES), 0) < BS
            left[at, :, pair * BS:(pair + 2) * BS] = jnp.where(upper, high, turned - high).astype(jnp.bfloat16)

    def far_left(k, carry):
        transposed(partner(k) * cap, k)
        return carry

    lax.fori_loop(1, n_dom, far_left, 0)
    for k in range(1, n_grp):
        late_copy(k).start()
    for t in range(cap):
        transposed(me * cap + t, 0 if t == 0 else n_dom + t - 1)

    def own_panels(n, carry):
        keep(n, own_dup[n])
        return carry

    lax.fori_loop(0, rows * kp, own_panels, 0)
    plan_copy.wait()

    def multiply(plane, parts, used_rows=range(rows), saved=None, last=True):
        def four(n, carry):
            e = n * 4
            total = None
            for group, index_of in parts:
                halves = []
                for pair in range(2):
                    blocks_here = [
                        jnp.where(low, panels[index_of(r, e + 2 * pair)], panels[index_of(r, e + 2 * pair + 1)])
                        for r in used_rows
                    ]
                    high = [b[0:BS] for b in blocks_here]
                    rest = [b[BS:2 * BS] for b in blocks_here]
                    halves.append(jnp.concatenate(high + rest + high, axis=0))
                right = jnp.concatenate(halves, axis=1)
                first, depth = used_rows[0] * BS, len(used_rows) * BS
                lhs_high = dense[group, :, first:first + depth]
                lhs = jnp.concatenate([lhs_high, lhs_high, dense[group, :, width + first:width + first + depth]], axis=1)
                product = jnp.dot(lhs, right, preferred_element_type=jnp.float32)
                total = product if total is None else total + product
            for pair in range(2):
                value = total[:, pair * LANES:(pair + 1) * LANES]
                if not last:
                    for i in range(rows):
                        blocks[i, saved + 2 * n + pair] = value[i * BS:(i + 1) * BS]
                    continue
                if saved is not None:
                    value += jnp.concatenate([blocks[i, saved + 2 * n + pair] for i in range(rows)], axis=0)
                high = value.astype(jnp.bfloat16).astype(jnp.float32)
                rest = value - high
                turned = pltpu.roll(jnp.where(low, rest, high), BS, 1)
                at = plane * plane_ids + e + 2 * pair
                ap[at] = jnp.where(low, high, turned).astype(jnp.bfloat16)
                ap[at + 1] = jnp.where(low, turned, rest).astype(jnp.bfloat16)
            return carry

        lax.fori_loop(0, plane_ids // 4, four, 0, unroll=4)

    def near_index(origin):
        return lambda r, e: plan_s[origin, r, e]

    def far_index(group):
        def index_of(r, e):
            n = group * rows + r
            return plan_s[n_grp + n // hs, n % hs, e]
        return index_of

    def part_copy(s, k, window=None):
        first, last = stages[s][1:] if window is None else window
        here = pl.ds(first * BS, (last - first) * BS)
        return pltpu.make_async_remote_copy(
            src_ref=partial.at[k, :, here], dst_ref=arrived.at[k - 1, :, here],
            send_sem=part_send.at[s, k - 1], recv_sem=part_recv.at[s, k - 1],
            device_id={"dom": partner(k)},
        )

    def slot_rows(s, owner_dom, slot, at, window=None):
        first, last = stages[s][1:] if window is None else window
        line = hs + owner[0, slot]
        for c in range(first, last, 2):
            right = jnp.concatenate([ap[plan_s[sort_at + owner_dom, line, c + h]] for h in range(2)], axis=1)
            product = jnp.dot(left[at], right, preferred_element_type=jnp.float32)
            both = product[:BS] + product[BS:]
            one, two = both[:, :LANES], both[:, LANES:]
            partial[at, :, c * BS:(c + 2) * BS] = jnp.where(low, one, two) + pltpu.roll(jnp.where(low, two, one), BS, 1)

    def exchange(s):
        if merge and s == len(stages) - 1:
            exchange_merged()
            return

        def far_slot(step, carry):
            k = n_dom - step
            target = partner(k)
            slot_rows(s, target, target * cap, k)

            @pl.when(step > 1)
            def _():
                part_copy(s, k + 1).start()

            return carry

        lax.fori_loop(1, n_dom, far_slot, 0)
        own_slots(s, lambda: part_copy(s, 1).start())

    def own_slots(s, then=None):
        first, last = stages[s][1:]
        here = slice(first * BS, last * BS)
        slot_rows(s, me, me * cap, 0)
        if then is not None:
            then()
        for t in range(1, cap):
            slot_rows(s, me, me * cap + t, n_dom + t - 1)
        for r in range(owned):
            total = partial[0, :, here] * (owner[0, me * cap] == r).astype(jnp.float32)
            for t in range(1, cap):
                total += partial[n_dom + t - 1, :, here] * (owner[0, me * cap + t] == r).astype(jnp.float32)
            summed[r, :, here] = total

    def collect(s):
        if merge and s == len(stages) - 1:
            collect_merged()
            return
        first, last = stages[s][1:]

        def one(step, carry):
            k = n_dom - step
            part_copy(s, k).wait_recv()
            row = dom_in[partner(k), row_at:row_at + 1, :]
            for c in range(first, last, 2):
                here = slice(c * BS, (c + 2) * BS)
                value = arrived[k - 1, :, here]
                for r in range(owned):
                    summed[r, :, here] += jnp.where(row == r, value, 0.0)
            return carry

        lax.fori_loop(1, n_dom, one, 0)

    def way_window(way):
        first, last = stages[-1][1:]
        middle = (first + last) // 2
        return (first, middle) if way == 0 else (middle, last)

    def feed_copy(k, way, to, place):
        first, last = way_window(way)
        return pltpu.make_async_remote_copy(
            src_ref=partial.at[k, :, pl.ds(first * BS, (last - first) * BS)], dst_ref=feed.at[way, place],
            send_sem=feed_send.at[way, place], recv_sem=feed_recv.at[way, place],
            device_id={"dom": partner(to)},
        )

    def merged_copy(way):
        return pltpu.make_async_remote_copy(
            src_ref=merged.at[way], dst_ref=merged_in.at[way], send_sem=merged_send.at[way], recv_sem=merged_recv.at[way],
            device_id={"dom": partner(4 if way == 0 else 2)},
        )

    def feeds_of(k):
        if k > 5:
            return [feed_copy(k, 0, k - 4, k - 6), feed_copy(k, 1, k - 2, k - 6)]
        if k == 5:
            return [feed_copy(k, 0, 1, 2)]
        return [feed_copy(k, 1, 1, 2)] if k == 3 else []

    def direct_of(k):
        s = len(stages) - 1
        if k == 1:
            return [part_copy(s, k)]
        return [part_copy(s, k, way_window(0 if k < 4 else 1))] if k < 6 else []

    def exchange_merged():
        s = len(stages) - 1
        ready = []
        for k in (7, 6, 5, 3, 4, 2, 1):
            for way in range(2):
                slot_rows(s, partner(k), partner(k) * cap, k, way_window(way))
                for copy in ready:
                    copy.start()
                if k > 5:
                    ready = [feeds_of(k)[way]]
                elif k == 1:
                    ready = direct_of(k) if way == 1 else []
                else:
                    direct = (way == 0) == (k < 4)
                    ready = direct_of(k) if direct else feeds_of(k)
        own_slots(s)
        for copy in ready:
            copy.start()
        for way in range(2):
            window = way_window(way)
            for k in (7, 6, 5 if way == 0 else 3):
                feeds_of(k)[way if k > 5 else 0].wait_recv()
            for c in range(window[0], window[1], 2):
                here = slice((c - window[0]) * BS, (c - window[0] + 2) * BS)
                values = [feed[way, n, :, here] for n in range(3)]
                values.append(partial[4 if way == 0 else 2, :, c * BS:(c + 2) * BS])
                for r in range(owned):
                    total = None
                    for n in range(4):
                        term = jnp.where(source_row[4 * way + n:4 * way + n + 1, :] == r, values[n], 0.0)
                        total = term if total is None else total + term
                    merged[way, r, :, here] = total
        for way in range(2):
            merged_copy(way).start()

    def add_rows(row, values_of, window):
        for c in range(window[0], window[1], 2):
            here = slice(c * BS, (c + 2) * BS)
            value = values_of(here)
            for r in range(owned):
                summed[r, :, here] += jnp.where(row == r, value, 0.0)

    def collect_merged():
        first, last = stages[-1][1:]
        for k in (1, 3, 2, 5, 4):
            direct_of(k)[0].wait_recv()
            window = (first, last) if k == 1 else way_window(0 if k < 4 else 1)
            add_rows(dom_in[partner(k), row_at:row_at + 1, :], lambda here: arrived[k - 1, :, here], window)
        for way in range(2):
            merged_copy(way).wait_recv()
            first, last = way_window(way)
            for r in range(owned):
                summed[r, :, first * BS:last * BS] += merged_in[way, r]

    def take_halo(k, carry):
        halo_copy(k).wait_recv()
        for h in range(hs):
            convert(near_count + partner(k) * hs + h, rows + partner(k) * hs + h)
        return carry

    def own_halo(h, carry):
        def write(a, value):
            stage[:, a, :] = value

        for t in range(tiles):
            duplicate(outgoing[me * hs + h, :, t * LANES:(t + 1) * LANES], write, 2 * t)
        for q in range(kp):
            keep((rows + me * hs + h) * kp + q, stage[q])
        return carry

    in_halves = plane_ids <= ka and rows % 4 == 0
    for step in range(n_grp - 1):
        origins = (g - 1 - step, g + 1 + step)
        exists = (origins[0] >= 0, origins[1] < n_grp)
        for r in range(rows):
            for direction in range(2):
                origin = origins[direction]

                @pl.when(exists[direction])
                def _():
                    line_copy(direction, step, r, table.at[origin * rows + r], origin).wait_recv()

                if step < n_grp - 2:
                    @pl.when(exists[direction] & can_send[direction])
                    def _():
                        line_copy(direction, step + 1, r, table.at[origin * rows + r], origin).start()

            if step > 0:
                for direction in range(2):
                    @pl.when(exists[direction])
                    def _():
                        convert(origins[direction] * rows + r, direction * rows + r)
                        if in_halves and r == rows // 2 - 1:
                            multiply(
                                origins[direction], [(origins[direction], near_index(origins[direction]))],
                                range(rows // 2), direction * plane_ids // 2, False,
                            )
        if step == 0:
            lax.fori_loop(0, hs, own_halo, 0)
            lax.fori_loop(1, n_dom, take_halo, 0)
            multiply(g, [(g, near_index(g))] + [(n_grp + n, far_index(n)) for n in range(far_groups)])
            for s in range(len(stages)):
                if stages[s][0] < 0:
                    exchange(s)
        for direction in range(2):
            @pl.when(exists[direction])
            def _():
                if step == 0:
                    def take(r, carry):
                        convert(origins[direction] * rows + r, direction * rows + r)
                        return carry

                    lax.fori_loop(0, rows, take, 0)
                parts = [(origins[direction], near_index(origins[direction]))]
                if step > 0 and in_halves:
                    multiply(origins[direction], parts, range(rows // 2, rows), direction * plane_ids // 2)
                else:
                    multiply(origins[direction], parts)
        for s in range(len(stages)):
            if stages[s][0] == step:
                exchange(s)

    for k in range(1, n_grp):
        late_copy(k).wait()
    anywhere = late_in[0]
    for k in range(1, n_grp):
        anywhere |= late_in[k]
    late[...] = jnp.max(jnp.max(anywhere, axis=0, keepdims=True), axis=1, keepdims=True)

    for s in range(len(stages)):
        collect(s)

    for r in range(owned):
        for c in range(0, kc, 2):
            value = summed[r, :, c * BS:(c + 2) * BS]
            turned = pltpu.roll(value, BS, 1)
            blocks[r, c] = jnp.where(low, value, turned)
            blocks[r, c + 1] = jnp.where(low, turned, value)

    def place_row(r, carry):
        for c in range(kc):
            blocks[owned, c] = blocks[r, plan_s[rank_at + me, hs + r, c]]
        for c in range(0, kc, SUB):
            for t in range(tiles):
                out[r, c:c + SUB, t * LANES:(t + 1) * LANES] = jnp.where(
                    low, blocks[owned, c:c + SUB, 2 * t, :], blocks[owned, c:c + SUB, 2 * t + 1, :]
                )
        return carry

    lax.fori_loop(0, owned, place_row, 0, unroll=True)

    def drain(k, carry):
        halo_copy(k).wait_send()
        for s in range(len(stages) - int(merge)):
            part_copy(s, k).wait_send()
        return carry

    lax.fori_loop(1, n_dom, drain, 0)
    if merge:
        for k in range(1, n_dom):
            for copy in feeds_of(k) + direct_of(k):
                copy.wait_send()
        for way in range(2):
            merged_copy(way).wait_send()
    for step in range(n_grp - 1):
        for r in range(rows):
            for direction in range(2):
                origin = g - step if direction == 0 else g + step
                exists = (origin >= 0) & (origin < n_grp)

                @pl.when(exists & can_send[direction])
                def _():
                    line_copy(direction, step, r, table.at[r], origin).wait_send()


def per_device(
    operator_blocks, operator_cols, halo_count, prolong_blocks, prolong_cols,
    prolong_slot, send_lists, slot_owner_row, coarse_pattern,
):
    n_grp = lax.axis_size("grp")
    n_dom = lax.axis_size("dom")
    rows, ka = operator_cols.shape
    kp = prolong_cols.shape[1]
    owned, kc = coarse_pattern.shape
    hs = send_lists.shape[1] // n_dom
    cap = slot_owner_row.shape[1] // n_dom
    total_ids = owned * n_grp * n_dom
    used = n_dom + cap - 1
    panel_count = n_grp * rows + n_dom * hs
    groups = panel_count // rows
    width = rows * BS
    plan_rows = n_grp + 3 * n_dom
    quarter, half = kc // 4, kc // 2
    at_once = ((n_grp - 2, 0, kc),)
    by_distance = ((n_grp - 4, 0, quarter), (n_grp - 3, quarter, half), (n_grp - 2, half, kc))
    assert n_grp >= 3 and quarter % 2 == 0
    part = quarter * BS
    through_chip = n_dom == 8 and hs + owned + 2 <= SUB and n_dom * cap <= LANES
    assert n_dom & (n_dom - 1) == 0 and (n_dom * hs) % rows == 0 and n_dom * hs >= rows
    assert kp == SUB and ka % SUB == 0 and kc % SUB == 0 and LANES % kc == 0
    assert owned < rows and kc <= ka
    assert rows % 2 == 0 and rows <= SUB and hs + owned < SUB and (owned * n_dom) % 4 == 0
    vm = lambda dtype, *shape: pltpu.VMEM(shape, dtype)
    f32, bf16, i32 = jnp.float32, jnp.bfloat16, jnp.int32
    sem = lambda *shape: pltpu.SemaphoreType.DMA(shape)
    def call(stages, merge, number, name):
        scratch = [
            vm(f32, rows, kp, BS * BS), vm(f32, rows, ka, BS * BS), vm(f32, panel_count, kp, BS * BS),
            vm(f32, n_dom * hs, kp, BS * BS),
            vm(i32, SUB, LANES), vm(i32, n_grp, SUB, LANES), vm(i32, SUB, LANES),
            vm(i32, n_dom, SUB, LANES), vm(i32, n_dom, SUB, LANES),
            vm(i32, plan_rows, SUB, LANES), pltpu.SMEM((plan_rows, SUB, LANES), i32),
            vm(f32, rows, ka, BS, LANES), vm(bf16, groups, width, 2 * width),
            vm(f32, rows * kp + 1, BS, LANES), vm(f32, kp, BS, LANES),
            vm(bf16, (rows + n_dom * hs) * kp + 1, 2 * BS, LANES), vm(bf16, used, 2 * BS, width),
            vm(bf16, total_ids, width, LANES),
            vm(f32, used, BS, kc * BS), vm(f32, n_dom - 1, BS, kc * BS), vm(f32, owned, BS, kc * BS),
            sem(2), sem(2, n_grp - 1, rows), sem(2, n_grp - 1, rows), sem(n_dom), sem(n_dom),
            sem(n_grp), sem(n_grp), sem(n_dom), sem(n_dom), sem(1),
            sem(len(stages), n_dom - 1), sem(len(stages), n_dom - 1),
            vm(i32, SUB, LANES), vm(i32, n_grp, SUB, LANES), sem(n_grp), sem(n_grp),
            vm(f32, 2, 3, BS, part if merge else LANES), vm(f32, 2, owned, BS, part if merge else LANES),
            vm(f32, 2, owned, BS, part if merge else LANES), vm(i32, SUB, LANES), sem(2, 3), sem(2, 3), sem(2), sem(2),
        ]
        held = sum(math.prod(x.shape) * x.dtype.itemsize for x in scratch if x.memory_space == pltpu.VMEM)
        return pl.pallas_call(
            functools.partial(fused_kernel, n_grp, n_dom, rows, hs, ka, kp, kc, cap, owned, stages, merge),
            out_shape=(
                jax.ShapeDtypeStruct((owned, kc, BS * BS), f32), jax.ShapeDtypeStruct((1, 1), i32),
            ),
            in_specs=[smem_spec()] * 5 + [vmem_spec()] * 2 + [any_spec()] * 2,
            out_specs=(vmem_spec(), vmem_spec()),
            scratch_shapes=scratch,
            compiler_params=pltpu.CompilerParams(
                collective_id=number, has_side_effects=True, vmem_limit_bytes=min(held + SPARE, MOST_VMEM)
            ),
            name=name,
        )

    args = (
        operator_cols, halo_count, prolong_slot, send_lists, slot_owner_row, prolong_cols, coarse_pattern,
        prolong_blocks, operator_blocks,
    )
    args = tuple(pltpu.with_memory_space_constraint(x, pltpu.HBM) for x in args)
    result, late = call(by_distance, through_chip, 0, "coarse_rows")(*args)
    result = lax.cond(late.reshape(()) > 0, lambda: call(at_once, False, 1, "coarse_rows_at_once")(*args)[0], lambda: result)
    return result


def solution(mesh):
    blocks = P(("grp", "dom"), None, None)
    lists = P(("grp", "dom"), None)
    return jax.shard_map(
        per_device,
        mesh=mesh,
        in_specs=(blocks, lists, P(("grp", "dom")), blocks, lists, lists, lists, lists, lists),
        out_specs=blocks,
        check_vma=False,
    )
```
